32 devices in a mesh: energy: 2 (over x), mom: 16 (over z, y, core).
Axes of the slice: x: 2, y: 2, z: 4, core: 2. Of those that a mesh axis runs over, the one named last changes fastest.
Arguments:
- source: float32 [256, 128, 1024], P(('energy', 'mom')), parts along dimension 0, may hold values from -6 to 6
- green: float32 [256, 1024], P(('energy', 'mom')), parts along dimension 0, may hold values from 0.1 to 0.6
- couple_one: float32 [2, 4, 128, 128], replicated, may hold values from -0.5 to 0.5
- couple_two: float32 [2, 4, 128, 128], replicated, may hold values from -0.5 to 0.5
- p_bracket: int32 [2, 1024], replicated, may hold values from 0 to 28
- q_bracket: int32 [2, 1024], replicated, may hold values from 0 to 28
- p_weight: float32 [2, 4, 1024], replicated, may hold values from -0.25 to 1
- q_weight: float32 [2, 4, 1024], replicated, may hold values from -0.25 to 1
- qr_bracket: int32 [2, 1024], replicated, may hold values from 0 to 28
- r_bracket: int32 [2, 1024], replicated, may hold values from 0 to 28
- qr_weight: float32 [2, 4, 1024], replicated, may hold values from -0.25 to 1
- r_weight: float32 [2, 4, 1024], replicated, may hold values from -0.25 to 1
Outputs:
- amplitude: float32 [256, 128, 1024], P(('energy', 'mom')), parts along dimension 0
- component: float32 [256, 128, 1024], P(('energy', 'mom')), parts along dimension 0
The draws below stay inside these ranges and needn't reach their ends.
There are 2 independent parts, one for each index of `energy`. The reference program is written for one: setup_inputs(seed, part) draws one part's arguments, and reference() takes and returns one part's arrays. A program takes and returns all parts, laid end to end along the dimension named above; an argument that names none is the same for every part. Nothing has to cross between parts.
All inputs are finite; a program needn't handle non-finite values.
Results may differ from the reference program's by a relative error of at most 0.0001.
Values sent between devices are 32-bit elements; how exact they have to be, the bound alone decides.
No kernel may reach another device: no remote copies, remote signals or barrier semaphores. Data moves between devices by JAX's collectives and lax.ppermute only.
A program may use at most 128 MiB of HBM per device.

```python
import math
import jax
import jax.numpy as jnp
from jax import lax

P_SIZE = 32
Q = 32
R = 32
CH = 128
K = 2
ITERS = 2


def touch_ends(values, rng, low, top_value):
    longest = values.shape.index(max(values.shape))
    spots = []
    for shift in (0, 1):
        where = [jax.random.randint(jax.random.fold_in(rng, axis), (), 0, length) for axis, length in enumerate(values.shape)]
        where[longest] = (where[longest] + shift) % values.shape[longest]
        spots.append(tuple(where))
    return values.at[spots[0]].set(low).at[spots[1]].set(top_value)


def levels(rng, dims, pieces, smallest, top_value):
    loudness, own = 1.0, jax.random.fold_in(rng, 6)
    for position, blocks in pieces:
        draws = jnp.exp(jax.random.uniform(jax.random.fold_in(own, position), (blocks,), jnp.float32, smallest / len(pieces), top_value / len(pieces)))
        loudness = loudness * jnp.repeat(draws, dims[position] // blocks).reshape([-1 if axis == position else 1 for axis in range(len(dims))])
    return loudness


def noise(key, dims, width, limit, shards=(), held_as=jnp.bfloat16):
    loudness = levels(key, dims, shards, -0.22, 0.18) if shards else 1.0
    array = jax.random.normal(key, dims, jnp.float32) * width * loudness
    return jnp.minimum(jnp.maximum(array, -limit), limit).astype(held_as)


def setup_inputs(seed: int = 0, part: int = 0) -> dict:
    key_list = jax.random.split(jax.random.key(seed), 13)
    part_splits = jax.random.split(jax.random.fold_in(key_list[12], part), 13)
    return {
        "source": noise(part_splits[0], (4 * R, CH, P_SIZE * Q), 1.0, 6.0, ((0, 16),), jnp.float32),
        "green": jnp.clip(jnp.exp(math.log(0.6) - 1.7917595 * jax.random.uniform(part_splits[1], (4 * P_SIZE, Q * R), jnp.float32) ** levels(part_splits[1], (4 * P_SIZE, Q * R), ((0, 16),), -0.2, 0.2)), 0.1, 0.6),
        "couple_one": noise(key_list[2], (K, 4, CH, CH), CH ** -0.5, 0.5, (), jnp.float32),
        "couple_two": noise(key_list[3], (K, 4, CH, CH), CH ** -0.5, 0.5, (), jnp.float32),
        "p_bracket": touch_ends(jax.random.randint(key_list[4], (K, P_SIZE * Q), 0, P_SIZE - 3), jax.random.fold_in(key_list[4], 1), 0, (P_SIZE - 3) - 1).astype(jnp.int32),
        "q_bracket": touch_ends(jax.random.randint(key_list[5], (K, P_SIZE * Q), 0, Q - 3), jax.random.fold_in(key_list[5], 1), 0, (Q - 3) - 1).astype(jnp.int32),
        "p_weight": jnp.clip(jax.random.uniform(key_list[6], (K, 4, P_SIZE * Q), jnp.float32, -0.25, 1.0), -0.25, 1.0),
        "q_weight": jnp.clip(jax.random.uniform(key_list[7], (K, 4, P_SIZE * Q), jnp.float32, -0.25, 1.0), -0.25, 1.0),
        "qr_bracket": touch_ends(jax.random.randint(key_list[8], (K, Q * R), 0, Q - 3), jax.random.fold_in(key_list[8], 1), 0, (Q - 3) - 1).astype(jnp.int32),
        "r_bracket": touch_ends(jax.random.randint(key_list[9], (K, Q * R), 0, R - 3), jax.random.fold_in(key_list[9], 1), 0, (R - 3) - 1).astype(jnp.int32),
        "qr_weight": jnp.clip(jax.random.uniform(key_list[10], (K, 4, Q * R), jnp.float32, -0.25, 1.0), -0.25, 1.0),
        "r_weight": jnp.clip(jax.random.uniform(key_list[11], (K, 4, Q * R), jnp.float32, -0.25, 1.0), -0.25, 1.0),
    }


def spline_matrix(first_index, second_index, first_weight, second_weight, first_count, second_count):
    first_grid = jnp.arange(first_count, dtype=jnp.int32)[None, :] - first_index[:, None]
    second_grid = jnp.arange(second_count, dtype=jnp.int32)[None, :] - second_index[:, None]
    first_rows = jnp.zeros(first_grid.shape, jnp.float32)
    second_rows = jnp.zeros(second_grid.shape, jnp.float32)
    for offset in range(4):
        first_rows = first_rows + jnp.where(first_grid == offset, first_weight[offset][:, None], jnp.float32(0.0))
        second_rows = second_rows + jnp.where(second_grid == offset, second_weight[offset][:, None], jnp.float32(0.0))
    return (first_rows[:, :, None] * second_rows[:, None, :]).reshape(first_index.shape[0], first_count * second_count)


def class_mats(couple, row_count, start):
    classes = (start + jnp.arange(row_count, dtype=jnp.int32)) % 4
    select = jax.nn.one_hot(classes, 4, dtype=jnp.float32)
    return jnp.einsum('rc,cmn->rmn', select, couple, precision=lax.Precision.HIGHEST)


def mix(mats, values):
    return jnp.einsum('rmn,rnx->rmx', mats, values, precision=lax.Precision.HIGHEST)


def interp(values, smat):
    return jnp.einsum('rcx,yx->rcy', values, smat, precision=lax.Precision.HIGHEST)


def reference(source, green, couple_one, couple_two, p_bracket, q_bracket, p_weight, q_weight, qr_bracket, r_bracket, qr_weight, r_weight):
    quarter = CH // 4
    first_maps = [spline_matrix(p_bracket[k], q_bracket[k], p_weight[k], q_weight[k], P_SIZE, Q) for k in range(K)]
    second_maps = [spline_matrix(qr_bracket[k], r_bracket[k], qr_weight[k], r_weight[k], Q, R) for k in range(K)]
    mats_one = [class_mats(couple_one[k], 4 * R, 0) for k in range(K)]
    mats_two = [class_mats(couple_two[k], 4 * P_SIZE, 0) for k in range(K)]
    state = source
    component = None
    for step in range(ITERS):
        one = interp(mix(mats_one[0], state), first_maps[0])
        for k in range(1, K):
            one = one + interp(mix(mats_one[k], state), first_maps[k])
        regrouped = one.reshape(R, 4, 4, quarter, P_SIZE, Q).transpose(4, 2, 3, 1, 5, 0).reshape(4 * P_SIZE, CH, Q * R)
        total = mix(mats_two[0], interp(regrouped, second_maps[0]))
        for k in range(1, K):
            total = total + mix(mats_two[k], interp(regrouped, second_maps[k]))
        component = green[:, None, :] * total
        back = component.reshape(P_SIZE, 4, quarter, 4, Q, R).transpose(5, 3, 1, 2, 0, 4).reshape(4 * R, CH, P_SIZE * Q)
        state = source + back
    return state, component
```

```python
import functools

import jax
import jax.numpy as jnp
from jax import lax
from jax.experimental import pallas as pl
from jax.experimental.pallas import tpu as pltpu
from jax.sharding import PartitionSpec as P

ITERS = 2
LANES = 128
F32 = jnp.float32
BF16 = jnp.bfloat16


def split(value):
    high = value.astype(BF16)
    return high, (value - high.astype(F32)).astype(BF16)


def dot(a, b):
    return jnp.dot(a, b, preferred_element_type=F32)


def dot_nt(a, b):
    return lax.dot_general(a, b, (((1,), (1,)), ((), ())), preferred_element_type=F32)


def map_kernel(count, table_ref, high_ref, low_ref):
    table = table_ref[0]
    rows = table.shape[0]
    columns = high_ref.shape[1]
    lane = lax.broadcasted_iota(jnp.int32, (rows, LANES), 1)

    def factor(index, base):
        grid = index.astype(F32) - table[:, base : base + 1]
        total = jnp.zeros((rows, LANES), F32)
        for offset in range(4):
            column = 2 + 4 * base + offset
            total = total + jnp.where(grid == offset, table[:, column : column + 1], 0.0)
        return total

    shared = None
    for tile in range(columns // LANES):
        index = lane + tile * LANES
        if shared is None or LANES % count:
            shared = factor(lax.rem(index, count), 1)
        value = factor(lax.div(index, count), 0) * shared
        high, low = split(value)
        high_ref[:, tile * LANES : (tile + 1) * LANES] = high
        low_ref[:, tile * LANES : (tile + 1) * LANES] = low


def spline_maps(first, second, first_weight, second_weight, count):
    angles, size = first.shape
    table = jnp.concatenate(
        [
            first[..., None].astype(F32),
            second[..., None].astype(F32),
            first_weight.transpose(0, 2, 1),
            second_weight.transpose(0, 2, 1),
        ],
        axis=-1,
    )
    tile = min(256, size)
    out = jax.ShapeDtypeStruct((size, angles * size), BF16)
    spec = pl.BlockSpec((tile, size), lambda k, i: (i, k))
    return pl.pallas_call(
        functools.partial(map_kernel, count),
        grid=(angles, size // tile),
        in_specs=[pl.BlockSpec((1, tile, table.shape[2]), lambda k, i: (k, i, 0))],
        out_specs=[spec, spec],
        out_shape=[out, out],
        cost_estimate=pl.CostEstimate(
            flops=20 * angles * size * size,
            bytes_accessed=4 * angles * size * size,
            transcendentals=0,
        ),
        name="spline_maps",
    )(table)


def turn_kernel(quarter, source_ref, out_ref):
    for g in range(4):
        rows = [source_ref[c, g * quarter : (g + 1) * quarter, :] for c in range(4)]
        out_ref[g, 0] = jnp.concatenate(rows, axis=0).T


def turn_source(source):
    rows, channels, size = source.shape
    tile = min(256, size)
    return pl.pallas_call(
        functools.partial(turn_kernel, channels // 4),
        grid=(rows // 4, size // tile),
        in_specs=[pl.BlockSpec((4, channels, tile), lambda r, i: (r, 0, i))],
        out_specs=pl.BlockSpec((4, 1, tile, channels), lambda r, i: (0, r, i, 0)),
        out_shape=jax.ShapeDtypeStruct((4, rows // 4, size, channels), F32),
        cost_estimate=pl.CostEstimate(
            flops=0, bytes_accessed=8 * source.size, transcendentals=0
        ),
        name="turn_source",
    )(source)


def interpolate(high_ref, low_ref, mixed_high, mixed_low):
    high = high_ref[...]
    return (
        dot(high, mixed_high[...]) + dot(high, mixed_low[...]) + dot(low_ref[...], mixed_high[...])
    )


def one_kernel(g, arrived, base_ref, *refs):
    backs = refs[:arrived]
    couple_ref, high_ref, low_ref, out_ref, w_high, w_low, m_high, m_low = refs[arrived:]
    angles, _, channels, _ = couple_ref.shape
    quarter = channels // 4
    _, local, size, _ = base_ref.shape

    @pl.when(pl.program_id(0) == 0)
    def _():
        lane = lax.broadcasted_iota(jnp.int32, (quarter, channels), 1)
        for k in range(angles):
            for c in range(4):
                rows = couple_ref[k, c, g * quarter : (g + 1) * quarter, :]
                at = k * channels + c * quarter
                inside = lax.div(lane, quarter) == c
                for other in range(4):
                    shift = ((c - other) * quarter) % channels
                    moved = pltpu.roll(rows, shift, 1) if shift else rows
                    high, low = split(jnp.where(inside, moved, 0.0))
                    w_high[at : at + quarter, other * channels : (other + 1) * channels] = high
                    w_low[at : at + quarter, other * channels : (other + 1) * channels] = low
        tile = min(256, size)
        per = backs[0].shape[2] if arrived else 0

        for r in range(local):

            def step(i, carry, r=r):
                start = pl.multiple_of(i * tile, tile)
                parts = []
                for other in range(4):
                    part = base_ref[other, r, pl.ds(start, tile), :]
                    if arrived:
                        block = backs[other][pl.ds(i * (tile // per), tile // per), r]
                        part = part + block.reshape(tile, channels)
                    parts.append(part)
                high, low = split(jnp.concatenate(parts, axis=1))
                mixed = (
                    dot_nt(high, w_high[...]) + dot_nt(high, w_low[...]) + dot_nt(low, w_high[...])
                )
                high, low = split(mixed)
                for k in range(angles):
                    lanes = slice(k * channels, (k + 1) * channels)
                    rows = pl.ds(pl.multiple_of(k * size + i * tile, tile), tile)
                    m_high[rows, r * channels : (r + 1) * channels] = high[:, lanes]
                    m_low[rows, r * channels : (r + 1) * channels] = low[:, lanes]
                return carry

            lax.fori_loop(0, size // tile, step, 0)

    value = interpolate(high_ref, low_ref, m_high, m_low)
    parts, near, _, count, _ = out_ref.shape
    for r in range(local):
        block = value[:, r * channels : (r + 1) * channels]
        out_ref[:, :, r, :, :] = block.reshape(parts, near, count, channels)


def component_one(g, base, backs, couple, maps, near, devices):
    _, local, size, channels = base.shape
    angles = couple.shape[0]
    steps = 4
    count = size // (devices * near)
    arrived = len(backs)
    out = (devices, near, local, count, channels)
    products = 3 * 2 * local * channels * angles * size
    return pl.pallas_call(
        functools.partial(one_kernel, g, arrived),
        grid=(steps,),
        in_specs=[pl.BlockSpec(base.shape, lambda i: (0, 0, 0, 0))]
        + [pl.BlockSpec(back.shape, lambda i: (0, 0, 0, 0)) for back in backs]
        + [pl.BlockSpec(couple.shape, lambda i: (0, 0, 0, 0))]
        + [pl.BlockSpec((size // steps, angles * size), lambda i: (i, 0))] * 2,
        out_specs=pl.BlockSpec((devices // steps,) + out[1:], lambda i: (i, 0, 0, 0, 0)),
        out_shape=jax.ShapeDtypeStruct(out, F32),
        scratch_shapes=[pltpu.VMEM((angles * channels, 4 * channels), BF16)] * 2
        + [pltpu.VMEM((angles * size, local * channels), BF16)] * 2,
        compiler_params=pltpu.CompilerParams(vmem_limit_bytes=48 << 20),
        cost_estimate=pl.CostEstimate(
            flops=products * (size + 4 * channels),
            bytes_accessed=4 * base.size + 4 * angles * size * size,
            transcendentals=0,
        ),
        name="component_one",
    )(base, *backs, couple, *maps)


def two_kernel(x_ref, couple_ref, green_ref, high_ref, low_ref, out_ref, m_high, m_low):
    angles, channels, _ = couple_ref.shape
    devices, local, per, _ = x_ref.shape
    size = devices * per

    @pl.when(pl.program_id(0) == 0)
    def _():
        w_high, w_low = split(couple_ref[...].reshape(angles * channels, channels))
        tile = min(256, size)
        for p in range(local):

            def step(i, carry, p=p):
                block = x_ref[pl.ds(i * (tile // per), tile // per), p]
                high, low = split(block.reshape(tile, channels))
                mixed = dot_nt(high, w_high) + dot_nt(high, w_low) + dot_nt(low, w_high)
                high, low = split(mixed)
                for k in range(angles):
                    lanes = slice(k * channels, (k + 1) * channels)
                    rows = pl.ds(pl.multiple_of(k * size + i * tile, tile), tile)
                    m_high[rows, p * channels : (p + 1) * channels] = high[:, lanes]
                    m_low[rows, p * channels : (p + 1) * channels] = low[:, lanes]
                return carry

            lax.fori_loop(0, size // tile, step, 0)

    value = interpolate(high_ref, low_ref, m_high, m_low)
    parts, near, _, count, _ = out_ref.shape
    for p in range(local):
        block = value[:, p * channels : (p + 1) * channels] * green_ref[:, p : p + 1]
        out_ref[:, :, p, :, :] = block.reshape(parts, near, count, channels)


def component_two(g, arrived, couple, green, maps, near):
    devices, local, per, channels = arrived.shape
    size = devices * per
    angles = couple.shape[0]
    steps = 4
    out = (devices, near, local, per // near, channels)
    products = 3 * 2 * local * channels * angles * size
    return pl.pallas_call(
        two_kernel,
        grid=(steps,),
        in_specs=[
            pl.BlockSpec(arrived.shape, lambda i: (0, 0, 0, 0)),
            pl.BlockSpec((angles, None, channels, channels), lambda i: (0, g, 0, 0)),
            pl.BlockSpec((None, size // steps, local), lambda i: (g, i, 0)),
        ]
        + [pl.BlockSpec((size // steps, angles * size), lambda i: (i, 0))] * 2,
        out_specs=pl.BlockSpec((devices // steps,) + out[1:], lambda i: (i, 0, 0, 0, 0)),
        out_shape=jax.ShapeDtypeStruct(out, F32),
        scratch_shapes=[pltpu.VMEM((angles * size, local * channels), BF16)] * 2,
        compiler_params=pltpu.CompilerParams(vmem_limit_bytes=48 << 20),
        cost_estimate=pl.CostEstimate(
            flops=products * (size + channels),
            bytes_accessed=4 * arrived.size + 4 * angles * size * size,
            transcendentals=0,
        ),
        name="component_two",
    )(arrived, couple, green, *maps)


def amplitude_kernel(quarter, source_ref, back_ref, *refs):
    out_ref = refs[-1]
    back = back_ref[...]
    turned = back.reshape(-1, back.shape[-1]).T
    for c in range(4):
        out_ref[c] = source_ref[c] + turned[c * quarter : (c + 1) * quarter]


def amplitude_chunk(g, source, back, so_far):
    rows, channels, size = source.shape
    devices, local, per, _ = back.shape
    quarter = channels // 4
    tile = min(512, size)
    spec = pl.BlockSpec((4, quarter, tile), lambda r, i: (r, g, i))
    in_specs = [
        spec,
        pl.BlockSpec((tile // per, None, per, channels), lambda r, i: (i, r, 0, 0)),
    ]
    args = [source, back]
    aliases = {}
    if so_far is not None:
        in_specs.append(pl.BlockSpec(memory_space=pl.ANY))
        args.append(so_far)
        aliases = {2: 0}
    return pl.pallas_call(
        functools.partial(amplitude_kernel, quarter),
        grid=(local, size // tile),
        in_specs=in_specs,
        out_specs=spec,
        out_shape=jax.ShapeDtypeStruct(source.shape, F32),
        input_output_aliases=aliases,
        cost_estimate=pl.CostEstimate(
            flops=back.size, bytes_accessed=12 * back.size, transcendentals=0
        ),
        name="amplitude",
    )(*args)


def output_kernel(quarter, sent_ref, *refs):
    out_ref, turned_ref = refs[-2:]
    devices, near, count, channels = sent_ref.shape
    per_tile = LANES // (devices * near)
    for tile in range(count // per_tile):
        rows = [
            sent_ref[:, :, tile * per_tile + i, :].reshape(devices * near, channels)
            for i in range(per_tile)
        ]
        turned = jnp.concatenate(rows, axis=0).T
        for c in range(4):
            turned_ref[tile, pl.ds(c, quarter, stride=4), :] = turned[
                c * quarter : (c + 1) * quarter
            ]
        out_ref[:, tile * LANES : (tile + 1) * LANES] = turned_ref[tile]


def component_chunk(g, sent, so_far):
    devices, near, local, count, channels = sent.shape
    size = devices * near * count
    in_specs = [
        pl.BlockSpec((devices, near, None, count, channels), lambda p: (0, 0, p, 0, 0))
    ]
    args = [sent]
    aliases = {}
    if so_far is not None:
        in_specs.append(pl.BlockSpec(memory_space=pl.ANY))
        args.append(so_far)
        aliases = {1: 0}
    return pl.pallas_call(
        functools.partial(output_kernel, channels // 4),
        grid=(local,),
        in_specs=in_specs,
        out_specs=pl.BlockSpec((None, channels, size), lambda p: (4 * p + g, 0, 0)),
        out_shape=jax.ShapeDtypeStruct((4 * local, channels, size), F32),
        scratch_shapes=[pltpu.VMEM((size // LANES, channels, LANES), F32)],
        input_output_aliases=aliases,
        cost_estimate=pl.CostEstimate(
            flops=0, bytes_accessed=8 * sent.size, transcendentals=0
        ),
        name="component_out",
    )(*args)


def exchange(values):
    devices, near, local, count, channels = values.shape
    sent = values.reshape(devices, near, local * count, channels)
    return lax.all_to_all(sent, "mom", split_axis=0, concat_axis=0, tiled=True)


def shards(
    devices,
    source,
    green,
    couple_one,
    couple_two,
    p_bracket,
    q_bracket,
    p_weight,
    q_weight,
    qr_bracket,
    r_bracket,
    qr_weight,
    r_weight,
):
    rows_one, channels, size_one = source.shape
    rows_two, size_two = green.shape
    angles = couple_one.shape[0]
    quarter = channels // 4
    near_r, near_p = rows_one // 4, rows_two // 4
    r_size, p_size = devices * near_r, devices * near_p
    q_size = size_one // p_size

    base = turn_source(source)
    first_maps = spline_maps(p_bracket, q_bracket, p_weight, q_weight, q_size)

    def by_r(array):
        lead = array.shape[:-1]
        return array.reshape(lead + (q_size, r_size)).swapaxes(-1, -2).reshape(lead + (-1,))

    second_maps = spline_maps(
        by_r(r_bracket), by_r(qr_bracket), by_r(r_weight), by_r(qr_weight), q_size
    )
    couple_two = (
        couple_two.reshape(angles, 4, quarter, 4, quarter, 4)
        .transpose(0, 1, 3, 2, 5, 4)
        .reshape(couple_two.shape)
    )
    green = (
        green.reshape(near_p, 4, q_size, r_size)
        .transpose(1, 3, 2, 0)
        .reshape(4, size_two, near_p)
    )
    backs = []
    for step in range(ITERS):
        ones = [
            exchange(component_one(g, base, backs, couple_one, first_maps, near_p, devices))
            for g in range(4)
        ]
        twos = [
            component_two(g, ones[g], couple_two, green, second_maps, near_r) for g in range(4)
        ]
        backs = [exchange(two) for two in twos]
    component = None
    for g in range(4):
        component = component_chunk(g, twos[g], component)
    amplitude = None
    for g in range(4):
        amplitude = amplitude_chunk(g, source, backs[g], amplitude)
    return amplitude, component


def whole_map(first, second, first_weight, second_weight, first_count, second_count):
    first_rows = jnp.zeros((first.shape[0], first_count), F32)
    second_rows = jnp.zeros((second.shape[0], second_count), F32)
    first_grid = jnp.arange(first_count, dtype=jnp.int32)[None, :] - first[:, None]
    second_grid = jnp.arange(second_count, dtype=jnp.int32)[None, :] - second[:, None]
    for offset in range(4):
        first_rows += jnp.where(first_grid == offset, first_weight[offset][:, None], 0.0)
        second_rows += jnp.where(second_grid == offset, second_weight[offset][:, None], 0.0)
    return (first_rows[:, :, None] * second_rows[:, None, :]).reshape(first.shape[0], -1)


def row_mats(couple, rows, start):
    select = jax.nn.one_hot((start + jnp.arange(rows, dtype=jnp.int32)) % 4, 4, dtype=F32)
    return jnp.einsum("rc,kcmn->krmn", select, couple, precision=lax.Precision.HIGHEST)


def mix_rows(mats, values):
    return jnp.einsum("rmn,rnx->rmx", mats, values, precision=lax.Precision.HIGHEST)


def interpolate_rows(values, matrix):
    return jnp.einsum("rcx,yx->rcy", values, matrix, precision=lax.Precision.HIGHEST)


def shards_by_row(
    devices,
    source,
    green,
    couple_one,
    couple_two,
    p_bracket,
    q_bracket,
    p_weight,
    q_weight,
    qr_bracket,
    r_bracket,
    qr_weight,
    r_weight,
):
    rows_one, channels, size_one = source.shape
    rows_two, size_two = green.shape
    angles = couple_one.shape[0]
    quarter = channels // 4
    r_size, p_size = devices * rows_one // 4, devices * rows_two // 4
    q_size = size_one // p_size
    here = lax.axis_index("mom")
    first = [
        whole_map(p_bracket[k], q_bracket[k], p_weight[k], q_weight[k], p_size, q_size)
        for k in range(angles)
    ]
    second = [
        whole_map(qr_bracket[k], r_bracket[k], qr_weight[k], r_weight[k], q_size, r_size)
        for k in range(angles)
    ]
    mats_one = row_mats(couple_one, rows_one, here * rows_one)
    mats_two = row_mats(couple_two, rows_two, here * rows_two)
    state = source
    for step in range(ITERS):
        one = sum(interpolate_rows(mix_rows(mats_one[k], state), first[k]) for k in range(angles))
        sent = one.reshape(rows_one, 4, quarter, p_size, q_size).transpose(3, 1, 0, 2, 4)
        sent = sent.reshape(4 * p_size, rows_one, quarter * q_size)
        sent = lax.all_to_all(sent, "mom", split_axis=0, concat_axis=1, tiled=True)
        sent = sent.reshape(rows_two, r_size, 4, quarter, q_size).transpose(0, 3, 2, 4, 1)
        sent = sent.reshape(rows_two, channels, size_two)
        total = sum(mix_rows(mats_two[k], interpolate_rows(sent, second[k])) for k in range(angles))
        component = green[:, None, :] * total
        back = component.reshape(rows_two, quarter, 4, q_size, r_size).transpose(4, 2, 0, 1, 3)
        back = back.reshape(4 * r_size, rows_two, quarter * q_size)
        back = lax.all_to_all(back, "mom", split_axis=0, concat_axis=1, tiled=True)
        back = back.reshape(rows_one, p_size, 4, quarter, q_size).transpose(0, 2, 3, 1, 4)
        state = source + back.reshape(source.shape)
    return state, component


def solution(mesh):
    spread = ("energy", "mom")
    placed = (P(spread, None, None), P(spread, None)) + (P(),) * 10
    devices = mesh.shape["mom"]

    def body(source, green, *rest):
        whole_rows = source.shape[0] % 4 == 0 and green.shape[0] % 4 == 0
        chosen = shards if whole_rows and source.shape[1] == LANES else shards_by_row
        return chosen(devices, source, green, *rest)

    return jax.shard_map(
        body,
        mesh=mesh,
        in_specs=placed,
        out_specs=(P(spread, None, None), P(spread, None, None)),
        check_vma=False,
    )
```

```python
import functools

import jax
import jax.numpy as jnp
from jax import lax
from jax.experimental import pallas as pl
from jax.experimental.pallas import tpu as pltpu
from jax.sharding import PartitionSpec as P

ITERS = 2
LANES = 128
F32 = jnp.float32
BF16 = jnp.bfloat16
VMEM_LIMIT = 60 << 20


def split(value):
    high = value.astype(BF16)
    return high, (value - high.astype(F32)).astype(BF16)


def dot(a, b):
    return jnp.dot(a, b, preferred_element_type=F32)


def dot_nt(a, b):
    return lax.dot_general(a, b, (((1,), (1,)), ((), ())), preferred_element_type=F32)


def call(kernel, name, flops, moved, **kwargs):
    return pl.pallas_call(
        kernel,
        compiler_params=pltpu.CompilerParams(vmem_limit_bytes=VMEM_LIMIT),
        cost_estimate=pl.CostEstimate(flops=flops, bytes_accessed=moved, transcendentals=0),
        name=name,
        **kwargs,
    )


def map_kernel(count, table_ref, high_ref, low_ref):
    table = table_ref[0]
    rows = table.shape[0]
    columns = high_ref.shape[1]
    lane = lax.broadcasted_iota(jnp.int32, (rows, LANES), 1)

    def factor(index, base):
        grid = index.astype(F32) - table[:, base : base + 1]
        total = jnp.zeros((rows, LANES), F32)
        for offset in range(4):
            column = 2 + 4 * base + offset
            total = jnp.where(grid == offset, table[:, column : column + 1], total)
        return total

    first = factor(lane, 0)
    second = factor(lax.rem(lane, count), 1)
    for tile in range(columns // LANES):
        index = lax.div(lane + tile * LANES, count)
        value = jnp.take_along_axis(first, index, axis=1) * second
        high, low = split(value)
        high_ref[:, tile * LANES : (tile + 1) * LANES] = high
        low_ref[:, tile * LANES : (tile + 1) * LANES] = low


def spline_maps(first, second, first_weight, second_weight, count):
    angles, size = first.shape
    table = jnp.concatenate(
        [
            first[..., None].astype(F32),
            second[..., None].astype(F32),
            first_weight.transpose(0, 2, 1),
            second_weight.transpose(0, 2, 1),
        ],
        axis=-1,
    )
    tile = min(256, size)
    out = jax.ShapeDtypeStruct((size, angles * size), BF16)
    spec = pl.BlockSpec((tile, size), lambda k, i: (i, k))
    return call(
        functools.partial(map_kernel, count),
        "spline_maps",
        10 * angles * size * size,
        4 * angles * size * size,
        grid=(angles, size // tile),
        in_specs=[pl.BlockSpec((1, tile, table.shape[2]), lambda k, i: (k, i, 0))],
        out_specs=[spec, spec],
        out_shape=[out, out],
    )(table)


def interpolate(high_ref, low_ref, mixed_high, mixed_low, product):
    high = high_ref[...]
    return (
        product(high, mixed_high[...])
        + product(high, mixed_low[...])
        + product(low_ref[...], mixed_high[...])
    )


def spread_out(value, out_ref, scale_ref=None):
    parts, blocks, near, local, count, channels = out_ref.shape
    for b in range(blocks):
        for n in range(local):
            at = b * local + n
            block = value[:, at * channels : (at + 1) * channels]
            if scale_ref is not None:
                block = block * scale_ref[:, at : at + 1]
            out_ref[:, b, :, n, :, :] = block.reshape(parts, near, count, channels)


def first_kernel(blocks, steps, local, source_ref, couple_ref, high_ref, low_ref, out_ref, m_high, m_low):
    angles, channels, _ = couple_ref.shape
    quarter = channels // 4
    size = source_ref.shape[1]
    i = pl.program_id(0)

    @pl.when(i < steps)
    def _():
        rows = [
            couple_ref[k, g * quarter : (g + 1) * quarter, :] for k in range(angles) for g in blocks
        ]
        w_high, w_low = split(jnp.concatenate(rows, axis=0))
        high, low = split(source_ref[...])
        high, low = split(dot(w_high, high) + dot(w_low, high) + dot(w_high, low))
        r, c = lax.div(i, 4), lax.rem(i, 4)
        for k in range(angles):
            for b in range(len(blocks)):
                at = (k * len(blocks) + b) * quarter
                to = pl.multiple_of((b * local + r) * channels + c * quarter, quarter)
                m_high[pl.ds(to, quarter), k * size : (k + 1) * size] = high[at : at + quarter]
                m_low[pl.ds(to, quarter), k * size : (k + 1) * size] = low[at : at + quarter]

    @pl.when(i >= steps)
    def _():
        spread_out(interpolate(high_ref, low_ref, m_high, m_low, dot_nt), out_ref)


def first_one(blocks, source, couple, maps, near, devices):
    rows, channels, size = source.shape
    local = rows // 4
    angles = couple.shape[0]
    tiles = 4
    out = (devices, len(blocks), near, local, size // (devices * near), channels)
    wide = len(blocks) * local * channels

    def tile(i):
        return jnp.maximum(i - rows, 0)

    return call(
        functools.partial(first_kernel, blocks, rows, local),
        "component_one_first",
        6 * wide * angles * size * (size + channels),
        4 * source.size + 4 * angles * size * size,
        grid=(rows + tiles,),
        in_specs=[
            pl.BlockSpec((None, channels, size), lambda i: (jnp.minimum(i, rows - 1), 0, 0)),
            pl.BlockSpec((angles, None, channels, channels), lambda i: (0, lax.rem(i, 4), 0, 0)),
        ]
        + [pl.BlockSpec((size // tiles, angles * size), lambda i: (tile(i), 0))] * 2,
        out_specs=pl.BlockSpec((devices // tiles,) + out[1:], lambda i: (tile(i), 0, 0, 0, 0, 0)),
        out_shape=jax.ShapeDtypeStruct(out, F32),
        scratch_shapes=[pltpu.VMEM((wide, angles * size), BF16)] * 2,
    )(source, couple, *maps)


def later_kernel(blocks, steps, arrived, *refs):
    backs = refs[:arrived]
    couple_ref, high_ref, low_ref, out_ref, w_high, w_low, m_high, m_low = refs[arrived:]
    angles, _, channels, _ = couple_ref.shape
    quarter = channels // 4
    parts, _, local, per, _ = backs[0].shape
    tile = parts * per
    size = tile * steps
    i = pl.program_id(0)

    @pl.when(i == 0)
    def _():
        lane = lax.broadcasted_iota(jnp.int32, (quarter, channels), 1)
        for k in range(angles):
            for b, g in enumerate(blocks):
                for c in range(4):
                    rows = couple_ref[k, c, g * quarter : (g + 1) * quarter, :]
                    at = (k * len(blocks) + b) * channels + c * quarter
                    inside = lax.div(lane, quarter) == c
                    for other in range(4):
                        shift = ((c - other) * quarter) % channels
                        moved = pltpu.roll(rows, shift, 1) if shift else rows
                        high, low = split(jnp.where(inside, moved, 0.0))
                        lanes = slice(other * channels, (other + 1) * channels)
                        w_high[at : at + quarter, lanes] = high
                        w_low[at : at + quarter, lanes] = low

    @pl.when(i < steps)
    def _():
        for r in range(local):
            pieces = [
                back[:, b, r].reshape(tile, channels)
                for back in backs
                for b in range(back.shape[1])
            ]
            high, low = split(jnp.concatenate(pieces, axis=1))
            mixed = dot_nt(high, w_high[...]) + dot_nt(low, w_high[...]) + dot_nt(high, w_low[...])
            high, low = split(mixed)
            for k in range(angles):
                rows = pl.ds(pl.multiple_of(k * size + i * tile, tile), tile)
                for b in range(len(blocks)):
                    at = (k * len(blocks) + b) * channels
                    to = (b * local + r) * channels
                    m_high[rows, to : to + channels] = high[:, at : at + channels]
                    m_low[rows, to : to + channels] = low[:, at : at + channels]

    @pl.when(i >= steps)
    def _():
        spread_out(interpolate(high_ref, low_ref, m_high, m_low, dot), out_ref)


def later_one(blocks, backs, couple, maps, near):
    devices, _, local, per, channels = backs[0].shape
    size = devices * per
    angles = couple.shape[0]
    steps = tiles = 4
    out = (devices, len(blocks), near, local, size // (devices * near), channels)
    wide = len(blocks) * local * channels

    def tile(i):
        return jnp.maximum(i - steps, 0)

    def step(i):
        return jnp.minimum(i, steps - 1)

    return call(
        functools.partial(later_kernel, blocks, steps, len(backs)),
        "component_one_later",
        6 * wide * angles * size * (size + 4 * channels),
        4 * sum(back.size for back in backs) + 4 * angles * size * size,
        grid=(steps + tiles,),
        in_specs=[
            pl.BlockSpec((devices // steps,) + back.shape[1:], lambda i: (step(i), 0, 0, 0, 0))
            for back in backs
        ]
        + [pl.BlockSpec(couple.shape, lambda i: (0, 0, 0, 0))]
        + [pl.BlockSpec((size // tiles, angles * size), lambda i: (tile(i), 0))] * 2,
        out_specs=pl.BlockSpec((devices // tiles,) + out[1:], lambda i: (tile(i), 0, 0, 0, 0, 0)),
        out_shape=jax.ShapeDtypeStruct(out, F32),
        scratch_shapes=[pltpu.VMEM((angles * len(blocks) * channels, 4 * channels), BF16)] * 2
        + [pltpu.VMEM((angles * size, wide), BF16)] * 2,
    )(*backs, couple, *maps)


def two_kernel(blocks, steps, arrived, *refs):
    values = refs[:arrived]
    couple_ref, green_ref, high_ref, low_ref, out_ref = refs[arrived : arrived + 5]
    turned, w_high, w_low, m_high, m_low = refs[arrived + 5 :]
    angles, _, channels, _ = couple_ref.shape
    quarter = channels // 4
    parts, _, local, per, _ = values[0].shape
    tile = parts * per
    size = tile * steps
    i = pl.program_id(0)

    @pl.when(i == 0)
    def _():
        for k in range(angles):
            for b, g in enumerate(blocks):
                at = k * len(blocks) + b
                rows = [couple_ref[k, g, pl.ds(c, quarter, stride=4), :] for c in range(4)]
                turned[at] = jnp.concatenate(rows, axis=0).T
                rows = [turned[at, pl.ds(c, quarter, stride=4), :] for c in range(4)]
                high, low = split(jnp.concatenate(rows, axis=0))
                w_high[b, :, k * channels : (k + 1) * channels] = high
                w_low[b, :, k * channels : (k + 1) * channels] = low

    @pl.when(i < steps)
    def _():
        for b in range(len(blocks)):
            for p in range(local):
                value = values[0][:, b, p]
                for other in values[1:]:
                    value = value + other[:, b, p]
                high, low = split(value.reshape(tile, channels))
                mixed = dot(high, w_high[b]) + dot(low, w_high[b]) + dot(high, w_low[b])
                high, low = split(mixed)
                to = (b * local + p) * channels
                for k in range(angles):
                    rows = pl.ds(pl.multiple_of(k * size + i * tile, tile), tile)
                    lanes = slice(k * channels, (k + 1) * channels)
                    m_high[rows, to : to + channels] = high[:, lanes]
                    m_low[rows, to : to + channels] = low[:, lanes]

    @pl.when(i >= steps)
    def _():
        spread_out(interpolate(high_ref, low_ref, m_high, m_low, dot), out_ref, green_ref)


def component_two(blocks, values, couple, green, maps, near):
    devices, _, local, per, channels = values[0].shape
    size = devices * per
    angles = couple.shape[0]
    steps = tiles = 4
    out = (devices, len(blocks), near, local, per // near, channels)
    wide = len(blocks) * local * channels

    def tile(i):
        return jnp.maximum(i - steps, 0)

    def step(i):
        return jnp.minimum(i, steps - 1)

    return call(
        functools.partial(two_kernel, blocks, steps, len(values)),
        "component_two",
        6 * wide * angles * size * (size + channels),
        4 * len(values) * values[0].size + 4 * angles * size * size,
        grid=(steps + tiles,),
        in_specs=[
            pl.BlockSpec((devices // steps,) + value.shape[1:], lambda i: (step(i), 0, 0, 0, 0))
            for value in values
        ]
        + [
            pl.BlockSpec(couple.shape, lambda i: (0, 0, 0, 0)),
            pl.BlockSpec((size // tiles, green.shape[1]), lambda i: (tile(i), 0)),
        ]
        + [pl.BlockSpec((size // tiles, angles * size), lambda i: (tile(i), 0))] * 2,
        out_specs=pl.BlockSpec((devices // tiles,) + out[1:], lambda i: (tile(i), 0, 0, 0, 0, 0)),
        out_shape=jax.ShapeDtypeStruct(out, F32),
        scratch_shapes=[pltpu.VMEM((angles * len(blocks), channels, channels), F32)]
        + [pltpu.VMEM((len(blocks), channels, angles * channels), BF16)] * 2
        + [pltpu.VMEM((angles * size, wide), BF16)] * 2,
    )(*values, couple, green, *maps)


def amplitude_kernel(quarter, source_ref, back_ref, *refs):
    out_ref = refs[-1]
    back = back_ref[...]
    turned = back.reshape(-1, back.shape[-1]).T
    for c in range(4):
        out_ref[c] = source_ref[c] + turned[c * quarter : (c + 1) * quarter]


def amplitude_chunk(blocks, source, back, so_far):
    rows, channels, size = source.shape
    devices, _, local, per, _ = back.shape
    quarter = channels // 4
    tile = min(512, size)
    spec = pl.BlockSpec((4, quarter, tile), lambda b, r, i: (r, blocks[0] + b, i))
    in_specs = [
        spec,
        pl.BlockSpec((tile // per, None, None, per, channels), lambda b, r, i: (i, b, r, 0, 0)),
    ]
    args = [source, back]
    aliases = {}
    if so_far is not None:
        in_specs.append(pl.BlockSpec(memory_space=pl.ANY))
        args.append(so_far)
        aliases = {2: 0}
    return call(
        functools.partial(amplitude_kernel, quarter),
        "amplitude",
        back.size,
        12 * back.size,
        grid=(len(blocks), local, size // tile),
        in_specs=in_specs,
        out_specs=spec,
        out_shape=jax.ShapeDtypeStruct(source.shape, F32),
        input_output_aliases=aliases,
    )(*args)


def output_kernel(quarter, sent_ref, *refs):
    out_ref, turned_ref = refs[-2:]
    devices, near, count, channels = sent_ref.shape
    per_tile = LANES // (devices * near)
    for tile in range(count // per_tile):
        rows = [
            sent_ref[:, :, tile * per_tile + i, :].reshape(devices * near, channels)
            for i in range(per_tile)
        ]
        turned = jnp.concatenate(rows, axis=0).T
        for c in range(4):
            turned_ref[tile, pl.ds(c, quarter, stride=4), :] = turned[
                c * quarter : (c + 1) * quarter
            ]
        out_ref[:, tile * LANES : (tile + 1) * LANES] = turned_ref[tile]


def component_chunk(blocks, sent, so_far):
    devices, _, near, local, count, channels = sent.shape
    size = devices * near * count
    in_specs = [
        pl.BlockSpec(
            (devices, None, near, None, count, channels), lambda b, p: (0, b, 0, p, 0, 0)
        )
    ]
    args = [sent]
    aliases = {}
    if so_far is not None:
        in_specs.append(pl.BlockSpec(memory_space=pl.ANY))
        args.append(so_far)
        aliases = {1: 0}
    return call(
        functools.partial(output_kernel, channels // 4),
        "component_out",
        0,
        8 * sent.size,
        grid=(len(blocks), local),
        in_specs=in_specs,
        out_specs=pl.BlockSpec(
            (None, channels, size), lambda b, p: (4 * p + blocks[0] + b, 0, 0)
        ),
        out_shape=jax.ShapeDtypeStruct((4 * local, channels, size), F32),
        scratch_shapes=[pltpu.VMEM((size // LANES, channels, LANES), F32)],
        input_output_aliases=aliases,
    )(*args)


def exchange(values):
    devices, blocks, near, local, count, channels = values.shape
    sent = values.reshape(devices, blocks, near, local * count, channels)
    return lax.all_to_all(sent, "mom", split_axis=0, concat_axis=0, tiled=True)


CHUNKS = ((0,), (1, 2, 3))


def shards(
    devices,
    source,
    green,
    couple_one,
    couple_two,
    p_bracket,
    q_bracket,
    p_weight,
    q_weight,
    qr_bracket,
    r_bracket,
    qr_weight,
    r_weight,
):
    rows_one, channels, size_one = source.shape
    rows_two, size_two = green.shape
    near_r, near_p = rows_one // 4, rows_two // 4
    r_size, p_size = devices * near_r, devices * near_p
    q_size = size_one // p_size

    first_maps = spline_maps(p_bracket, q_bracket, p_weight, q_weight, q_size)

    def by_r(array):
        lead = array.shape[:-1]
        return array.reshape(lead + (q_size, r_size)).swapaxes(-1, -2).reshape(lead + (-1,))

    second_maps = spline_maps(
        by_r(r_bracket), by_r(qr_bracket), by_r(r_weight), by_r(qr_weight), q_size
    )
    green = green.reshape(near_p, 4, q_size, r_size).transpose(3, 2, 1, 0)
    green = green.reshape(size_two, 4 * near_p)
    arrived = []
    for step in range(ITERS):
        if step == 0:
            ones = [
                first_one(blocks, source, couple_one, first_maps, near_p, devices)
                for blocks in CHUNKS
            ]
        else:
            ones = [later_one(blocks, backs, couple_one, first_maps, near_p) for blocks in CHUNKS]
        arrived.append([exchange(one) for one in ones])
        values = [arrived[0]] + ([arrived[step]] if step else [])
        twos = []
        for n, blocks in enumerate(CHUNKS):
            lanes = slice(blocks[0] * near_p, (blocks[-1] + 1) * near_p)
            twos.append(
                component_two(
                    blocks,
                    [value[n] for value in values],
                    couple_two,
                    green[:, lanes],
                    second_maps,
                    near_r,
                )
            )
        backs = [exchange(two) for two in twos]
    component = amplitude = None
    for blocks, two in zip(CHUNKS, twos):
        component = component_chunk(blocks, two, component)
    for blocks, back in zip(CHUNKS, backs):
        amplitude = amplitude_chunk(blocks, source, back, amplitude)
    return amplitude, component


def whole_map(first, second, first_weight, second_weight, first_count, second_count):
    first_rows = jnp.zeros((first.shape[0], first_count), F32)
    second_rows = jnp.zeros((second.shape[0], second_count), F32)
    first_grid = jnp.arange(first_count, dtype=jnp.int32)[None, :] - first[:, None]
    second_grid = jnp.arange(second_count, dtype=jnp.int32)[None, :] - second[:, None]
    for offset in range(4):
        first_rows += jnp.where(first_grid == offset, first_weight[offset][:, None], 0.0)
        second_rows += jnp.where(second_grid == offset, second_weight[offset][:, None], 0.0)
    return (first_rows[:, :, None] * second_rows[:, None, :]).reshape(first.shape[0], -1)


def row_mats(couple, rows, start):
    select = jax.nn.one_hot((start + jnp.arange(rows, dtype=jnp.int32)) % 4, 4, dtype=F32)
    return jnp.einsum("rc,kcmn->krmn", select, couple, precision=lax.Precision.HIGHEST)


def mix_rows(mats, values):
    return jnp.einsum("rmn,rnx->rmx", mats, values, precision=lax.Precision.HIGHEST)


def interpolate_rows(values, matrix):
    return jnp.einsum("rcx,yx->rcy", values, matrix, precision=lax.Precision.HIGHEST)


def shards_by_row(
    devices,
    source,
    green,
    couple_one,
    couple_two,
    p_bracket,
    q_bracket,
    p_weight,
    q_weight,
    qr_bracket,
    r_bracket,
    qr_weight,
    r_weight,
):
    rows_one, channels, size_one = source.shape
    rows_two, size_two = green.shape
    angles = couple_one.shape[0]
    quarter = channels // 4
    r_size, p_size = devices * rows_one // 4, devices * rows_two // 4
    q_size = size_one // p_size
    here = lax.axis_index("mom")
    first = [
        whole_map(p_bracket[k], q_bracket[k], p_weight[k], q_weight[k], p_size, q_size)
        for k in range(angles)
    ]
    second = [
        whole_map(qr_bracket[k], r_bracket[k], qr_weight[k], r_weight[k], q_size, r_size)
        for k in range(angles)
    ]
    mats_one = row_mats(couple_one, rows_one, here * rows_one)
    mats_two = row_mats(couple_two, rows_two, here * rows_two)
    state = source
    for step in range(ITERS):
        one = sum(interpolate_rows(mix_rows(mats_one[k], state), first[k]) for k in range(angles))
        sent = one.reshape(rows_one, 4, quarter, p_size, q_size).transpose(3, 1, 0, 2, 4)
        sent = sent.reshape(4 * p_size, rows_one, quarter * q_size)
        sent = lax.all_to_all(sent, "mom", split_axis=0, concat_axis=1, tiled=True)
        sent = sent.reshape(rows_two, r_size, 4, quarter, q_size).transpose(0, 3, 2, 4, 1)
        sent = sent.reshape(rows_two, channels, size_two)
        total = sum(mix_rows(mats_two[k], interpolate_rows(sent, second[k])) for k in range(angles))
        component = green[:, None, :] * total
        back = component.reshape(rows_two, quarter, 4, q_size, r_size).transpose(4, 2, 0, 1, 3)
        back = back.reshape(4 * r_size, rows_two, quarter * q_size)
        back = lax.all_to_all(back, "mom", split_axis=0, concat_axis=1, tiled=True)
        back = back.reshape(rows_one, p_size, 4, quarter, q_size).transpose(0, 2, 3, 1, 4)
        state = source + back.reshape(source.shape)
    return state, component


def solution(mesh):
    spread = ("energy", "mom")
    placed = (P(spread, None, None), P(spread, None)) + (P(),) * 10
    devices = mesh.shape["mom"]

    def body(source, green, *rest):
        whole_rows = source.shape[0] % 4 == 0 and green.shape[0] % 4 == 0
        chosen = shards if whole_rows and source.shape[1] == LANES else shards_by_row
        return chosen(devices, source, green, *rest)

    return jax.shard_map(
        body,
        mesh=mesh,
        in_specs=placed,
        out_specs=(P(spread, None, None), P(spread, None, None)),
        check_vma=False,
    )
```

```python
import functools

import jax
import jax.numpy as jnp
from jax import lax
from jax.experimental import pallas as pl
from jax.experimental.pallas import tpu as pltpu
from jax.sharding import PartitionSpec as P

ITERS = 2
LANES = 128
F32 = jnp.float32
BF16 = jnp.bfloat16
VMEM_LIMIT = 60 << 20
MAP_ROWS = 512
TILES = 2
SOURCE_ROWS = 4


def split(value):
    high = value.astype(BF16)
    return high, (value - high.astype(F32)).astype(BF16)


def dot(a, b):
    return jnp.dot(a, b, preferred_element_type=F32)


def dot_nt(a, b):
    return lax.dot_general(a, b, (((1,), (1,)), ((), ())), preferred_element_type=F32)


def call(kernel, name, flops, moved, args, grid, in_specs, out_specs, out_shape, scratch_shapes=(), scalars=(), aliases=None):
    return pl.pallas_call(
        kernel,
        grid_spec=pltpu.PrefetchScalarGridSpec(
            num_scalar_prefetch=len(scalars),
            grid=grid,
            in_specs=in_specs,
            out_specs=out_specs,
            scratch_shapes=scratch_shapes,
        ),
        out_shape=out_shape,
        input_output_aliases=aliases or {},
        compiler_params=pltpu.CompilerParams(vmem_limit_bytes=VMEM_LIMIT),
        cost_estimate=pl.CostEstimate(flops=flops, bytes_accessed=moved, transcendentals=0),
        name=name,
    )(*scalars, *args)


def map_kernel(count, first_ref, second_ref, first_weight_ref, second_weight_ref, high_ref, low_ref):
    rows, columns = high_ref.shape
    k = pl.program_id(0)
    table = jnp.concatenate(
        [
            first_ref[pl.ds(k, 1), :].astype(F32),
            second_ref[pl.ds(k, 1), :].astype(F32),
            first_weight_ref[...],
            second_weight_ref[...],
            jnp.zeros((6, rows), F32),
        ],
        axis=0,
    ).T
    lane = lax.broadcasted_iota(jnp.int32, (1, LANES), 1)
    group = lax.div(lane, count)

    def factor(index, base):
        grid = index.astype(F32) - table[:, base : base + 1]
        total = jnp.zeros((rows, LANES), F32)
        for offset in range(4):
            column = 2 + 4 * base + offset
            total = jnp.where(grid == offset, table[:, column : column + 1], total)
        return total

    first_high, first_low = split(factor(lane, 0))
    second = factor(lane - group * count, 1)
    node = lax.broadcasted_iota(jnp.int32, (LANES, columns), 0)
    column = lax.broadcasted_iota(jnp.int32, (LANES, columns), 1)
    chosen = jnp.where(
        jnp.logical_and(column >= node * count, column < (node + 1) * count), 1.0, 0.0
    ).astype(BF16)
    for tile in range(columns // LANES):
        lanes = slice(tile * LANES, (tile + 1) * LANES)
        spread = dot(first_high, chosen[:, lanes]) + dot(first_low, chosen[:, lanes])
        high, low = split(spread * second)
        high_ref[:, lanes] = high
        low_ref[:, lanes] = low


def spline_maps(first, second, first_weight, second_weight, count):
    angles, size = first.shape
    tile = min(MAP_ROWS, size)
    out = jax.ShapeDtypeStruct((size, angles * size), BF16)
    spec = pl.BlockSpec((tile, size), lambda k, i: (i, k))
    return call(
        functools.partial(map_kernel, count),
        "spline_maps",
        10 * angles * size * size,
        4 * angles * size * size,
        (first, second, first_weight, second_weight),
        grid=(angles, size // tile),
        in_specs=[pl.BlockSpec((angles, tile), lambda k, i: (0, i))] * 2
        + [pl.BlockSpec((None, 4, tile), lambda k, i: (k, 0, i))] * 2,
        out_specs=[spec, spec],
        out_shape=[out, out],
    )


def interpolate(high_ref, low_ref, mixed_high, mixed_low, product):
    high = high_ref[...]
    return (
        product(high, mixed_high[...])
        + product(high, mixed_low[...])
        + product(low_ref[...], mixed_high[...])
    )


def spread_out(flip, value, out_ref, scale_ref=None):
    parts, blocks, near, local, count, channels = out_ref.shape
    rows = near * count
    for b in range(blocks):
        for n in range(local):
            at = b * local + n
            block = value[:, at * channels : (at + 1) * channels]
            if scale_ref is not None:
                block = block * scale_ref[:, at : at + 1]
            for j in range(parts):
                piece = block[j * rows : (j + 1) * rows].reshape(near, count, channels)
                out_ref[j ^ (flip & (parts - 1)), b, :, n, :, :] = piece


def out_spec(shape, tile):
    parts = shape[0] // TILES
    return pl.BlockSpec(
        (parts,) + shape[1:],
        lambda i, flip: (tile(i) ^ lax.div(flip[0], parts), 0, 0, 0, 0, 0),
    )


def gather(me, sets, whole_ref):
    blocks, local, _, channels = whole_ref.shape
    per = sets[0][0].shape[3]
    for s in range(len(sets[0])):
        rows = pl.ds(pl.multiple_of((me ^ s) * per, per), per)
        for b in range(blocks):
            for n in range(local):
                value = sets[0][s][0, b, n]
                for other in sets[1:]:
                    value = value + other[s][0, b, n]
                whole_ref[b, n, rows, :] = value


def first_kernel(blocks, steps, flip_ref, source_ref, couple_ref, high_ref, low_ref, out_ref, m_high, m_low):
    angles, _, channels, _ = couple_ref.shape
    quarter = channels // 4
    together, _, size = source_ref.shape
    i = pl.program_id(0)
    count = angles * len(blocks) * quarter
    local = steps * together // 4

    @pl.when(i < steps)
    def _():
        for n in range(together):
            row = i * together + n
            r, c = lax.div(row, 4), lax.rem(row, 4)
            rows = [
                couple_ref[k, c, g * quarter : (g + 1) * quarter, :]
                for k in range(angles)
                for g in blocks
            ]
            w_high, w_low = split(jnp.concatenate(rows, axis=0))
            high, low = split(source_ref[n])
            both = dot(jnp.concatenate([w_high, w_low], axis=0), high)
            high, low = split(both[:count] + both[count:] + dot(w_high, low))
            for k in range(angles):
                lanes = slice(k * size, (k + 1) * size)
                for b in range(len(blocks)):
                    at = (k * len(blocks) + b) * quarter
                    to = pl.multiple_of((b * local + r) * channels + c * quarter, quarter)
                    m_high[pl.ds(to, quarter), lanes] = high[at : at + quarter]
                    m_low[pl.ds(to, quarter), lanes] = low[at : at + quarter]

    @pl.when(i >= steps)
    def _():
        spread_out(flip_ref[0], interpolate(high_ref, low_ref, m_high, m_low, dot_nt), out_ref)


def first_one(blocks, flip, source, couple, maps, near, devices):
    rows, channels, size = source.shape
    local = rows // 4
    angles = couple.shape[0]
    together = SOURCE_ROWS
    steps = rows // together
    out = (devices, len(blocks), near, local, size // (devices * near), channels)
    wide = len(blocks) * local * channels

    def tile(i):
        return jnp.maximum(i - steps, 0)

    return call(
        functools.partial(first_kernel, blocks, steps),
        "component_one_first",
        6 * wide * angles * size * (size + channels),
        4 * source.size + 4 * angles * size * size,
        (source, couple, *maps),
        grid=(steps + TILES,),
        in_specs=[
            pl.BlockSpec((together, channels, size), lambda i, f: (jnp.minimum(i, steps - 1), 0, 0)),
            pl.BlockSpec(couple.shape, lambda i, f: (0, 0, 0, 0)),
        ]
        + [pl.BlockSpec((size // TILES, angles * size), lambda i, f: (tile(i), 0))] * 2,
        out_specs=out_spec(out, tile),
        out_shape=jax.ShapeDtypeStruct(out, F32),
        scratch_shapes=[pltpu.VMEM((wide, angles * size), BF16)] * 2,
        scalars=(flip,),
    )


def chunk_specs(chunk):
    if not isinstance(chunk, list):
        return [chunk], [pl.BlockSpec(chunk.shape, lambda i, f: (0, 0, 0, 0, 0))]
    spec = pl.BlockSpec((1,) + chunk[0].shape[1:], lambda i, f: (0, 0, 0, 0, 0))
    return chunk, [spec] * len(chunk)


def later_kernel(blocks, counts, flip_ref, *refs):
    chunks = []
    for count in counts:
        chunks.append(refs[:count])
        refs = refs[count:]
    couple_ref, high_ref, low_ref, out_ref, w_high, w_low, m_high, m_low = refs[:8]
    wholes = list(refs[8:])
    angles, _, channels, _ = couple_ref.shape
    quarter = channels // 4
    size = high_ref.shape[1] // angles
    _, _, local, per, _ = chunks[0][0].shape

    @pl.when(pl.program_id(0) == 0)
    def _():
        lane = lax.broadcasted_iota(jnp.int32, (quarter, channels), 1)
        for k in range(angles):
            for b, g in enumerate(blocks):
                for c in range(4):
                    rows = couple_ref[k, c, g * quarter : (g + 1) * quarter, :]
                    at = (k * len(blocks) + b) * channels + c * quarter
                    inside = lax.div(lane, quarter) == c
                    for other in range(4):
                        shift = ((c - other) * quarter) % channels
                        moved = pltpu.roll(rows, shift, 1) if shift else rows
                        high, low = split(jnp.where(inside, moved, 0.0))
                        lanes = slice(other * channels, (other + 1) * channels)
                        w_high[at : at + quarter, lanes] = high
                        w_low[at : at + quarter, lanes] = low
        sources = []
        for chunk in chunks:
            if len(chunk) > 1:
                whole = wholes.pop(0)
                gather(flip_ref[1], [chunk], whole)
                sources += [(whole, b, True) for b in range(whole.shape[0])]
            else:
                sources += [(chunk[0], b, False) for b in range(chunk[0].shape[1])]
        rows = min(256, size)

        def step(t, carry):
            for r in range(local):
                pieces = []
                for ref, b, flat in sources:
                    if flat:
                        pieces.append(ref[b, r, pl.ds(pl.multiple_of(t * rows, rows), rows), :])
                    else:
                        piece = ref[pl.ds(t * (rows // per), rows // per), b, r]
                        pieces.append(piece.reshape(rows, channels))
                high, low = split(jnp.concatenate(pieces, axis=1))
                mixed = (
                    dot_nt(high, w_high[...]) + dot_nt(low, w_high[...]) + dot_nt(high, w_low[...])
                )
                high, low = split(mixed)
                for k in range(angles):
                    here = pl.ds(pl.multiple_of(k * size + t * rows, rows), rows)
                    for b in range(len(blocks)):
                        at = (k * len(blocks) + b) * channels
                        to = (b * local + r) * channels
                        m_high[here, to : to + channels] = high[:, at : at + channels]
                        m_low[here, to : to + channels] = low[:, at : at + channels]
            return carry

        lax.fori_loop(0, size // rows, step, 0)

    spread_out(flip_ref[0], interpolate(high_ref, low_ref, m_high, m_low, dot), out_ref)


def later_one(blocks, flip, chunks, couple, maps, near, devices):
    _, _, local, per, channels = chunks[0][0].shape if isinstance(chunks[0], list) else chunks[0].shape
    size = devices * per
    angles = couple.shape[0]
    out = (devices, len(blocks), near, local, size // (devices * near), channels)
    wide = len(blocks) * local * channels
    operands, specs, counts, wholes = [], [], [], []
    for chunk in chunks:
        some, some_specs = chunk_specs(chunk)
        operands += some
        specs += some_specs
        counts.append(len(some))
        if isinstance(chunk, list):
            wholes.append(pltpu.VMEM((chunk[0].shape[1], local, size, channels), F32))
    return call(
        functools.partial(later_kernel, blocks, counts),
        "component_one_later",
        6 * wide * angles * size * (size + 4 * channels),
        16 * local * size * channels + 4 * angles * size * size,
        (*operands, couple, *maps),
        grid=(TILES,),
        in_specs=specs
        + [pl.BlockSpec(couple.shape, lambda i, f: (0, 0, 0, 0))]
        + [pl.BlockSpec((size // TILES, angles * size), lambda i, f: (i, 0))] * 2,
        out_specs=out_spec(out, lambda i: i),
        out_shape=jax.ShapeDtypeStruct(out, F32),
        scratch_shapes=[pltpu.VMEM((angles * len(blocks) * channels, 4 * channels), BF16)] * 2
        + [pltpu.VMEM((angles * size, wide), BF16)] * 2
        + wholes,
        scalars=(flip,),
    )


def two_kernel(blocks, counts, flip_ref, *refs):
    chunks = []
    for count in counts:
        chunks.append(refs[:count])
        refs = refs[count:]
    couple_ref, green_ref, high_ref, low_ref, out_ref, turned, w_high, w_low, m_high, m_low = refs[:10]
    angles, _, channels, _ = couple_ref.shape
    quarter = channels // 4
    size = high_ref.shape[1] // angles
    _, _, local, per, _ = chunks[0][0].shape

    @pl.when(pl.program_id(0) == 0)
    def _():
        for k in range(angles):
            for b, g in enumerate(blocks):
                at = k * len(blocks) + b
                rows = [couple_ref[k, g, pl.ds(c, quarter, stride=4), :] for c in range(4)]
                turned[at] = jnp.concatenate(rows, axis=0).T
                rows = [turned[at, pl.ds(c, quarter, stride=4), :] for c in range(4)]
                high, low = split(jnp.concatenate(rows, axis=0))
                w_high[b, :, k * channels : (k + 1) * channels] = high
                w_low[b, :, k * channels : (k + 1) * channels] = low
        if counts[0] > 1:
            gather(flip_ref[1], chunks, refs[10])
        rows = min(256, size)

        def step(t, carry):
            for b in range(len(blocks)):
                for p in range(local):
                    if counts[0] > 1:
                        here = pl.ds(pl.multiple_of(t * rows, rows), rows)
                        value = refs[10][b, p, here, :]
                    else:
                        here = pl.ds(t * (rows // per), rows // per)
                        value = chunks[0][0][here, b, p]
                        for other in chunks[1:]:
                            value = value + other[0][here, b, p]
                        value = value.reshape(rows, channels)
                    high, low = split(value)
                    mixed = dot(high, w_high[b]) + dot(low, w_high[b]) + dot(high, w_low[b])
                    high, low = split(mixed)
                    to = (b * local + p) * channels
                    for k in range(angles):
                        here = pl.ds(pl.multiple_of(k * size + t * rows, rows), rows)
                        lanes = slice(k * channels, (k + 1) * channels)
                        m_high[here, to : to + channels] = high[:, lanes]
                        m_low[here, to : to + channels] = low[:, lanes]
            return carry

        lax.fori_loop(0, size // rows, step, 0)

    spread_out(flip_ref[0], interpolate(high_ref, low_ref, m_high, m_low, dot), out_ref, green_ref)


def component_two(blocks, flip, chunks, couple, green, maps, near, devices):
    _, _, local, per, channels = chunks[0][0].shape if isinstance(chunks[0], list) else chunks[0].shape
    size = devices * per
    angles = couple.shape[0]
    out = (devices, len(blocks), near, local, per // near, channels)
    wide = len(blocks) * local * channels
    operands, specs, counts = [], [], []
    for chunk in chunks:
        some, some_specs = chunk_specs(chunk)
        operands += some
        specs += some_specs
        counts.append(len(some))
    wholes = [pltpu.VMEM((len(blocks), local, size, channels), F32)] if counts[0] > 1 else []
    return call(
        functools.partial(two_kernel, blocks, counts),
        "component_two",
        6 * wide * angles * size * (size + channels),
        4 * len(chunks) * wide * size + 4 * angles * size * size,
        (*operands, couple, green, *maps),
        grid=(TILES,),
        in_specs=specs
        + [
            pl.BlockSpec(couple.shape, lambda i, f: (0, 0, 0, 0)),
            pl.BlockSpec((size // TILES, green.shape[1]), lambda i, f: (i, 0)),
        ]
        + [pl.BlockSpec((size // TILES, angles * size), lambda i, f: (i, 0))] * 2,
        out_specs=out_spec(out, lambda i: i),
        out_shape=jax.ShapeDtypeStruct(out, F32),
        scratch_shapes=[pltpu.VMEM((angles * len(blocks), channels, channels), F32)]
        + [pltpu.VMEM((len(blocks), channels, angles * channels), BF16)] * 2
        + [pltpu.VMEM((angles * size, wide), BF16)] * 2
        + wholes,
        scalars=(flip,),
    )


def amplitude_kernel(quarter, count, flip_ref, source_ref, *refs):
    backs, out_ref = refs[:count], refs[-1]
    if count > 1:
        out_ref, whole_ref = refs[-2:]
        per = backs[0].shape[1]
        for s in range(count):
            rows = pl.ds(pl.multiple_of((flip_ref[1] ^ s) * per, per), per)
            whole_ref[rows, :] = backs[s][0]
        turned = whole_ref[...].T
    else:
        back = backs[0][...]
        turned = back.reshape(-1, back.shape[-1]).T
    for c in range(4):
        out_ref[c] = source_ref[c] + turned[c * quarter : (c + 1) * quarter]


def amplitude_chunk(blocks, flip, source, chunk, so_far):
    rows, channels, size = source.shape
    quarter = channels // 4
    backs = chunk if isinstance(chunk, list) else [chunk]
    _, _, local, per, _ = backs[0].shape
    spec = pl.BlockSpec((4, quarter, size), lambda b, r, f: (r, blocks[0] + b, 0))
    depth = 1 if len(backs) > 1 else backs[0].shape[0]
    back_spec = pl.BlockSpec((depth, None, None, per, channels), lambda b, r, f: (0, b, r, 0, 0))
    in_specs = [spec] + [back_spec] * len(backs)
    args = [source, *backs]
    aliases = {}
    if so_far is not None:
        in_specs.append(pl.BlockSpec(memory_space=pl.ANY))
        args.append(so_far)
        aliases = {len(args): 0}
    moved = len(blocks) * local * channels * size
    return call(
        functools.partial(amplitude_kernel, quarter, len(backs)),
        "amplitude",
        moved,
        12 * moved,
        args,
        grid=(len(blocks), local),
        in_specs=in_specs,
        out_specs=spec,
        out_shape=jax.ShapeDtypeStruct(source.shape, F32),
        scratch_shapes=[pltpu.VMEM((size, channels), F32)] if len(backs) > 1 else [],
        scalars=(flip,),
        aliases=aliases,
    )


def output_kernel(quarter, flip_ref, sent_ref, *refs):
    out_ref, whole_ref, turned_ref = refs[-3:]
    devices, near, count, channels = sent_ref.shape
    per_tile = LANES // (devices * near)
    for d in range(devices):
        whole_ref[d] = sent_ref[d ^ flip_ref[0]]
    for tile in range(count // per_tile):
        rows = [
            whole_ref[:, :, tile * per_tile + i, :].reshape(devices * near, channels)
            for i in range(per_tile)
        ]
        turned = jnp.concatenate(rows, axis=0).T
        for c in range(4):
            turned_ref[tile, pl.ds(c, quarter, stride=4), :] = turned[
                c * quarter : (c + 1) * quarter
            ]
        out_ref[:, tile * LANES : (tile + 1) * LANES] = turned_ref[tile]


def component_chunk(blocks, flip, sent, so_far):
    devices, _, near, local, count, channels = sent.shape
    size = devices * near * count
    in_specs = [
        pl.BlockSpec(
            (devices, None, near, None, count, channels), lambda b, p, f: (0, b, 0, p, 0, 0)
        )
    ]
    args = [sent]
    aliases = {}
    if so_far is not None:
        in_specs.append(pl.BlockSpec(memory_space=pl.ANY))
        args.append(so_far)
        aliases = {2: 0}
    return call(
        functools.partial(output_kernel, channels // 4),
        "component_out",
        0,
        8 * sent.size,
        args,
        grid=(len(blocks), local),
        in_specs=in_specs,
        out_specs=pl.BlockSpec(
            (None, channels, size), lambda b, p, f: (4 * p + blocks[0] + b, 0, 0)
        ),
        out_shape=jax.ShapeDtypeStruct((4 * local, channels, size), F32),
        scratch_shapes=[
            pltpu.VMEM((devices, near, count, channels), F32),
            pltpu.VMEM((size // LANES, channels, LANES), F32),
        ],
        scalars=(flip,),
        aliases=aliases,
    )


def exchange(values, pairs):
    devices, blocks, near, local, count, channels = values.shape
    sent = values.reshape(devices, blocks, near, local * count, channels)
    if not pairs:
        return lax.all_to_all(sent, "mom", split_axis=0, concat_axis=0, tiled=True)
    arrived = [sent]
    for s in range(1, devices):
        route = [(d, d ^ s) for d in range(devices)]
        arrived.append(lax.ppermute(sent[s : s + 1], "mom", route))
    return arrived


CHUNKS = (((0,), False), ((1, 2, 3), True))


def shards(
    devices,
    source,
    green,
    couple_one,
    couple_two,
    p_bracket,
    q_bracket,
    p_weight,
    q_weight,
    qr_bracket,
    r_bracket,
    qr_weight,
    r_weight,
):
    rows_one, channels, size_one = source.shape
    rows_two, size_two = green.shape
    near_r, near_p = rows_one // 4, rows_two // 4
    r_size, p_size = devices * near_r, devices * near_p
    q_size = size_one // p_size
    me = lax.axis_index("mom").astype(jnp.int32)
    flips = [jnp.stack([me if pairs else jnp.int32(0), me]) for _, pairs in CHUNKS]

    first_maps = spline_maps(p_bracket, q_bracket, p_weight, q_weight, q_size)

    def by_r(array):
        lead = array.shape[:-1]
        return array.reshape(lead + (q_size, r_size)).swapaxes(-1, -2).reshape(lead + (-1,))

    second_maps = spline_maps(
        by_r(r_bracket), by_r(qr_bracket), by_r(r_weight), by_r(qr_weight), q_size
    )
    green = green.reshape(near_p, 4, q_size, r_size).transpose(3, 2, 1, 0)
    green = green.reshape(size_two, 4 * near_p)
    arrived = []
    for step in range(ITERS):
        ones = []
        for flip, (blocks, pairs) in zip(flips, CHUNKS):
            if step == 0:
                one = first_one(blocks, flip, source, couple_one, first_maps, near_p, devices)
            else:
                one = later_one(blocks, flip, backs, couple_one, first_maps, near_p, devices)
            ones.append(exchange(one, pairs))
        arrived.append(ones)
        twos = []
        backs = []
        for n, (flip, (blocks, pairs)) in enumerate(zip(flips, CHUNKS)):
            chunks = [arrived[0][n]] + ([arrived[step][n]] if step else [])
            lanes = slice(blocks[0] * near_p, (blocks[-1] + 1) * near_p)
            two = component_two(
                blocks, flip, chunks, couple_two, green[:, lanes], second_maps, near_r, devices
            )
            twos.append(two)
            backs.append(exchange(two, pairs))
    component = amplitude = None
    for flip, (blocks, _), two, back in zip(flips, CHUNKS, twos, backs):
        component = component_chunk(blocks, flip, two, component)
        amplitude = amplitude_chunk(blocks, flip, source, back, amplitude)
    return amplitude, component


def whole_map(first, second, first_weight, second_weight, first_count, second_count):
    first_rows = jnp.zeros((first.shape[0], first_count), F32)
    second_rows = jnp.zeros((second.shape[0], second_count), F32)
    first_grid = jnp.arange(first_count, dtype=jnp.int32)[None, :] - first[:, None]
    second_grid = jnp.arange(second_count, dtype=jnp.int32)[None, :] - second[:, None]
    for offset in range(4):
        first_rows += jnp.where(first_grid == offset, first_weight[offset][:, None], 0.0)
        second_rows += jnp.where(second_grid == offset, second_weight[offset][:, None], 0.0)
    return (first_rows[:, :, None] * second_rows[:, None, :]).reshape(first.shape[0], -1)


def row_mats(couple, rows, start):
    select = jax.nn.one_hot((start + jnp.arange(rows, dtype=jnp.int32)) % 4, 4, dtype=F32)
    return jnp.einsum("rc,kcmn->krmn", select, couple, precision=lax.Precision.HIGHEST)


def mix_rows(mats, values):
    return jnp.einsum("rmn,rnx->rmx", mats, values, precision=lax.Precision.HIGHEST)


def interpolate_rows(values, matrix):
    return jnp.einsum("rcx,yx->rcy", values, matrix, precision=lax.Precision.HIGHEST)


def shards_by_row(
    devices,
    source,
    green,
    couple_one,
    couple_two,
    p_bracket,
    q_bracket,
    p_weight,
    q_weight,
    qr_bracket,
    r_bracket,
    qr_weight,
    r_weight,
):
    rows_one, channels, size_one = source.shape
    rows_two, size_two = green.shape
    angles = couple_one.shape[0]
    quarter = channels // 4
    r_size, p_size = devices * rows_one // 4, devices * rows_two // 4
    q_size = size_one // p_size
    here = lax.axis_index("mom")
    first = [
        whole_map(p_bracket[k], q_bracket[k], p_weight[k], q_weight[k], p_size, q_size)
        for k in range(angles)
    ]
    second = [
        whole_map(qr_bracket[k], r_bracket[k], qr_weight[k], r_weight[k], q_size, r_size)
        for k in range(angles)
    ]
    mats_one = row_mats(couple_one, rows_one, here * rows_one)
    mats_two = row_mats(couple_two, rows_two, here * rows_two)
    state = source
    for step in range(ITERS):
        one = sum(interpolate_rows(mix_rows(mats_one[k], state), first[k]) for k in range(angles))
        sent = one.reshape(rows_one, 4, quarter, p_size, q_size).transpose(3, 1, 0, 2, 4)
        sent = sent.reshape(4 * p_size, rows_one, quarter * q_size)
        sent = lax.all_to_all(sent, "mom", split_axis=0, concat_axis=1, tiled=True)
        sent = sent.reshape(rows_two, r_size, 4, quarter, q_size).transpose(0, 3, 2, 4, 1)
        sent = sent.reshape(rows_two, channels, size_two)
        total = sum(mix_rows(mats_two[k], interpolate_rows(sent, second[k])) for k in range(angles))
        component = green[:, None, :] * total
        back = component.reshape(rows_two, quarter, 4, q_size, r_size).transpose(4, 2, 0, 1, 3)
        back = back.reshape(4 * r_size, rows_two, quarter * q_size)
        back = lax.all_to_all(back, "mom", split_axis=0, concat_axis=1, tiled=True)
        back = back.reshape(rows_one, p_size, 4, quarter, q_size).transpose(0, 2, 3, 1, 4)
        state = source + back.reshape(source.shape)
    return state, component


def solution(mesh):
    spread = ("energy", "mom")
    placed = (P(spread, None, None), P(spread, None)) + (P(),) * 10
    devices = mesh.shape["mom"]

    def body(source, green, *rest):
        whole_rows = source.shape[0] % 4 == 0 and green.shape[0] % 4 == 0
        chosen = shards if whole_rows and source.shape[1] == LANES else shards_by_row
        return chosen(devices, source, green, *rest)

    return jax.shard_map(
        body,
        mesh=mesh,
        in_specs=placed,
        out_specs=(P(spread, None, None), P(spread, None, None)),
        check_vma=False,
    )
```

```python
import functools


import jax
import jax.numpy as jnp
from jax import lax
from jax.experimental import pallas as pl
from jax.experimental.pallas import tpu as pltpu
from jax.sharding import PartitionSpec as P

ITERS = 2
LANES = 128
F32 = jnp.float32
BF16 = jnp.bfloat16
VMEM_LIMIT = 60 << 20
MAP_ROWS = 512
TILES = 2
SOURCE_ROWS = 4


def split(value):
    high = value.astype(BF16)
    return high, (value - high.astype(F32)).astype(BF16)


def dot(a, b):
    return jnp.dot(a, b, preferred_element_type=F32)


def dot_nt(a, b):
    return lax.dot_general(a, b, (((1,), (1,)), ((), ())), preferred_element_type=F32)


def call(kernel, flops, moved, args, grid, in_specs, out_specs, out_shape, scratch_shapes=(), scalars=(), aliases=None):
    return pl.pallas_call(
        kernel,
        grid_spec=pltpu.PrefetchScalarGridSpec(
            num_scalar_prefetch=len(scalars),
            grid=grid,
            in_specs=in_specs,
            out_specs=out_specs,
            scratch_shapes=scratch_shapes,
        ),
        out_shape=out_shape,
        input_output_aliases=aliases or {},
        compiler_params=pltpu.CompilerParams(vmem_limit_bytes=VMEM_LIMIT),
        cost_estimate=pl.CostEstimate(flops=flops, bytes_accessed=moved, transcendentals=0),
    )(*scalars, *args)


def map_kernel(count, first_ref, second_ref, first_weight_ref, second_weight_ref, high_ref, low_ref):
    rows, columns = high_ref.shape
    k = pl.program_id(0)
    table = jnp.concatenate(
        [
            first_ref[pl.ds(k, 1), :].astype(F32),
            second_ref[pl.ds(k, 1), :].astype(F32),
            first_weight_ref[...],
            second_weight_ref[...],
            jnp.zeros((6, rows), F32),
        ],
        axis=0,
    ).T
    lane = lax.broadcasted_iota(jnp.int32, (1, LANES), 1)
    group = lax.div(lane, count)

    def factor(index, base):
        grid = index.astype(F32) - table[:, base : base + 1]
        total = jnp.zeros((rows, LANES), F32)
        for offset in range(4):
            column = 2 + 4 * base + offset
            total = jnp.where(grid == offset, table[:, column : column + 1], total)
        return total

    first_high, first_low = split(factor(lane, 0))
    second = factor(lane - group * count, 1)
    node = lax.broadcasted_iota(jnp.int32, (LANES, columns), 0)
    column = lax.broadcasted_iota(jnp.int32, (LANES, columns), 1)
    chosen = jnp.where(
        jnp.logical_and(column >= node * count, column < (node + 1) * count), 1.0, 0.0
    ).astype(BF16)
    for tile in range(columns // LANES):
        lanes = slice(tile * LANES, (tile + 1) * LANES)
        spread = dot(first_high, chosen[:, lanes]) + dot(first_low, chosen[:, lanes])
        high, low = split(spread * second)
        high_ref[:, lanes] = high
        low_ref[:, lanes] = low


def spline_maps(first, second, first_weight, second_weight, count):
    angles, size = first.shape
    tile = min(MAP_ROWS, size)
    out = jax.ShapeDtypeStruct((size, angles * size), BF16)
    spec = pl.BlockSpec((tile, size), lambda k, i: (i, k))
    return call(
        functools.partial(map_kernel, count),
        10 * angles * size * size,
        4 * angles * size * size,
        (first, second, first_weight, second_weight),
        grid=(angles, size // tile),
        in_specs=[pl.BlockSpec((angles, tile), lambda k, i: (0, i))] * 2
        + [pl.BlockSpec((None, 4, tile), lambda k, i: (k, 0, i))] * 2,
        out_specs=[spec, spec],
        out_shape=[out, out],
    )


def interpolate(high_ref, low_ref, mixed_high, mixed_low, product):
    high = high_ref[...]
    return (
        product(high, mixed_high[...])
        + product(high, mixed_low[...])
        + product(low_ref[...], mixed_high[...])
    )


def spread_out(flip, value, out_ref, scale_ref=None):
    parts, blocks, near, local, count, channels = out_ref.shape
    rows = near * count
    for b in range(blocks):
        for n in range(local):
            at = b * local + n
            block = value[:, at * channels : (at + 1) * channels]
            if scale_ref is not None:
                block = block * scale_ref[:, at : at + 1]
            for j in range(parts):
                piece = block[j * rows : (j + 1) * rows].reshape(near, count, channels)
                out_ref[j ^ (flip & (parts - 1)), b, :, n, :, :] = piece


def out_spec(shape, tile):
    parts = shape[0] // TILES
    return pl.BlockSpec(
        (parts,) + shape[1:],
        lambda i, flip: (tile(i) ^ lax.div(flip[0], parts), 0, 0, 0, 0, 0),
    )


def gather(me, sets, whole_ref):
    blocks, local, _, _ = whole_ref.shape
    per = sets[0][0].shape[3]
    for s in range(len(sets[0])):
        rows = pl.ds(pl.multiple_of((me ^ s) * per, per), per)
        for b in range(blocks):
            for n in range(local):
                value = sets[0][s][0, b, n]
                for other in sets[1:]:
                    value = value + other[s][0, b, n]
                whole_ref[b, n, rows, :] = value


def first_kernel(blocks, steps, flip_ref, source_ref, couple_ref, high_ref, low_ref, out_ref, m_high, m_low):
    angles, _, channels, _ = couple_ref.shape
    quarter = channels // 4
    together, _, size = source_ref.shape
    i = pl.program_id(0)
    count = angles * len(blocks) * quarter
    local = steps * together // 4

    @pl.when(i < steps)
    def _():
        for n in range(together):
            row = i * together + n
            r, c = lax.div(row, 4), lax.rem(row, 4)
            rows = [
                couple_ref[k, c, g * quarter : (g + 1) * quarter, :]
                for k in range(angles)
                for g in blocks
            ]
            w_high, w_low = split(jnp.concatenate(rows, axis=0))
            high, low = split(source_ref[n])
            both = dot(jnp.concatenate([w_high, w_low], axis=0), high)
            high, low = split(both[:count] + both[count:] + dot(w_high, low))
            for k in range(angles):
                lanes = slice(k * size, (k + 1) * size)
                for b in range(len(blocks)):
                    at = (k * len(blocks) + b) * quarter
                    to = pl.multiple_of((b * local + r) * channels + c * quarter, quarter)
                    m_high[pl.ds(to, quarter), lanes] = high[at : at + quarter]
                    m_low[pl.ds(to, quarter), lanes] = low[at : at + quarter]

    @pl.when(i >= steps)
    def _():
        spread_out(flip_ref[0], interpolate(high_ref, low_ref, m_high, m_low, dot_nt), out_ref)


def first_one(blocks, flip, source, couple, maps, near, devices):
    rows, channels, size = source.shape
    local = rows // 4
    angles = couple.shape[0]
    together = SOURCE_ROWS
    steps = rows // together
    out = (devices, len(blocks), near, local, size // (devices * near), channels)
    wide = len(blocks) * local * channels

    def tile(i):
        return jnp.maximum(i - steps, 0)

    return call(
        functools.partial(first_kernel, blocks, steps),
        6 * wide * angles * size * (size + channels),
        4 * source.size + 4 * angles * size * size,
        (source, couple, *maps),
        grid=(steps + TILES,),
        in_specs=[
            pl.BlockSpec((together, channels, size), lambda i, f: (jnp.minimum(i, steps - 1), 0, 0)),
            pl.BlockSpec(couple.shape, lambda i, f: (0, 0, 0, 0)),
        ]
        + [pl.BlockSpec((size // TILES, angles * size), lambda i, f: (tile(i), 0))] * 2,
        out_specs=out_spec(out, tile),
        out_shape=jax.ShapeDtypeStruct(out, F32),
        scratch_shapes=[pltpu.VMEM((wide, angles * size), BF16)] * 2,
        scalars=(flip,),
    )


def chunk_specs(chunk):
    if not isinstance(chunk, list):
        return [chunk], [pl.BlockSpec(chunk.shape, lambda i, f: (0, 0, 0, 0, 0))]
    spec = pl.BlockSpec((1,) + chunk[0].shape[1:], lambda i, f: (0, 0, 0, 0, 0))
    return chunk, [spec] * len(chunk)


def later_kernel(blocks, counts, flip_ref, *refs):
    chunks = []
    for count in counts:
        chunks.append(refs[:count])
        refs = refs[count:]
    couple_ref, high_ref, low_ref, out_ref, w_high, w_low, m_high, m_low = refs[:8]
    wholes = list(refs[8:])
    angles, _, channels, _ = couple_ref.shape
    quarter = channels // 4
    size = high_ref.shape[1] // angles
    _, _, local, per, _ = chunks[0][0].shape

    @pl.when(pl.program_id(0) == 0)
    def _():
        lane = lax.broadcasted_iota(jnp.int32, (quarter, channels), 1)
        for k in range(angles):
            for b, g in enumerate(blocks):
                for c in range(4):
                    rows = couple_ref[k, c, g * quarter : (g + 1) * quarter, :]
                    at = (k * len(blocks) + b) * channels + c * quarter
                    inside = lax.div(lane, quarter) == c
                    for other in range(4):
                        shift = ((c - other) * quarter) % channels
                        moved = pltpu.roll(rows, shift, 1) if shift else rows
                        high, low = split(jnp.where(inside, moved, 0.0))
                        lanes = slice(other * channels, (other + 1) * channels)
                        w_high[at : at + quarter, lanes] = high
                        w_low[at : at + quarter, lanes] = low
        sources = []
        for chunk in chunks:
            if len(chunk) > 1:
                whole = wholes.pop(0)
                gather(flip_ref[1], [chunk], whole)
                sources += [(whole, b, True) for b in range(whole.shape[0])]
            else:
                sources += [(chunk[0], b, False) for b in range(chunk[0].shape[1])]
        rows = min(256, size)

        def step(t, carry):
            for r in range(local):
                pieces = []
                for ref, b, flat in sources:
                    if flat:
                        pieces.append(ref[b, r, pl.ds(pl.multiple_of(t * rows, rows), rows), :])
                    else:
                        piece = ref[pl.ds(t * (rows // per), rows // per), b, r]
                        pieces.append(piece.reshape(rows, channels))
                high, low = split(jnp.concatenate(pieces, axis=1))
                mixed = (
                    dot_nt(high, w_high[...]) + dot_nt(low, w_high[...]) + dot_nt(high, w_low[...])
                )
                high, low = split(mixed)
                for k in range(angles):
                    here = pl.ds(pl.multiple_of(k * size + t * rows, rows), rows)
                    for b in range(len(blocks)):
                        at = (k * len(blocks) + b) * channels
                        to = (b * local + r) * channels
                        m_high[here, to : to + channels] = high[:, at : at + channels]
                        m_low[here, to : to + channels] = low[:, at : at + channels]
            return carry

        lax.fori_loop(0, size // rows, step, 0)

    spread_out(flip_ref[0], interpolate(high_ref, low_ref, m_high, m_low, dot), out_ref)


def later_one(blocks, flip, chunks, couple, maps, near, devices):
    _, _, local, per, channels = chunks[0][0].shape if isinstance(chunks[0], list) else chunks[0].shape
    size = devices * per
    angles = couple.shape[0]
    out = (devices, len(blocks), near, local, size // (devices * near), channels)
    wide = len(blocks) * local * channels
    operands, specs, counts, wholes = [], [], [], []
    for chunk in chunks:
        some, some_specs = chunk_specs(chunk)
        operands += some
        specs += some_specs
        counts.append(len(some))
        if isinstance(chunk, list):
            wholes.append(pltpu.VMEM((chunk[0].shape[1], local, size, channels), F32))
    return call(
        functools.partial(later_kernel, blocks, counts),
        6 * wide * angles * size * (size + 4 * channels),
        16 * local * size * channels + 4 * angles * size * size,
        (*operands, couple, *maps),
        grid=(TILES,),
        in_specs=specs
        + [pl.BlockSpec(couple.shape, lambda i, f: (0, 0, 0, 0))]
        + [pl.BlockSpec((size // TILES, angles * size), lambda i, f: (i, 0))] * 2,
        out_specs=out_spec(out, lambda i: i),
        out_shape=jax.ShapeDtypeStruct(out, F32),
        scratch_shapes=[pltpu.VMEM((angles * len(blocks) * channels, 4 * channels), BF16)] * 2
        + [pltpu.VMEM((angles * size, wide), BF16)] * 2
        + wholes,
        scalars=(flip,),
    )


def two_kernel(blocks, counts, flip_ref, *refs):
    chunks = []
    for count in counts:
        chunks.append(refs[:count])
        refs = refs[count:]
    couple_ref, green_ref, high_ref, low_ref, out_ref, turned, w_high, w_low, m_high, m_low = refs[:10]
    angles, _, channels, _ = couple_ref.shape
    quarter = channels // 4
    size = high_ref.shape[1] // angles
    _, _, local, per, _ = chunks[0][0].shape

    @pl.when(pl.program_id(0) == 0)
    def _():
        for k in range(angles):
            for b, g in enumerate(blocks):
                at = k * len(blocks) + b
                rows = [couple_ref[k, g, pl.ds(c, quarter, stride=4), :] for c in range(4)]
                turned[at] = jnp.concatenate(rows, axis=0).T
                rows = [turned[at, pl.ds(c, quarter, stride=4), :] for c in range(4)]
                high, low = split(jnp.concatenate(rows, axis=0))
                w_high[b, :, k * channels : (k + 1) * channels] = high
                w_low[b, :, k * channels : (k + 1) * channels] = low
        if counts[0] > 1:
            gather(flip_ref[1], chunks, refs[10])
        rows = min(256, size)

        def step(t, carry):
            for b in range(len(blocks)):
                for p in range(local):
                    if counts[0] > 1:
                        here = pl.ds(pl.multiple_of(t * rows, rows), rows)
                        value = refs[10][b, p, here, :]
                    else:
                        here = pl.ds(t * (rows // per), rows // per)
                        value = chunks[0][0][here, b, p]
                        for other in chunks[1:]:
                            value = value + other[0][here, b, p]
                        value = value.reshape(rows, channels)
                    high, low = split(value)
                    mixed = dot(high, w_high[b]) + dot(low, w_high[b]) + dot(high, w_low[b])
                    high, low = split(mixed)
                    to = (b * local + p) * channels
                    for k in range(angles):
                        here = pl.ds(pl.multiple_of(k * size + t * rows, rows), rows)
                        lanes = slice(k * channels, (k + 1) * channels)
                        m_high[here, to : to + channels] = high[:, lanes]
                        m_low[here, to : to + channels] = low[:, lanes]
            return carry

        lax.fori_loop(0, size // rows, step, 0)

    spread_out(flip_ref[0], interpolate(high_ref, low_ref, m_high, m_low, dot), out_ref, green_ref)


def component_two(blocks, flip, chunks, couple, green, maps, near, devices):
    _, _, local, per, channels = chunks[0][0].shape if isinstance(chunks[0], list) else chunks[0].shape
    size = devices * per
    angles = couple.shape[0]
    out = (devices, len(blocks), near, local, per // near, channels)
    wide = len(blocks) * local * channels
    operands, specs, counts = [], [], []
    for chunk in chunks:
        some, some_specs = chunk_specs(chunk)
        operands += some
        specs += some_specs
        counts.append(len(some))
    wholes = [pltpu.VMEM((len(blocks), local, size, channels), F32)] if counts[0] > 1 else []
    return call(
        functools.partial(two_kernel, blocks, counts),
        6 * wide * angles * size * (size + channels),
        4 * len(chunks) * wide * size + 4 * angles * size * size,
        (*operands, couple, green, *maps),
        grid=(TILES,),
        in_specs=specs
        + [
            pl.BlockSpec(couple.shape, lambda i, f: (0, 0, 0, 0)),
            pl.BlockSpec((size // TILES, green.shape[1]), lambda i, f: (i, 0)),
        ]
        + [pl.BlockSpec((size // TILES, angles * size), lambda i, f: (i, 0))] * 2,
        out_specs=out_spec(out, lambda i: i),
        out_shape=jax.ShapeDtypeStruct(out, F32),
        scratch_shapes=[pltpu.VMEM((angles * len(blocks), channels, channels), F32)]
        + [pltpu.VMEM((len(blocks), channels, angles * channels), BF16)] * 2
        + [pltpu.VMEM((angles * size, wide), BF16)] * 2
        + wholes,
        scalars=(flip,),
    )


def amplitude_kernel(quarter, count, flip_ref, source_ref, *refs):
    backs, out_ref = refs[:count], refs[-1]
    if count > 1:
        out_ref, whole_ref = refs[-2:]
        per = backs[0].shape[1]
        for s in range(count):
            rows = pl.ds(pl.multiple_of((flip_ref[1] ^ s) * per, per), per)
            whole_ref[rows, :] = backs[s][0]
        turned = whole_ref[...].T
    else:
        back = backs[0][...]
        turned = back.reshape(-1, back.shape[-1]).T
    for c in range(4):
        out_ref[c] = source_ref[c] + turned[c * quarter : (c + 1) * quarter]


def amplitude_chunk(blocks, flip, source, chunk, so_far):
    _, channels, size = source.shape
    quarter = channels // 4
    backs = chunk if isinstance(chunk, list) else [chunk]
    _, _, local, per, _ = backs[0].shape
    spec = pl.BlockSpec((4, quarter, size), lambda b, r, f: (r, blocks[0] + b, 0))
    depth = 1 if len(backs) > 1 else backs[0].shape[0]
    back_spec = pl.BlockSpec((depth, None, None, per, channels), lambda b, r, f: (0, b, r, 0, 0))
    in_specs = [spec] + [back_spec] * len(backs)
    args = [source, *backs]
    aliases = {}
    if so_far is not None:
        in_specs.append(pl.BlockSpec(memory_space=pl.ANY))
        args.append(so_far)
        aliases = {len(args): 0}
    moved = len(blocks) * local * channels * size
    return call(
        functools.partial(amplitude_kernel, quarter, len(backs)),
        moved,
        12 * moved,
        args,
        grid=(len(blocks), local),
        in_specs=in_specs,
        out_specs=spec,
        out_shape=jax.ShapeDtypeStruct(source.shape, F32),
        scratch_shapes=[pltpu.VMEM((size, channels), F32)] if len(backs) > 1 else [],
        scalars=(flip,),
        aliases=aliases,
    )


def output_kernel(quarter, flip_ref, sent_ref, *refs):
    out_ref, whole_ref, turned_ref = refs[-3:]
    devices, near, count, channels = sent_ref.shape
    per_tile = LANES // (devices * near)
    for d in range(devices):
        whole_ref[d] = sent_ref[d ^ flip_ref[0]]
    for tile in range(count // per_tile):
        rows = [
            whole_ref[:, :, tile * per_tile + i, :].reshape(devices * near, channels)
            for i in range(per_tile)
        ]
        turned = jnp.concatenate(rows, axis=0).T
        for c in range(4):
            turned_ref[tile, pl.ds(c, quarter, stride=4), :] = turned[
                c * quarter : (c + 1) * quarter
            ]
        out_ref[:, tile * LANES : (tile + 1) * LANES] = turned_ref[tile]


def component_chunk(blocks, flip, sent, so_far):
    devices, _, near, local, count, channels = sent.shape
    size = devices * near * count
    in_specs = [
        pl.BlockSpec(
            (devices, None, near, None, count, channels), lambda b, p, f: (0, b, 0, p, 0, 0)
        )
    ]
    args = [sent]
    aliases = {}
    if so_far is not None:
        in_specs.append(pl.BlockSpec(memory_space=pl.ANY))
        args.append(so_far)
        aliases = {2: 0}
    return call(
        functools.partial(output_kernel, channels // 4),
        0,
        8 * sent.size,
        args,
        grid=(len(blocks), local),
        in_specs=in_specs,
        out_specs=pl.BlockSpec(
            (None, channels, size), lambda b, p, f: (4 * p + blocks[0] + b, 0, 0)
        ),
        out_shape=jax.ShapeDtypeStruct((4 * local, channels, size), F32),
        scratch_shapes=[
            pltpu.VMEM((devices, near, count, channels), F32),
            pltpu.VMEM((size // LANES, channels, LANES), F32),
        ],
        scalars=(flip,),
        aliases=aliases,
    )


def exchange(values, pairs):
    devices, blocks, near, local, count, channels = values.shape
    sent = values.reshape(devices, blocks, near, local * count, channels)
    if not pairs:
        return lax.all_to_all(sent, "mom", split_axis=0, concat_axis=0, tiled=True)
    arrived = [sent]
    for s in range(1, devices):
        route = [(d, d ^ s) for d in range(devices)]
        arrived.append(lax.ppermute(sent[s : s + 1], "mom", route))
    return arrived


CHUNKS = (((0, 1), False), ((2, 3), True))


def shards(
    devices,
    source,
    green,
    couple_one,
    couple_two,
    p_bracket,
    q_bracket,
    p_weight,
    q_weight,
    qr_bracket,
    r_bracket,
    qr_weight,
    r_weight,
):
    rows_one, _, size_one = source.shape
    rows_two, size_two = green.shape
    near_r, near_p = rows_one // 4, rows_two // 4
    r_size, p_size = devices * near_r, devices * near_p
    q_size = size_one // p_size
    me = lax.axis_index("mom").astype(jnp.int32)
    flips = [jnp.stack([me if pairs else jnp.int32(0), me]) for _, pairs in CHUNKS]

    first_maps = spline_maps(p_bracket, q_bracket, p_weight, q_weight, q_size)

    def by_r(array):
        lead = array.shape[:-1]
        return array.reshape(lead + (q_size, r_size)).swapaxes(-1, -2).reshape(lead + (-1,))

    second_maps = spline_maps(
        by_r(r_bracket), by_r(qr_bracket), by_r(r_weight), by_r(qr_weight), q_size
    )
    green = green.reshape(near_p, 4, q_size, r_size).transpose(3, 2, 1, 0)
    green = green.reshape(size_two, 4 * near_p)
    arrived = []
    for step in range(ITERS):
        ones = []
        for flip, (blocks, pairs) in zip(flips, CHUNKS):
            if step == 0:
                one = first_one(blocks, flip, source, couple_one, first_maps, near_p, devices)
            else:
                one = later_one(blocks, flip, backs, couple_one, first_maps, near_p, devices)
            ones.append(exchange(one, pairs))
        arrived.append(ones)
        twos = []
        backs = []
        for n, (flip, (blocks, pairs)) in enumerate(zip(flips, CHUNKS)):
            chunks = [arrived[0][n]] + ([arrived[step][n]] if step else [])
            lanes = slice(blocks[0] * near_p, (blocks[-1] + 1) * near_p)
            scale = green[:, lanes]
            two = component_two(
                blocks, flip, chunks, couple_two, scale, second_maps, near_r, devices
            )
            twos.append(two)
            backs.append(exchange(two, pairs))
    component = amplitude = None
    for flip, (blocks, _), two, back in zip(flips, CHUNKS, twos, backs):
        component = component_chunk(blocks, flip, two, component)
        amplitude = amplitude_chunk(blocks, flip, source, back, amplitude)
    return amplitude, component


def whole_map(first, second, first_weight, second_weight, first_count, second_count):
    first_rows = jnp.zeros((first.shape[0], first_count), F32)
    second_rows = jnp.zeros((second.shape[0], second_count), F32)
    first_grid = jnp.arange(first_count, dtype=jnp.int32)[None, :] - first[:, None]
    second_grid = jnp.arange(second_count, dtype=jnp.int32)[None, :] - second[:, None]
    for offset in range(4):
        first_rows += jnp.where(first_grid == offset, first_weight[offset][:, None], 0.0)
        second_rows += jnp.where(second_grid == offset, second_weight[offset][:, None], 0.0)
    return (first_rows[:, :, None] * second_rows[:, None, :]).reshape(first.shape[0], -1)


def row_mats(couple, rows, start):
    select = jax.nn.one_hot((start + jnp.arange(rows, dtype=jnp.int32)) % 4, 4, dtype=F32)
    return jnp.einsum("rc,kcmn->krmn", select, couple, precision=lax.Precision.HIGHEST)


def mix_rows(mats, values):
    return jnp.einsum("rmn,rnx->rmx", mats, values, precision=lax.Precision.HIGHEST)


def interpolate_rows(values, matrix):
    return jnp.einsum("rcx,yx->rcy", values, matrix, precision=lax.Precision.HIGHEST)


def shards_by_row(
    devices,
    source,
    green,
    couple_one,
    couple_two,
    p_bracket,
    q_bracket,
    p_weight,
    q_weight,
    qr_bracket,
    r_bracket,
    qr_weight,
    r_weight,
):
    rows_one, channels, size_one = source.shape
    rows_two, size_two = green.shape
    angles = couple_one.shape[0]
    quarter = channels // 4
    r_size, p_size = devices * rows_one // 4, devices * rows_two // 4
    q_size = size_one // p_size
    here = lax.axis_index("mom")
    first = [
        whole_map(p_bracket[k], q_bracket[k], p_weight[k], q_weight[k], p_size, q_size)
        for k in range(angles)
    ]
    second = [
        whole_map(qr_bracket[k], r_bracket[k], qr_weight[k], r_weight[k], q_size, r_size)
        for k in range(angles)
    ]
    mats_one = row_mats(couple_one, rows_one, here * rows_one)
    mats_two = row_mats(couple_two, rows_two, here * rows_two)
    state = source
    for _ in range(ITERS):
        one = sum(interpolate_rows(mix_rows(mats_one[k], state), first[k]) for k in range(angles))
        sent = one.reshape(rows_one, 4, quarter, p_size, q_size).transpose(3, 1, 0, 2, 4)
        sent = sent.reshape(4 * p_size, rows_one, quarter * q_size)
        sent = lax.all_to_all(sent, "mom", split_axis=0, concat_axis=1, tiled=True)
        sent = sent.reshape(rows_two, r_size, 4, quarter, q_size).transpose(0, 3, 2, 4, 1)
        sent = sent.reshape(rows_two, channels, size_two)
        total = sum(mix_rows(mats_two[k], interpolate_rows(sent, second[k])) for k in range(angles))
        component = green[:, None, :] * total
        back = component.reshape(rows_two, quarter, 4, q_size, r_size).transpose(4, 2, 0, 1, 3)
        back = back.reshape(4 * r_size, rows_two, quarter * q_size)
        back = lax.all_to_all(back, "mom", split_axis=0, concat_axis=1, tiled=True)
        back = back.reshape(rows_one, p_size, 4, quarter, q_size).transpose(0, 2, 3, 1, 4)
        state = source + back.reshape(source.shape)
    return state, component


def solution(mesh):
    spread = ("energy", "mom")
    placed = (P(spread, None, None), P(spread, None)) + (P(),) * 10
    devices = mesh.shape["mom"]

    def body(source, green, *rest):
        whole_rows = source.shape[0] % 4 == 0 and green.shape[0] % 4 == 0
        chosen = shards if whole_rows and source.shape[1] == LANES else shards_by_row
        return chosen(devices, source, green, *rest)

    return jax.shard_map(
        body,
        mesh=mesh,
        in_specs=placed,
        out_specs=(P(spread, None, None), P(spread, None, None)),
        check_vma=False,
    )
```

```python
import functools


import jax
import jax.numpy as jnp
from jax import lax
from jax.experimental import pallas as pl
from jax.experimental.pallas import tpu as pltpu
from jax.sharding import PartitionSpec as P

ITERS = 2
LANES = 128
F32 = jnp.float32
BF16 = jnp.bfloat16
VMEM_LIMIT = 60 << 20
PIECES = 4
TILES = 4
SOURCE_ROWS = 4


def split(value):
    high = value.astype(BF16)
    return high, (value - high.astype(F32)).astype(BF16)


def dot(a, b):
    return jnp.dot(a, b, preferred_element_type=F32)


def dot_nt(a, b):
    return lax.dot_general(a, b, (((1,), (1,)), ((), ())), preferred_element_type=F32)


def call(kernel, flops, moved, args, grid, in_specs, out_specs, out_shape, scratch_shapes=(), scalars=(), aliases=None):
    return pl.pallas_call(
        kernel,
        grid_spec=pltpu.PrefetchScalarGridSpec(
            num_scalar_prefetch=len(scalars),
            grid=grid,
            in_specs=in_specs,
            out_specs=out_specs,
            scratch_shapes=scratch_shapes,
        ),
        out_shape=out_shape,
        input_output_aliases=aliases or {},
        compiler_params=pltpu.CompilerParams(vmem_limit_bytes=VMEM_LIMIT),
        cost_estimate=pl.CostEstimate(flops=flops, bytes_accessed=moved, transcendentals=0),
    )(*scalars, *args)


def map_factors(count, k, rows, first_ref, second_ref, first_weight_ref, second_weight_ref):
    size = rows.size
    table = jnp.concatenate(
        [
            first_ref[k : k + 1, rows].astype(F32),
            second_ref[k : k + 1, rows].astype(F32),
            first_weight_ref[k, :, rows],
            second_weight_ref[k, :, rows],
            jnp.zeros((6, size), F32),
        ],
        axis=0,
    ).T
    lane = lax.broadcasted_iota(jnp.int32, (1, LANES), 1)

    def factor(index, base):
        grid = index.astype(F32) - table[:, base : base + 1]
        total = jnp.zeros((size, LANES), F32)
        for offset in range(4):
            column = 2 + 4 * base + offset
            total = jnp.where(grid == offset, table[:, column : column + 1], total)
        return total

    high, low = split(factor(lane, 0))
    return high, low, factor(lane - lax.div(lane, count) * count, 1)


def chosen_nodes(count, columns):
    node = lax.broadcasted_iota(jnp.int32, (LANES, columns), 0)
    column = lax.broadcasted_iota(jnp.int32, (LANES, columns), 1)
    inside = jnp.logical_and(column >= node * count, column < (node + 1) * count)
    return jnp.where(inside, 1.0, 0.0).astype(BF16)


def build_rows(count, rows, inputs, chosen, high_ref, low_ref):
    angles, size = inputs[0].shape
    for k in range(angles):
        first_high, first_low, second = map_factors(count, k, rows, *inputs)
        for tile in range(size // LANES):
            lanes = slice(tile * LANES, (tile + 1) * LANES)
            spread = dot(first_high, chosen[:, lanes]) + dot(first_low, chosen[:, lanes])
            high, low = split(spread * second)
            lanes = slice(k * size + tile * LANES, k * size + (tile + 1) * LANES)
            high_ref[:, lanes] = high
            low_ref[:, lanes] = low


def map_kernel(count, *refs):
    inputs, (high_ref, low_ref) = refs[:4], refs[4:]
    size = high_ref.shape[0]
    start = pl.multiple_of(pl.program_id(0) * size, size)
    chosen = chosen_nodes(count, inputs[0].shape[1])
    build_rows(count, pl.ds(start, size), inputs, chosen, high_ref, low_ref)


def spline_maps(first, second, first_weight, second_weight, count):
    angles, size = first.shape
    tile = size // PIECES
    out = jax.ShapeDtypeStruct((size, angles * size), BF16)
    spec = pl.BlockSpec((tile, angles * size), lambda i: (i, 0))
    return call(
        functools.partial(map_kernel, count),
        10 * angles * size * size,
        4 * angles * size * size,
        (first, second, first_weight, second_weight),
        grid=(PIECES,),
        in_specs=[pl.BlockSpec(memory_space=pltpu.VMEM)] * 4,
        out_specs=[spec, spec],
        out_shape=[out, out],
    )


def interpolate(high_ref, low_ref, mixed_high, mixed_low, product):
    high = high_ref[...]
    return (
        product(high, mixed_high[...])
        + product(high, mixed_low[...])
        + product(low_ref[...], mixed_high[...])
    )


def spread_out(flip, value, out_ref, scale_ref=None):
    parts, blocks, near, local, count, channels = out_ref.shape
    rows = near * count
    for b in range(blocks):
        for n in range(local):
            at = b * local + n
            block = value[:, at * channels : (at + 1) * channels]
            if scale_ref is not None:
                block = block * scale_ref[:, at : at + 1]
            for j in range(parts):
                piece = block[j * rows : (j + 1) * rows].reshape(near, count, channels)
                out_ref[j ^ (flip & (parts - 1)), b, :, n, :, :] = piece


def out_spec(shape, tile):
    parts = shape[0] // TILES
    return pl.BlockSpec(
        (parts,) + shape[1:],
        lambda i, flip: (tile(i) ^ lax.div(flip[0], parts), 0, 0, 0, 0, 0),
    )


def gather(me, sets, whole_ref):
    blocks, local, _, _ = whole_ref.shape
    per = sets[0][0].shape[3]
    for s in range(len(sets[0])):
        rows = pl.ds(pl.multiple_of((me ^ s) * per, per), per)
        for b in range(blocks):
            for n in range(local):
                value = sets[0][s][0, b, n]
                for other in sets[1:]:
                    value = value + other[s][0, b, n]
                whole_ref[b, n, rows, :] = value


def finish_rows(flip, t, value, held_ref, out_ref, sems, scale_ref=None):
    devices, blocks, near, local, count, channels = held_ref.shape
    parts = devices // PIECES
    rows = near * count
    group = t ^ lax.div(flip, parts)
    for b in range(blocks):
        for n in range(local):
            at = b * local + n
            block = value[:, at * channels : (at + 1) * channels]
            if scale_ref is not None:
                start = pl.multiple_of(t * parts * rows, parts * rows)
                block = block * scale_ref[pl.ds(start, parts * rows), at : at + 1]
            for j in range(parts):
                piece = block[j * rows : (j + 1) * rows].reshape(near, count, channels)
                held_ref[group * parts + (j ^ (flip & (parts - 1))), b, :, n, :, :] = piece
    part = pl.ds(group * parts, parts)
    pltpu.make_async_copy(held_ref.at[part], out_ref.at[part], sems.at[group]).start()


def finish_copies(held_ref, out_ref, sems):
    parts = held_ref.shape[0] // PIECES
    for t in range(PIECES):
        part = pl.ds(t * parts, parts)
        pltpu.make_async_copy(held_ref.at[part], out_ref.at[part], sems.at[t]).wait()


def mix_source(blocks, source_ref, held, sems, couple_ref, m_high, m_low):
    angles, _, channels, _ = couple_ref.shape
    rows, _, size = held.shape
    quarter = channels // 4
    count = angles * len(blocks) * quarter
    local = rows // 4

    def step(row, carry):
        pltpu.make_async_copy(source_ref.at[row], held.at[row], sems.at[row]).wait()
        r, c = lax.div(row, 4), lax.rem(row, 4)
        picked = [
            couple_ref[k, c, g * quarter : (g + 1) * quarter, :]
            for k in range(angles)
            for g in blocks
        ]
        w_high, w_low = split(jnp.concatenate(picked, axis=0))
        high, low = split(held[row])
        both = dot(jnp.concatenate([w_high, w_low], axis=0), high)
        high, low = split(both[:count] + both[count:] + dot(w_high, low))
        for k in range(angles):
            lanes = slice(k * size, (k + 1) * size)
            for b in range(len(blocks)):
                at = (k * len(blocks) + b) * quarter
                to = pl.multiple_of((b * local + r) * channels + c * quarter, quarter)
                m_high[pl.ds(to, quarter), lanes] = high[at : at + quarter]
                m_low[pl.ds(to, quarter), lanes] = low[at : at + quarter]
        return carry

    lax.fori_loop(0, rows, step, 0)


def building_kernel(blocks, count, flip_ref, source_ref, couple_ref, *refs):
    inputs = refs[:4]
    out_ref, made_high, made_low = refs[4:7]
    held_source, source_sems, high_buf, low_buf, map_sems, m_high, m_low, held_ref, sems = refs[7:]
    for row in range(source_ref.shape[0]):
        pltpu.make_async_copy(source_ref.at[row], held_source.at[row], source_sems.at[row]).start()
    mix_source(blocks, source_ref, held_source, source_sems, couple_ref, m_high, m_low)
    size = inputs[0].shape[1]
    rows = size // PIECES
    chosen = chosen_nodes(count, size)
    made = ((high_buf, made_high), (low_buf, made_low))

    def step(t, carry):
        part = pl.ds(pl.multiple_of(t * rows, rows), rows)
        build_rows(count, part, inputs, chosen, high_buf.at[part], low_buf.at[part])
        for n, (buf, to) in enumerate(made):
            pltpu.make_async_copy(buf.at[part], to.at[part], map_sems.at[n, t]).start()
        value = interpolate(high_buf.at[part], low_buf.at[part], m_high, m_low, dot_nt)
        finish_rows(flip_ref[0], t, value, held_ref, out_ref, sems)
        return carry

    lax.fori_loop(0, PIECES, step, 0)
    finish_copies(held_ref, out_ref, sems)
    for t in range(PIECES):
        part = pl.ds(t * rows, rows)
        for n, (buf, to) in enumerate(made):
            pltpu.make_async_copy(buf.at[part], to.at[part], map_sems.at[n, t]).wait()


def first_one_building(blocks, flip, source, couple, inputs, near, devices, count):
    rows, channels, size = source.shape
    local = rows // 4
    angles = couple.shape[0]
    out = (devices, len(blocks), near, local, size // (devices * near), channels)
    wide = len(blocks) * local * channels
    vmem = pl.BlockSpec(memory_space=pltpu.VMEM)
    anywhere = pl.BlockSpec(memory_space=pl.ANY)
    made = jax.ShapeDtypeStruct((size, angles * size), BF16)
    return call(
        functools.partial(building_kernel, blocks, count),
        6 * wide * angles * size * (size + channels),
        4 * source.size + 4 * angles * size * size,
        (source, couple, *inputs),
        grid=(),
        in_specs=[anywhere] + [vmem] * 5,
        out_specs=[anywhere] * 3,
        out_shape=[jax.ShapeDtypeStruct(out, F32), made, made],
        scratch_shapes=[pltpu.VMEM(source.shape, F32), pltpu.SemaphoreType.DMA((rows,))]
        + [pltpu.VMEM(made.shape, BF16)] * 2
        + [pltpu.SemaphoreType.DMA((2, PIECES))]
        + [pltpu.VMEM((wide, angles * size), BF16)] * 2
        + [pltpu.VMEM(out, F32), pltpu.SemaphoreType.DMA((PIECES,))],
        scalars=(flip,),
    )


def first_kernel(blocks, steps, flip_ref, source_ref, couple_ref, high_ref, low_ref, out_ref, m_high, m_low):
    angles, _, channels, _ = couple_ref.shape
    quarter = channels // 4
    together, _, size = source_ref.shape
    i = pl.program_id(0)
    count = angles * len(blocks) * quarter
    local = steps * together // 4

    @pl.when(i < steps)
    def _():
        for n in range(together):
            row = i * together + n
            r, c = lax.div(row, 4), lax.rem(row, 4)
            rows = [
                couple_ref[k, c, g * quarter : (g + 1) * quarter, :]
                for k in range(angles)
                for g in blocks
            ]
            w_high, w_low = split(jnp.concatenate(rows, axis=0))
            high, low = split(source_ref[n])
            both = dot(jnp.concatenate([w_high, w_low], axis=0), high)
            high, low = split(both[:count] + both[count:] + dot(w_high, low))
            for k in range(angles):
                lanes = slice(k * size, (k + 1) * size)
                for b in range(len(blocks)):
                    at = (k * len(blocks) + b) * quarter
                    to = pl.multiple_of((b * local + r) * channels + c * quarter, quarter)
                    m_high[pl.ds(to, quarter), lanes] = high[at : at + quarter]
                    m_low[pl.ds(to, quarter), lanes] = low[at : at + quarter]

    @pl.when(i >= steps)
    def _():
        spread_out(flip_ref[0], interpolate(high_ref, low_ref, m_high, m_low, dot_nt), out_ref)


def first_one(blocks, flip, source, couple, maps, near, devices):
    rows, channels, size = source.shape
    local = rows // 4
    angles = couple.shape[0]
    together = SOURCE_ROWS
    steps = rows // together
    out = (devices, len(blocks), near, local, size // (devices * near), channels)
    wide = len(blocks) * local * channels

    def tile(i):
        return jnp.maximum(i - steps, 0)

    return call(
        functools.partial(first_kernel, blocks, steps),
        6 * wide * angles * size * (size + channels),
        4 * source.size + 4 * angles * size * size,
        (source, couple, *maps),
        grid=(steps + TILES,),
        in_specs=[
            pl.BlockSpec((together, channels, size), lambda i, f: (jnp.minimum(i, steps - 1), 0, 0)),
            pl.BlockSpec(couple.shape, lambda i, f: (0, 0, 0, 0)),
        ]
        + [pl.BlockSpec((size // TILES, angles * size), lambda i, f: (tile(i), 0))] * 2,
        out_specs=out_spec(out, tile),
        out_shape=jax.ShapeDtypeStruct(out, F32),
        scratch_shapes=[pltpu.VMEM((wide, angles * size), BF16)] * 2,
        scalars=(flip,),
    )


def chunk_specs(chunk):
    if not isinstance(chunk, list):
        return [chunk], [pl.BlockSpec(chunk.shape, lambda i, f: (0, 0, 0, 0, 0))]
    spec = pl.BlockSpec((1,) + chunk[0].shape[1:], lambda i, f: (0, 0, 0, 0, 0))
    return chunk, [spec] * len(chunk)


def later_kernel(blocks, counts, flip_ref, *refs):
    chunks = []
    for count in counts:
        chunks.append(refs[:count])
        refs = refs[count:]
    couple_ref, high_ref, low_ref, out_ref, w_high, w_low, m_high, m_low = refs[:8]
    wholes = list(refs[8:])
    angles, _, channels, _ = couple_ref.shape
    quarter = channels // 4
    size = high_ref.shape[1] // angles
    _, _, local, per, _ = chunks[0][0].shape

    @pl.when(pl.program_id(0) == 0)
    def _():
        lane = lax.broadcasted_iota(jnp.int32, (quarter, channels), 1)
        for k in range(angles):
            for b, g in enumerate(blocks):
                for c in range(4):
                    rows = couple_ref[k, c, g * quarter : (g + 1) * quarter, :]
                    at = (k * len(blocks) + b) * channels + c * quarter
                    inside = lax.div(lane, quarter) == c
                    for other in range(4):
                        shift = ((c - other) * quarter) % channels
                        moved = pltpu.roll(rows, shift, 1) if shift else rows
                        high, low = split(jnp.where(inside, moved, 0.0))
                        lanes = slice(other * channels, (other + 1) * channels)
                        w_high[at : at + quarter, lanes] = high
                        w_low[at : at + quarter, lanes] = low
        sources = []
        for chunk in chunks:
            if len(chunk) > 1:
                whole = wholes.pop(0)
                gather(flip_ref[1], [chunk], whole)
                sources += [(whole, b, True) for b in range(whole.shape[0])]
            else:
                sources += [(chunk[0], b, False) for b in range(chunk[0].shape[1])]
        rows = min(256, size)

        def step(t, carry):
            for r in range(local):
                pieces = []
                for ref, b, flat in sources:
                    if flat:
                        pieces.append(ref[b, r, pl.ds(pl.multiple_of(t * rows, rows), rows), :])
                    else:
                        piece = ref[pl.ds(t * (rows // per), rows // per), b, r]
                        pieces.append(piece.reshape(rows, channels))
                high, low = split(jnp.concatenate(pieces, axis=1))
                mixed = (
                    dot_nt(high, w_high[...]) + dot_nt(low, w_high[...]) + dot_nt(high, w_low[...])
                )
                high, low = split(mixed)
                for k in range(angles):
                    here = pl.ds(pl.multiple_of(k * size + t * rows, rows), rows)
                    for b in range(len(blocks)):
                        at = (k * len(blocks) + b) * channels
                        to = (b * local + r) * channels
                        m_high[here, to : to + channels] = high[:, at : at + channels]
                        m_low[here, to : to + channels] = low[:, at : at + channels]
            return carry

        lax.fori_loop(0, size // rows, step, 0)

    spread_out(flip_ref[0], interpolate(high_ref, low_ref, m_high, m_low, dot), out_ref)


def later_one(blocks, flip, chunks, couple, maps, near, devices):
    _, _, local, per, channels = chunks[0][0].shape if isinstance(chunks[0], list) else chunks[0].shape
    size = devices * per
    angles = couple.shape[0]
    out = (devices, len(blocks), near, local, size // (devices * near), channels)
    wide = len(blocks) * local * channels
    operands, specs, counts, wholes = [], [], [], []
    for chunk in chunks:
        some, some_specs = chunk_specs(chunk)
        operands += some
        specs += some_specs
        counts.append(len(some))
        if isinstance(chunk, list):
            wholes.append(pltpu.VMEM((chunk[0].shape[1], local, size, channels), F32))
    return call(
        functools.partial(later_kernel, blocks, counts),
        6 * wide * angles * size * (size + 4 * channels),
        16 * local * size * channels + 4 * angles * size * size,
        (*operands, couple, *maps),
        grid=(TILES,),
        in_specs=specs
        + [pl.BlockSpec(couple.shape, lambda i, f: (0, 0, 0, 0))]
        + [pl.BlockSpec((size // TILES, angles * size), lambda i, f: (i, 0))] * 2,
        out_specs=out_spec(out, lambda i: i),
        out_shape=jax.ShapeDtypeStruct(out, F32),
        scratch_shapes=[pltpu.VMEM((angles * len(blocks) * channels, 4 * channels), BF16)] * 2
        + [pltpu.VMEM((angles * size, wide), BF16)] * 2
        + wholes,
        scalars=(flip,),
    )


def two_kernel(blocks, counts, flip_ref, *refs):
    chunks = []
    for count in counts:
        chunks.append(refs[:count])
        refs = refs[count:]
    couple_ref, green_ref, high_ref, low_ref, out_ref, turned, w_high, w_low, m_high, m_low = refs[:10]
    angles, _, channels, _ = couple_ref.shape
    quarter = channels // 4
    size = high_ref.shape[1] // angles
    _, _, local, per, _ = chunks[0][0].shape

    @pl.when(pl.program_id(0) == 0)
    def _():
        for k in range(angles):
            for b, g in enumerate(blocks):
                at = k * len(blocks) + b
                rows = [couple_ref[k, g, pl.ds(c, quarter, stride=4), :] for c in range(4)]
                turned[at] = jnp.concatenate(rows, axis=0).T
                rows = [turned[at, pl.ds(c, quarter, stride=4), :] for c in range(4)]
                high, low = split(jnp.concatenate(rows, axis=0))
                w_high[b, :, k * channels : (k + 1) * channels] = high
                w_low[b, :, k * channels : (k + 1) * channels] = low
        if counts[0] > 1:
            gather(flip_ref[1], chunks, refs[10])
        rows = min(256, size)

        def step(t, carry):
            for b in range(len(blocks)):
                for p in range(local):
                    if counts[0] > 1:
                        here = pl.ds(pl.multiple_of(t * rows, rows), rows)
                        value = refs[10][b, p, here, :]
                    else:
                        here = pl.ds(t * (rows // per), rows // per)
                        value = chunks[0][0][here, b, p]
                        for other in chunks[1:]:
                            value = value + other[0][here, b, p]
                        value = value.reshape(rows, channels)
                    high, low = split(value)
                    mixed = dot(high, w_high[b]) + dot(low, w_high[b]) + dot(high, w_low[b])
                    high, low = split(mixed)
                    to = (b * local + p) * channels
                    for k in range(angles):
                        here = pl.ds(pl.multiple_of(k * size + t * rows, rows), rows)
                        lanes = slice(k * channels, (k + 1) * channels)
                        m_high[here, to : to + channels] = high[:, lanes]
                        m_low[here, to : to + channels] = low[:, lanes]
            return carry

        lax.fori_loop(0, size // rows, step, 0)

    spread_out(flip_ref[0], interpolate(high_ref, low_ref, m_high, m_low, dot), out_ref, green_ref)


def component_two(blocks, flip, chunks, couple, green, maps, near, devices):
    _, _, local, per, channels = chunks[0][0].shape if isinstance(chunks[0], list) else chunks[0].shape
    size = devices * per
    angles = couple.shape[0]
    out = (devices, len(blocks), near, local, per // near, channels)
    wide = len(blocks) * local * channels
    operands, specs, counts = [], [], []
    for chunk in chunks:
        some, some_specs = chunk_specs(chunk)
        operands += some
        specs += some_specs
        counts.append(len(some))
    wholes = [pltpu.VMEM((len(blocks), local, size, channels), F32)] if counts[0] > 1 else []
    return call(
        functools.partial(two_kernel, blocks, counts),
        6 * wide * angles * size * (size + channels),
        4 * len(chunks) * wide * size + 4 * angles * size * size,
        (*operands, couple, green, *maps),
        grid=(TILES,),
        in_specs=specs
        + [
            pl.BlockSpec(couple.shape, lambda i, f: (0, 0, 0, 0)),
            pl.BlockSpec((size // TILES, green.shape[1]), lambda i, f: (i, 0)),
        ]
        + [pl.BlockSpec((size // TILES, angles * size), lambda i, f: (i, 0))] * 2,
        out_specs=out_spec(out, lambda i: i),
        out_shape=jax.ShapeDtypeStruct(out, F32),
        scratch_shapes=[pltpu.VMEM((angles * len(blocks), channels, channels), F32)]
        + [pltpu.VMEM((len(blocks), channels, angles * channels), BF16)] * 2
        + [pltpu.VMEM((angles * size, wide), BF16)] * 2
        + wholes,
        scalars=(flip,),
    )


def amplitude_kernel(quarter, count, flip_ref, source_ref, *refs):
    backs, out_ref = refs[:count], refs[-1]
    if count > 1:
        out_ref, whole_ref = refs[-2:]
        per = backs[0].shape[1]
        for s in range(count):
            rows = pl.ds(pl.multiple_of((flip_ref[1] ^ s) * per, per), per)
            whole_ref[rows, :] = backs[s][0]
        turned = whole_ref[...].T
    else:
        back = backs[0][...]
        turned = back.reshape(-1, back.shape[-1]).T
    for c in range(4):
        out_ref[c] = source_ref[c] + turned[c * quarter : (c + 1) * quarter]


def amplitude_chunk(blocks, flip, source, chunk, so_far):
    _, channels, size = source.shape
    quarter = channels // 4
    backs = chunk if isinstance(chunk, list) else [chunk]
    _, _, local, per, _ = backs[0].shape
    spec = pl.BlockSpec((4, quarter, size), lambda b, r, f: (r, blocks[0] + b, 0))
    depth = 1 if len(backs) > 1 else backs[0].shape[0]
    back_spec = pl.BlockSpec((depth, None, None, per, channels), lambda b, r, f: (0, b, r, 0, 0))
    in_specs = [spec] + [back_spec] * len(backs)
    args = [source, *backs]
    aliases = {}
    if so_far is not None:
        in_specs.append(pl.BlockSpec(memory_space=pl.ANY))
        args.append(so_far)
        aliases = {len(args): 0}
    moved = len(blocks) * local * channels * size
    return call(
        functools.partial(amplitude_kernel, quarter, len(backs)),
        moved,
        12 * moved,
        args,
        grid=(len(blocks), local),
        in_specs=in_specs,
        out_specs=spec,
        out_shape=jax.ShapeDtypeStruct(source.shape, F32),
        scratch_shapes=[pltpu.VMEM((size, channels), F32)] if len(backs) > 1 else [],
        scalars=(flip,),
        aliases=aliases,
    )


def output_kernel(quarter, flip_ref, sent_ref, *refs):
    out_ref, whole_ref, turned_ref = refs[-3:]
    devices, near, count, channels = sent_ref.shape
    per_tile = LANES // (devices * near)
    for d in range(devices):
        whole_ref[d] = sent_ref[d ^ flip_ref[0]]
    for tile in range(count // per_tile):
        rows = [
            whole_ref[:, :, tile * per_tile + i, :].reshape(devices * near, channels)
            for i in range(per_tile)
        ]
        turned = jnp.concatenate(rows, axis=0).T
        for c in range(4):
            turned_ref[tile, pl.ds(c, quarter, stride=4), :] = turned[
                c * quarter : (c + 1) * quarter
            ]
        out_ref[:, tile * LANES : (tile + 1) * LANES] = turned_ref[tile]


def component_chunk(blocks, flip, sent, so_far):
    devices, _, near, local, count, channels = sent.shape
    size = devices * near * count
    in_specs = [
        pl.BlockSpec(
            (devices, None, near, None, count, channels), lambda b, p, f: (0, b, 0, p, 0, 0)
        )
    ]
    args = [sent]
    aliases = {}
    if so_far is not None:
        in_specs.append(pl.BlockSpec(memory_space=pl.ANY))
        args.append(so_far)
        aliases = {2: 0}
    return call(
        functools.partial(output_kernel, channels // 4),
        0,
        8 * sent.size,
        args,
        grid=(len(blocks), local),
        in_specs=in_specs,
        out_specs=pl.BlockSpec(
            (None, channels, size), lambda b, p, f: (4 * p + blocks[0] + b, 0, 0)
        ),
        out_shape=jax.ShapeDtypeStruct((4 * local, channels, size), F32),
        scratch_shapes=[
            pltpu.VMEM((devices, near, count, channels), F32),
            pltpu.VMEM((size // LANES, channels, LANES), F32),
        ],
        scalars=(flip,),
        aliases=aliases,
    )


def exchange(values, pairs):
    devices, blocks, near, local, count, channels = values.shape
    sent = values.reshape(devices, blocks, near, local * count, channels)
    if not pairs:
        return lax.all_to_all(sent, "mom", split_axis=0, concat_axis=0, tiled=True)
    arrived = [sent]
    for s in range(1, devices):
        route = [(d, d ^ s) for d in range(devices)]
        arrived.append(lax.ppermute(sent[s : s + 1], "mom", route))
    return arrived


CHUNKS = (((0, 1), True), ((2, 3), False))


def shards(
    devices,
    source,
    green,
    couple_one,
    couple_two,
    p_bracket,
    q_bracket,
    p_weight,
    q_weight,
    qr_bracket,
    r_bracket,
    qr_weight,
    r_weight,
):
    rows_one, _, size_one = source.shape
    rows_two, size_two = green.shape
    near_r, near_p = rows_one // 4, rows_two // 4
    r_size, p_size = devices * near_r, devices * near_p
    q_size = size_one // p_size
    me = lax.axis_index("mom").astype(jnp.int32)
    flips = [jnp.stack([me if pairs else jnp.int32(0), me]) for _, pairs in CHUNKS]

    first_inputs = (p_bracket, q_bracket, p_weight, q_weight)

    def by_r(array):
        lead = array.shape[:-1]
        return array.reshape(lead + (q_size, r_size)).swapaxes(-1, -2).reshape(lead + (-1,))

    second_maps = spline_maps(
        by_r(r_bracket), by_r(qr_bracket), by_r(r_weight), by_r(qr_weight), q_size
    )
    green = green.reshape(near_p, 4, q_size, r_size).transpose(3, 2, 1, 0)
    green = green.reshape(size_two, 4 * near_p)
    arrived = []
    for step in range(ITERS):
        ones = []
        for flip, (blocks, pairs) in zip(flips, CHUNKS):
            if step == 0:
                if not ones:
                    one, *first_maps = first_one_building(
                        blocks, flip, source, couple_one, first_inputs, near_p, devices, q_size
                    )
                else:
                    one = first_one(blocks, flip, source, couple_one, first_maps, near_p, devices)
            else:
                one = later_one(blocks, flip, backs, couple_one, first_maps, near_p, devices)
            ones.append(exchange(one, pairs))
        arrived.append(ones)
        twos = []
        backs = []
        for n, (flip, (blocks, pairs)) in enumerate(zip(flips, CHUNKS)):
            chunks = [arrived[0][n]] + ([arrived[step][n]] if step else [])
            lanes = slice(blocks[0] * near_p, (blocks[-1] + 1) * near_p)
            scale = green[:, lanes]
            two = component_two(
                blocks, flip, chunks, couple_two, scale, second_maps, near_r, devices
            )
            twos.append(two)
            backs.append(exchange(two, pairs))
    component = amplitude = None
    for flip, (blocks, _), two, back in zip(flips, CHUNKS, twos, backs):
        component = component_chunk(blocks, flip, two, component)
        amplitude = amplitude_chunk(blocks, flip, source, back, amplitude)
    return amplitude, component


def whole_map(first, second, first_weight, second_weight, first_count, second_count):
    first_rows = jnp.zeros((first.shape[0], first_count), F32)
    second_rows = jnp.zeros((second.shape[0], second_count), F32)
    first_grid = jnp.arange(first_count, dtype=jnp.int32)[None, :] - first[:, None]
    second_grid = jnp.arange(second_count, dtype=jnp.int32)[None, :] - second[:, None]
    for offset in range(4):
        first_rows += jnp.where(first_grid == offset, first_weight[offset][:, None], 0.0)
        second_rows += jnp.where(second_grid == offset, second_weight[offset][:, None], 0.0)
    return (first_rows[:, :, None] * second_rows[:, None, :]).reshape(first.shape[0], -1)


def row_mats(couple, rows, start):
    select = jax.nn.one_hot((start + jnp.arange(rows, dtype=jnp.int32)) % 4, 4, dtype=F32)
    return jnp.einsum("rc,kcmn->krmn", select, couple, precision=lax.Precision.HIGHEST)


def mix_rows(mats, values):
    return jnp.einsum("rmn,rnx->rmx", mats, values, precision=lax.Precision.HIGHEST)


def interpolate_rows(values, matrix):
    return jnp.einsum("rcx,yx->rcy", values, matrix, precision=lax.Precision.HIGHEST)


def shards_by_row(
    devices,
    source,
    green,
    couple_one,
    couple_two,
    p_bracket,
    q_bracket,
    p_weight,
    q_weight,
    qr_bracket,
    r_bracket,
    qr_weight,
    r_weight,
):
    rows_one, channels, size_one = source.shape
    rows_two, size_two = green.shape
    angles = couple_one.shape[0]
    quarter = channels // 4
    r_size, p_size = devices * rows_one // 4, devices * rows_two // 4
    q_size = size_one // p_size
    here = lax.axis_index("mom")
    first = [
        whole_map(p_bracket[k], q_bracket[k], p_weight[k], q_weight[k], p_size, q_size)
        for k in range(angles)
    ]
    second = [
        whole_map(qr_bracket[k], r_bracket[k], qr_weight[k], r_weight[k], q_size, r_size)
        for k in range(angles)
    ]
    mats_one = row_mats(couple_one, rows_one, here * rows_one)
    mats_two = row_mats(couple_two, rows_two, here * rows_two)
    state = source
    for _ in range(ITERS):
        one = sum(interpolate_rows(mix_rows(mats_one[k], state), first[k]) for k in range(angles))
        sent = one.reshape(rows_one, 4, quarter, p_size, q_size).transpose(3, 1, 0, 2, 4)
        sent = sent.reshape(4 * p_size, rows_one, quarter * q_size)
        sent = lax.all_to_all(sent, "mom", split_axis=0, concat_axis=1, tiled=True)
        sent = sent.reshape(rows_two, r_size, 4, quarter, q_size).transpose(0, 3, 2, 4, 1)
        sent = sent.reshape(rows_two, channels, size_two)
        total = sum(mix_rows(mats_two[k], interpolate_rows(sent, second[k])) for k in range(angles))
        component = green[:, None, :] * total
        back = component.reshape(rows_two, quarter, 4, q_size, r_size).transpose(4, 2, 0, 1, 3)
        back = back.reshape(4 * r_size, rows_two, quarter * q_size)
        back = lax.all_to_all(back, "mom", split_axis=0, concat_axis=1, tiled=True)
        back = back.reshape(rows_one, p_size, 4, quarter, q_size).transpose(0, 2, 3, 1, 4)
        state = source + back.reshape(source.shape)
    return state, component


def solution(mesh):
    spread = ("energy", "mom")
    placed = (P(spread, None, None), P(spread, None)) + (P(),) * 10
    devices = mesh.shape["mom"]

    def body(source, green, *rest):
        whole_rows = source.shape[0] % 4 == 0 and green.shape[0] % 4 == 0
        chosen = shards if whole_rows and source.shape[1] == LANES else shards_by_row
        return chosen(devices, source, green, *rest)

    return jax.shard_map(
        body,
        mesh=mesh,
        in_specs=placed,
        out_specs=(P(spread, None, None), P(spread, None, None)),
        check_vma=False,
    )
```

```python
import functools


import jax
import jax.numpy as jnp
from jax import lax
from jax.experimental import pallas as pl
from jax.experimental.pallas import tpu as pltpu
from jax.sharding import PartitionSpec as P

ITERS = 2
LANES = 128
F32 = jnp.float32
BF16 = jnp.bfloat16
VMEM_LIMIT = 60 << 20
PIECES = 4
TILES = 4
SOURCE_ROWS = 4


def split(value):
    high = value.astype(BF16)
    return high, (value - high.astype(F32)).astype(BF16)


def dot(a, b):
    return jnp.dot(a, b, preferred_element_type=F32)


def dot_nt(a, b):
    return lax.dot_general(a, b, (((1,), (1,)), ((), ())), preferred_element_type=F32)


def call(kernel, flops, moved, args, grid, in_specs, out_specs, out_shape, scratch_shapes=(), scalars=(), aliases=None, limit=VMEM_LIMIT):
    return pl.pallas_call(
        kernel,
        grid_spec=pltpu.PrefetchScalarGridSpec(
            num_scalar_prefetch=len(scalars),
            grid=grid,
            in_specs=in_specs,
            out_specs=out_specs,
            scratch_shapes=scratch_shapes,
        ),
        out_shape=out_shape,
        input_output_aliases=aliases or {},
        compiler_params=pltpu.CompilerParams(vmem_limit_bytes=limit),
        cost_estimate=pl.CostEstimate(flops=flops, bytes_accessed=moved, transcendentals=0),
    )(*scalars, *args)


def map_factors(count, k, rows, first_ref, second_ref, first_weight_ref, second_weight_ref):
    size = rows.size
    table = jnp.concatenate(
        [
            first_ref[k : k + 1, rows].astype(F32),
            second_ref[k : k + 1, rows].astype(F32),
            first_weight_ref[k, :, rows],
            second_weight_ref[k, :, rows],
            jnp.zeros((6, size), F32),
        ],
        axis=0,
    ).T
    lane = lax.broadcasted_iota(jnp.int32, (1, LANES), 1)

    def factor(index, base):
        grid = index.astype(F32) - table[:, base : base + 1]
        total = jnp.zeros((size, LANES), F32)
        for offset in range(4):
            column = 2 + 4 * base + offset
            total = jnp.where(grid == offset, table[:, column : column + 1], total)
        return total

    high, low = split(factor(lane, 0))
    return high, low, factor(lane - lax.div(lane, count) * count, 1)


def chosen_nodes(count, columns):
    node = lax.broadcasted_iota(jnp.int32, (LANES, columns), 0)
    column = lax.broadcasted_iota(jnp.int32, (LANES, columns), 1)
    inside = jnp.logical_and(column >= node * count, column < (node + 1) * count)
    return jnp.where(inside, 1.0, 0.0).astype(BF16)


def build_rows(count, rows, inputs, chosen, high_ref, low_ref):
    angles, size = inputs[0].shape
    for k in range(angles):
        first_high, first_low, second = map_factors(count, k, rows, *inputs)
        for tile in range(size // LANES):
            lanes = slice(tile * LANES, (tile + 1) * LANES)
            spread = dot(first_high, chosen[:, lanes]) + dot(first_low, chosen[:, lanes])
            high, low = split(spread * second)
            lanes = slice(k * size + tile * LANES, k * size + (tile + 1) * LANES)
            high_ref[:, lanes] = high
            low_ref[:, lanes] = low


def map_kernel(count, *refs):
    inputs, (high_ref, low_ref) = refs[:4], refs[4:]
    size = high_ref.shape[0]
    start = pl.multiple_of(pl.program_id(0) * size, size)
    chosen = chosen_nodes(count, inputs[0].shape[1])
    build_rows(count, pl.ds(start, size), inputs, chosen, high_ref, low_ref)


def spline_maps(first, second, first_weight, second_weight, count):
    angles, size = first.shape
    tile = size // PIECES
    out = jax.ShapeDtypeStruct((size, angles * size), BF16)
    spec = pl.BlockSpec((tile, angles * size), lambda i: (i, 0))
    return call(
        functools.partial(map_kernel, count),
        10 * angles * size * size,
        4 * angles * size * size,
        (first, second, first_weight, second_weight),
        grid=(PIECES,),
        in_specs=[pl.BlockSpec(memory_space=pltpu.VMEM)] * 4,
        out_specs=[spec, spec],
        out_shape=[out, out],
    )


def interpolate(high_ref, low_ref, mixed_high, mixed_low, product):
    high = high_ref[...]
    return (
        product(high, mixed_high[...])
        + product(high, mixed_low[...])
        + product(low_ref[...], mixed_high[...])
    )


def spread_out(flip, value, out_ref, scale_ref=None):
    parts, blocks, near, local, count, channels = out_ref.shape
    rows = near * count
    for b in range(blocks):
        for n in range(local):
            at = b * local + n
            block = value[:, at * channels : (at + 1) * channels]
            if scale_ref is not None:
                block = block * scale_ref[:, at : at + 1]
            for j in range(parts):
                piece = block[j * rows : (j + 1) * rows].reshape(near, count, channels)
                out_ref[j ^ (flip & (parts - 1)), b, :, n, :, :] = piece


def out_spec(shape, tile):
    parts = shape[0] // TILES
    return pl.BlockSpec(
        (parts,) + shape[1:],
        lambda i, flip: (tile(i) ^ lax.div(flip[0], parts), 0, 0, 0, 0, 0),
    )


def gather(me, sets, whole_ref):
    blocks, local, _, _ = whole_ref.shape
    per = sets[0][0].shape[3]
    for s in range(len(sets[0])):
        rows = pl.ds(pl.multiple_of((me ^ s) * per, per), per)
        for b in range(blocks):
            for n in range(local):
                value = sets[0][s][0, b, n]
                for other in sets[1:]:
                    value = value + other[s][0, b, n]
                whole_ref[b, n, rows, :] = value


def finish_rows(flip, t, value, held_ref, out_ref, sems, scale_ref=None):
    devices, blocks, near, local, count, channels = held_ref.shape
    parts = devices // PIECES
    rows = near * count
    group = t ^ lax.div(flip, parts)
    for b in range(blocks):
        for n in range(local):
            at = b * local + n
            block = value[:, at * channels : (at + 1) * channels]
            if scale_ref is not None:
                start = pl.multiple_of(t * parts * rows, parts * rows)
                block = block * scale_ref[pl.ds(start, parts * rows), at : at + 1]
            for j in range(parts):
                piece = block[j * rows : (j + 1) * rows].reshape(near, count, channels)
                held_ref[group * parts + (j ^ (flip & (parts - 1))), b, :, n, :, :] = piece
    part = pl.ds(group * parts, parts)
    pltpu.make_async_copy(held_ref.at[part], out_ref.at[part], sems.at[group]).start()


def finish_copies(held_ref, out_ref, sems):
    parts = held_ref.shape[0] // PIECES
    for t in range(PIECES):
        part = pl.ds(t * parts, parts)
        pltpu.make_async_copy(held_ref.at[part], out_ref.at[part], sems.at[t]).wait()


def mix_source(blocks, source_ref, held, sems, couple_ref, m_high, m_low):
    angles, _, channels, _ = couple_ref.shape
    rows, _, size = held.shape
    quarter = channels // 4
    count = angles * len(blocks) * quarter
    local = rows // 4

    def step(row, carry):
        pltpu.make_async_copy(source_ref.at[row], held.at[row], sems.at[row]).wait()
        r, c = lax.div(row, 4), lax.rem(row, 4)
        picked = [
            couple_ref[k, c, g * quarter : (g + 1) * quarter, :]
            for k in range(angles)
            for g in blocks
        ]
        w_high, w_low = split(jnp.concatenate(picked, axis=0))
        high, low = split(held[row])
        both = dot(jnp.concatenate([w_high, w_low], axis=0), high)
        high, low = split(both[:count] + both[count:] + dot(w_high, low))
        for k in range(angles):
            lanes = slice(k * size, (k + 1) * size)
            for b in range(len(blocks)):
                at = (k * len(blocks) + b) * quarter
                to = pl.multiple_of((b * local + r) * channels + c * quarter, quarter)
                m_high[pl.ds(to, quarter), lanes] = high[at : at + quarter]
                m_low[pl.ds(to, quarter), lanes] = low[at : at + quarter]
        return carry

    lax.fori_loop(0, rows, step, 0)


def building_kernel(blocks, count, flip_ref, source_ref, couple_ref, *refs):
    inputs = refs[:4]
    out_ref, made_high, made_low = refs[4:7]
    held_source, source_sems, high_buf, low_buf, map_sems, m_high, m_low, held_ref, sems = refs[7:]
    for row in range(source_ref.shape[0]):
        pltpu.make_async_copy(source_ref.at[row], held_source.at[row], source_sems.at[row]).start()
    mix_source(blocks, source_ref, held_source, source_sems, couple_ref, m_high, m_low)
    size = inputs[0].shape[1]
    rows = size // PIECES
    chosen = chosen_nodes(count, size)
    made = ((high_buf, made_high), (low_buf, made_low))

    def step(t, carry):
        part = pl.ds(pl.multiple_of(t * rows, rows), rows)
        build_rows(count, part, inputs, chosen, high_buf.at[part], low_buf.at[part])
        for n, (buf, to) in enumerate(made):
            pltpu.make_async_copy(buf.at[part], to.at[part], map_sems.at[n, t]).start()
        value = interpolate(high_buf.at[part], low_buf.at[part], m_high, m_low, dot_nt)
        finish_rows(flip_ref[0], t, value, held_ref, out_ref, sems)
        return carry

    lax.fori_loop(0, PIECES, step, 0)
    finish_copies(held_ref, out_ref, sems)
    for t in range(PIECES):
        part = pl.ds(t * rows, rows)
        for n, (buf, to) in enumerate(made):
            pltpu.make_async_copy(buf.at[part], to.at[part], map_sems.at[n, t]).wait()


def first_one_building(blocks, flip, source, couple, inputs, near, devices, count):
    rows, channels, size = source.shape
    local = rows // 4
    angles = couple.shape[0]
    out = (devices, len(blocks), near, local, size // (devices * near), channels)
    wide = len(blocks) * local * channels
    vmem = pl.BlockSpec(memory_space=pltpu.VMEM)
    anywhere = pl.BlockSpec(memory_space=pl.ANY)
    made = jax.ShapeDtypeStruct((size, angles * size), BF16)
    return call(
        functools.partial(building_kernel, blocks, count),
        6 * wide * angles * size * (size + channels),
        4 * source.size + 4 * angles * size * size,
        (source, couple, *inputs),
        grid=(),
        in_specs=[anywhere] + [vmem] * 5,
        out_specs=[anywhere] * 3,
        out_shape=[jax.ShapeDtypeStruct(out, F32), made, made],
        scratch_shapes=[pltpu.VMEM(source.shape, F32), pltpu.SemaphoreType.DMA((rows,))]
        + [pltpu.VMEM(made.shape, BF16)] * 2
        + [pltpu.SemaphoreType.DMA((2, PIECES))]
        + [pltpu.VMEM((wide, angles * size), BF16)] * 2
        + [pltpu.VMEM(out, F32), pltpu.SemaphoreType.DMA((PIECES,))],
        scalars=(flip,),
    )


def first_kernel(blocks, steps, flip_ref, source_ref, couple_ref, high_ref, low_ref, out_ref, m_high, m_low):
    angles, _, channels, _ = couple_ref.shape
    quarter = channels // 4
    together, _, size = source_ref.shape
    i = pl.program_id(0)
    count = angles * len(blocks) * quarter
    local = steps * together // 4

    @pl.when(i < steps)
    def _():
        for n in range(together):
            row = i * together + n
            r, c = lax.div(row, 4), lax.rem(row, 4)
            rows = [
                couple_ref[k, c, g * quarter : (g + 1) * quarter, :]
                for k in range(angles)
                for g in blocks
            ]
            w_high, w_low = split(jnp.concatenate(rows, axis=0))
            high, low = split(source_ref[n])
            both = dot(jnp.concatenate([w_high, w_low], axis=0), high)
            high, low = split(both[:count] + both[count:] + dot(w_high, low))
            for k in range(angles):
                lanes = slice(k * size, (k + 1) * size)
                for b in range(len(blocks)):
                    at = (k * len(blocks) + b) * quarter
                    to = pl.multiple_of((b * local + r) * channels + c * quarter, quarter)
                    m_high[pl.ds(to, quarter), lanes] = high[at : at + quarter]
                    m_low[pl.ds(to, quarter), lanes] = low[at : at + quarter]

    @pl.when(i >= steps)
    def _():
        spread_out(flip_ref[0], interpolate(high_ref, low_ref, m_high, m_low, dot_nt), out_ref)


def first_one(blocks, flip, source, couple, maps, near, devices):
    rows, channels, size = source.shape
    local = rows // 4
    angles = couple.shape[0]
    together = SOURCE_ROWS
    steps = rows // together
    out = (devices, len(blocks), near, local, size // (devices * near), channels)
    wide = len(blocks) * local * channels

    def tile(i):
        return jnp.maximum(i - steps, 0)

    return call(
        functools.partial(first_kernel, blocks, steps),
        6 * wide * angles * size * (size + channels),
        4 * source.size + 4 * angles * size * size,
        (source, couple, *maps),
        grid=(steps + TILES,),
        in_specs=[
            pl.BlockSpec((together, channels, size), lambda i, f: (jnp.minimum(i, steps - 1), 0, 0)),
            pl.BlockSpec(couple.shape, lambda i, f: (0, 0, 0, 0)),
        ]
        + [pl.BlockSpec((size // TILES, angles * size), lambda i, f: (tile(i), 0))] * 2,
        out_specs=out_spec(out, tile),
        out_shape=jax.ShapeDtypeStruct(out, F32),
        scratch_shapes=[pltpu.VMEM((wide, angles * size), BF16)] * 2,
        scalars=(flip,),
    )


def chunk_specs(chunk):
    if not isinstance(chunk, list):
        return [chunk], [pl.BlockSpec(chunk.shape, lambda i, f: (0, 0, 0, 0, 0))]
    spec = pl.BlockSpec((1,) + chunk[0].shape[1:], lambda i, f: (0, 0, 0, 0, 0))
    return chunk, [spec] * len(chunk)


def later_kernel(blocks, counts, flip_ref, *refs):
    chunks = []
    for count in counts:
        chunks.append(refs[:count])
        refs = refs[count:]
    couple_ref, high_ref, low_ref, out_ref, w_high, w_low, m_high, m_low = refs[:8]
    wholes = list(refs[8:])
    angles, _, channels, _ = couple_ref.shape
    quarter = channels // 4
    size = high_ref.shape[1] // angles
    _, _, local, per, _ = chunks[0][0].shape

    @pl.when(pl.program_id(0) == 0)
    def _():
        lane = lax.broadcasted_iota(jnp.int32, (quarter, channels), 1)
        for k in range(angles):
            for b, g in enumerate(blocks):
                for c in range(4):
                    rows = couple_ref[k, c, g * quarter : (g + 1) * quarter, :]
                    at = (k * len(blocks) + b) * channels + c * quarter
                    inside = lax.div(lane, quarter) == c
                    for other in range(4):
                        shift = ((c - other) * quarter) % channels
                        moved = pltpu.roll(rows, shift, 1) if shift else rows
                        high, low = split(jnp.where(inside, moved, 0.0))
                        lanes = slice(other * channels, (other + 1) * channels)
                        w_high[at : at + quarter, lanes] = high
                        w_low[at : at + quarter, lanes] = low
        sources = []
        for chunk in chunks:
            if len(chunk) > 1:
                whole = wholes.pop(0)
                gather(flip_ref[1], [chunk], whole)
                sources += [(whole, b, True) for b in range(whole.shape[0])]
            else:
                sources += [(chunk[0], b, False) for b in range(chunk[0].shape[1])]
        rows = min(256, size)

        def step(t, carry):
            for r in range(local):
                pieces = []
                for ref, b, flat in sources:
                    if flat:
                        pieces.append(ref[b, r, pl.ds(pl.multiple_of(t * rows, rows), rows), :])
                    else:
                        piece = ref[pl.ds(t * (rows // per), rows // per), b, r]
                        pieces.append(piece.reshape(rows, channels))
                high, low = split(jnp.concatenate(pieces, axis=1))
                mixed = (
                    dot_nt(high, w_high[...]) + dot_nt(low, w_high[...]) + dot_nt(high, w_low[...])
                )
                high, low = split(mixed)
                for k in range(angles):
                    here = pl.ds(pl.multiple_of(k * size + t * rows, rows), rows)
                    for b in range(len(blocks)):
                        at = (k * len(blocks) + b) * channels
                        to = (b * local + r) * channels
                        m_high[here, to : to + channels] = high[:, at : at + channels]
                        m_low[here, to : to + channels] = low[:, at : at + channels]
            return carry

        lax.fori_loop(0, size // rows, step, 0)

    spread_out(flip_ref[0], interpolate(high_ref, low_ref, m_high, m_low, dot), out_ref)


def later_one(blocks, flip, chunks, couple, maps, near, devices):
    _, _, local, per, channels = chunks[0][0].shape if isinstance(chunks[0], list) else chunks[0].shape
    size = devices * per
    angles = couple.shape[0]
    out = (devices, len(blocks), near, local, size // (devices * near), channels)
    wide = len(blocks) * local * channels
    operands, specs, counts, wholes = [], [], [], []
    for chunk in chunks:
        some, some_specs = chunk_specs(chunk)
        operands += some
        specs += some_specs
        counts.append(len(some))
        if isinstance(chunk, list):
            wholes.append(pltpu.VMEM((chunk[0].shape[1], local, size, channels), F32))
    return call(
        functools.partial(later_kernel, blocks, counts),
        6 * wide * angles * size * (size + 4 * channels),
        16 * local * size * channels + 4 * angles * size * size,
        (*operands, couple, *maps),
        grid=(TILES,),
        in_specs=specs
        + [pl.BlockSpec(couple.shape, lambda i, f: (0, 0, 0, 0))]
        + [pl.BlockSpec((size // TILES, angles * size), lambda i, f: (i, 0))] * 2,
        out_specs=out_spec(out, lambda i: i),
        out_shape=jax.ShapeDtypeStruct(out, F32),
        scratch_shapes=[pltpu.VMEM((angles * len(blocks) * channels, 4 * channels), BF16)] * 2
        + [pltpu.VMEM((angles * size, wide), BF16)] * 2
        + wholes,
        scalars=(flip,),
        limit=44 << 20,
    )


def two_kernel(blocks, counts, flip_ref, *refs):
    chunks = []
    for count in counts:
        chunks.append(refs[:count])
        refs = refs[count:]
    couple_ref, green_ref, high_ref, low_ref, out_ref, turned, w_high, w_low, m_high, m_low = refs[:10]
    angles, _, channels, _ = couple_ref.shape
    quarter = channels // 4
    size = high_ref.shape[1] // angles
    _, _, local, per, _ = chunks[0][0].shape

    @pl.when(pl.program_id(0) == 0)
    def _():
        for k in range(angles):
            for b, g in enumerate(blocks):
                at = k * len(blocks) + b
                rows = [couple_ref[k, g, pl.ds(c, quarter, stride=4), :] for c in range(4)]
                turned[at] = jnp.concatenate(rows, axis=0).T
                rows = [turned[at, pl.ds(c, quarter, stride=4), :] for c in range(4)]
                high, low = split(jnp.concatenate(rows, axis=0))
                w_high[b, :, k * channels : (k + 1) * channels] = high
                w_low[b, :, k * channels : (k + 1) * channels] = low
        if counts[0] > 1:
            gather(flip_ref[1], chunks, refs[10])
        rows = min(256, size)

        def step(t, carry):
            for b in range(len(blocks)):
                for p in range(local):
                    if counts[0] > 1:
                        here = pl.ds(pl.multiple_of(t * rows, rows), rows)
                        value = refs[10][b, p, here, :]
                    else:
                        here = pl.ds(t * (rows // per), rows // per)
                        value = chunks[0][0][here, b, p]
                        for other in chunks[1:]:
                            value = value + other[0][here, b, p]
                        value = value.reshape(rows, channels)
                    high, low = split(value)
                    mixed = dot(high, w_high[b]) + dot(low, w_high[b]) + dot(high, w_low[b])
                    high, low = split(mixed)
                    to = (b * local + p) * channels
                    for k in range(angles):
                        here = pl.ds(pl.multiple_of(k * size + t * rows, rows), rows)
                        lanes = slice(k * channels, (k + 1) * channels)
                        m_high[here, to : to + channels] = high[:, lanes]
                        m_low[here, to : to + channels] = low[:, lanes]
            return carry

        lax.fori_loop(0, size // rows, step, 0)

    spread_out(flip_ref[0], interpolate(high_ref, low_ref, m_high, m_low, dot), out_ref, green_ref)


def component_two(blocks, flip, chunks, couple, green, maps, near, devices):
    _, _, local, per, channels = chunks[0][0].shape if isinstance(chunks[0], list) else chunks[0].shape
    size = devices * per
    angles = couple.shape[0]
    out = (devices, len(blocks), near, local, per // near, channels)
    wide = len(blocks) * local * channels
    operands, specs, counts = [], [], []
    for chunk in chunks:
        some, some_specs = chunk_specs(chunk)
        operands += some
        specs += some_specs
        counts.append(len(some))
    wholes = [pltpu.VMEM((len(blocks), local, size, channels), F32)] if counts[0] > 1 else []
    return call(
        functools.partial(two_kernel, blocks, counts),
        6 * wide * angles * size * (size + channels),
        4 * len(chunks) * wide * size + 4 * angles * size * size,
        (*operands, couple, green, *maps),
        grid=(TILES,),
        in_specs=specs
        + [
            pl.BlockSpec(couple.shape, lambda i, f: (0, 0, 0, 0)),
            pl.BlockSpec((size // TILES, green.shape[1]), lambda i, f: (i, 0)),
        ]
        + [pl.BlockSpec((size // TILES, angles * size), lambda i, f: (i, 0))] * 2,
        out_specs=out_spec(out, lambda i: i),
        out_shape=jax.ShapeDtypeStruct(out, F32),
        scratch_shapes=[pltpu.VMEM((angles * len(blocks), channels, channels), F32)]
        + [pltpu.VMEM((len(blocks), channels, angles * channels), BF16)] * 2
        + [pltpu.VMEM((angles * size, wide), BF16)] * 2
        + wholes,
        scalars=(flip,),
    )


def amplitude_kernel(quarter, count, flip_ref, source_ref, *refs):
    backs, out_ref = refs[:count], refs[-1]
    if count > 1:
        out_ref, whole_ref = refs[-2:]
        per = backs[0].shape[1]
        for s in range(count):
            rows = pl.ds(pl.multiple_of((flip_ref[1] ^ s) * per, per), per)
            whole_ref[rows, :] = backs[s][0]
        turned = whole_ref[...].T
    else:
        back = backs[0][...]
        turned = back.reshape(-1, back.shape[-1]).T
    for c in range(4):
        out_ref[c] = source_ref[c] + turned[c * quarter : (c + 1) * quarter]


def amplitude_chunk(blocks, flip, source, chunk, so_far):
    _, channels, size = source.shape
    quarter = channels // 4
    backs = chunk if isinstance(chunk, list) else [chunk]
    _, _, local, per, _ = backs[0].shape
    spec = pl.BlockSpec((4, quarter, size), lambda b, r, f: (r, blocks[0] + b, 0))
    depth = 1 if len(backs) > 1 else backs[0].shape[0]
    back_spec = pl.BlockSpec((depth, None, None, per, channels), lambda b, r, f: (0, b, r, 0, 0))
    in_specs = [spec] + [back_spec] * len(backs)
    args = [source, *backs]
    aliases = {}
    if so_far is not None:
        in_specs.append(pl.BlockSpec(memory_space=pl.ANY))
        args.append(so_far)
        aliases = {len(args): 0}
    moved = len(blocks) * local * channels * size
    return call(
        functools.partial(amplitude_kernel, quarter, len(backs)),
        moved,
        12 * moved,
        args,
        grid=(len(blocks), local),
        in_specs=in_specs,
        out_specs=spec,
        out_shape=jax.ShapeDtypeStruct(source.shape, F32),
        scratch_shapes=[pltpu.VMEM((size, channels), F32)] if len(backs) > 1 else [],
        scalars=(flip,),
        aliases=aliases,
        limit=16 << 20,
    )


def output_kernel(quarter, flip_ref, sent_ref, *refs):
    out_ref, whole_ref, turned_ref = refs[-3:]
    devices, near, count, channels = sent_ref.shape
    per_tile = LANES // (devices * near)
    for d in range(devices):
        whole_ref[d] = sent_ref[d ^ flip_ref[0]]
    for tile in range(count // per_tile):
        rows = [
            whole_ref[:, :, tile * per_tile + i, :].reshape(devices * near, channels)
            for i in range(per_tile)
        ]
        turned = jnp.concatenate(rows, axis=0).T
        for c in range(4):
            turned_ref[tile, pl.ds(c, quarter, stride=4), :] = turned[
                c * quarter : (c + 1) * quarter
            ]
        out_ref[:, tile * LANES : (tile + 1) * LANES] = turned_ref[tile]


def component_chunk(blocks, flip, sent, so_far):
    devices, _, near, local, count, channels = sent.shape
    size = devices * near * count
    in_specs = [
        pl.BlockSpec(
            (devices, None, near, None, count, channels), lambda b, p, f: (0, b, 0, p, 0, 0)
        )
    ]
    args = [sent]
    aliases = {}
    if so_far is not None:
        in_specs.append(pl.BlockSpec(memory_space=pl.ANY))
        args.append(so_far)
        aliases = {2: 0}
    return call(
        functools.partial(output_kernel, channels // 4),
        0,
        8 * sent.size,
        args,
        grid=(len(blocks), local),
        in_specs=in_specs,
        out_specs=pl.BlockSpec(
            (None, channels, size), lambda b, p, f: (4 * p + blocks[0] + b, 0, 0)
        ),
        out_shape=jax.ShapeDtypeStruct((4 * local, channels, size), F32),
        scratch_shapes=[
            pltpu.VMEM((devices, near, count, channels), F32),
            pltpu.VMEM((size // LANES, channels, LANES), F32),
        ],
        scalars=(flip,),
        aliases=aliases,
    )


def exchange(values, pairs):
    devices, blocks, near, local, count, channels = values.shape
    sent = values.reshape(devices, blocks, near, local * count, channels)
    if not pairs:
        return lax.all_to_all(sent, "mom", split_axis=0, concat_axis=0, tiled=True)
    arrived = [sent]
    for s in range(1, devices):
        route = [(d, d ^ s) for d in range(devices)]
        arrived.append(lax.ppermute(sent[s : s + 1], "mom", route))
    return arrived


CHUNKS = (((0, 1), True), ((2, 3), False))


def shards(
    devices,
    source,
    green,
    couple_one,
    couple_two,
    p_bracket,
    q_bracket,
    p_weight,
    q_weight,
    qr_bracket,
    r_bracket,
    qr_weight,
    r_weight,
):
    rows_one, _, size_one = source.shape
    rows_two, size_two = green.shape
    near_r, near_p = rows_one // 4, rows_two // 4
    r_size, p_size = devices * near_r, devices * near_p
    q_size = size_one // p_size
    me = lax.axis_index("mom").astype(jnp.int32)
    flips = [jnp.stack([me if pairs else jnp.int32(0), me]) for _, pairs in CHUNKS]

    first_inputs = (p_bracket, q_bracket, p_weight, q_weight)

    def by_r(array):
        lead = array.shape[:-1]
        return array.reshape(lead + (q_size, r_size)).swapaxes(-1, -2).reshape(lead + (-1,))

    second_maps = spline_maps(
        by_r(r_bracket), by_r(qr_bracket), by_r(r_weight), by_r(qr_weight), q_size
    )
    green = green.reshape(near_p, 4, q_size, r_size).transpose(3, 2, 1, 0)
    green = green.reshape(size_two, 4 * near_p)
    arrived = []
    for step in range(ITERS):
        ones = []
        for flip, (blocks, pairs) in zip(flips, CHUNKS):
            if step == 0:
                if not ones:
                    one, *first_maps = first_one_building(
                        blocks, flip, source, couple_one, first_inputs, near_p, devices, q_size
                    )
                else:
                    one = first_one(blocks, flip, source, couple_one, first_maps, near_p, devices)
            else:
                one = later_one(blocks, flip, backs, couple_one, first_maps, near_p, devices)
            ones.append(exchange(one, pairs))
        arrived.append(ones)
        twos = []
        backs = []
        for n, (flip, (blocks, pairs)) in enumerate(zip(flips, CHUNKS)):
            chunks = [arrived[0][n]] + ([arrived[step][n]] if step else [])
            lanes = slice(blocks[0] * near_p, (blocks[-1] + 1) * near_p)
            scale = green[:, lanes]
            two = component_two(
                blocks, flip, chunks, couple_two, scale, second_maps, near_r, devices
            )
            twos.append(two)
            backs.append(exchange(two, pairs))
    component = amplitude = None
    for flip, (blocks, _), two, back in zip(flips, CHUNKS, twos, backs):
        component = component_chunk(blocks, flip, two, component)
        amplitude = amplitude_chunk(blocks, flip, source, back, amplitude)
    return amplitude, component


def whole_map(first, second, first_weight, second_weight, first_count, second_count):
    first_rows = jnp.zeros((first.shape[0], first_count), F32)
    second_rows = jnp.zeros((second.shape[0], second_count), F32)
    first_grid = jnp.arange(first_count, dtype=jnp.int32)[None, :] - first[:, None]
    second_grid = jnp.arange(second_count, dtype=jnp.int32)[None, :] - second[:, None]
    for offset in range(4):
        first_rows += jnp.where(first_grid == offset, first_weight[offset][:, None], 0.0)
        second_rows += jnp.where(second_grid == offset, second_weight[offset][:, None], 0.0)
    return (first_rows[:, :, None] * second_rows[:, None, :]).reshape(first.shape[0], -1)


def row_mats(couple, rows, start):
    select = jax.nn.one_hot((start + jnp.arange(rows, dtype=jnp.int32)) % 4, 4, dtype=F32)
    return jnp.einsum("rc,kcmn->krmn", select, couple, precision=lax.Precision.HIGHEST)


def mix_rows(mats, values):
    return jnp.einsum("rmn,rnx->rmx", mats, values, precision=lax.Precision.HIGHEST)


def interpolate_rows(values, matrix):
    return jnp.einsum("rcx,yx->rcy", values, matrix, precision=lax.Precision.HIGHEST)


def shards_by_row(
    devices,
    source,
    green,
    couple_one,
    couple_two,
    p_bracket,
    q_bracket,
    p_weight,
    q_weight,
    qr_bracket,
    r_bracket,
    qr_weight,
    r_weight,
):
    rows_one, channels, size_one = source.shape
    rows_two, size_two = green.shape
    angles = couple_one.shape[0]
    quarter = channels // 4
    r_size, p_size = devices * rows_one // 4, devices * rows_two // 4
    q_size = size_one // p_size
    here = lax.axis_index("mom")
    first = [
        whole_map(p_bracket[k], q_bracket[k], p_weight[k], q_weight[k], p_size, q_size)
        for k in range(angles)
    ]
    second = [
        whole_map(qr_bracket[k], r_bracket[k], qr_weight[k], r_weight[k], q_size, r_size)
        for k in range(angles)
    ]
    mats_one = row_mats(couple_one, rows_one, here * rows_one)
    mats_two = row_mats(couple_two, rows_two, here * rows_two)
    state = source
    for _ in range(ITERS):
        one = sum(interpolate_rows(mix_rows(mats_one[k], state), first[k]) for k in range(angles))
        sent = one.reshape(rows_one, 4, quarter, p_size, q_size).transpose(3, 1, 0, 2, 4)
        sent = sent.reshape(4 * p_size, rows_one, quarter * q_size)
        sent = lax.all_to_all(sent, "mom", split_axis=0, concat_axis=1, tiled=True)
        sent = sent.reshape(rows_two, r_size, 4, quarter, q_size).transpose(0, 3, 2, 4, 1)
        sent = sent.reshape(rows_two, channels, size_two)
        total = sum(mix_rows(mats_two[k], interpolate_rows(sent, second[k])) for k in range(angles))
        component = green[:, None, :] * total
        back = component.reshape(rows_two, quarter, 4, q_size, r_size).transpose(4, 2, 0, 1, 3)
        back = back.reshape(4 * r_size, rows_two, quarter * q_size)
        back = lax.all_to_all(back, "mom", split_axis=0, concat_axis=1, tiled=True)
        back = back.reshape(rows_one, p_size, 4, quarter, q_size).transpose(0, 2, 3, 1, 4)
        state = source + back.reshape(source.shape)
    return state, component


def solution(mesh):
    spread = ("energy", "mom")
    placed = (P(spread, None, None), P(spread, None)) + (P(),) * 10
    devices = mesh.shape["mom"]

    def body(source, green, *rest):
        whole_rows = source.shape[0] % 4 == 0 and green.shape[0] % 4 == 0
        chosen = shards if whole_rows and source.shape[1] == LANES else shards_by_row
        return chosen(devices, source, green, *rest)

    return jax.shard_map(
        body,
        mesh=mesh,
        in_specs=placed,
        out_specs=(P(spread, None, None), P(spread, None, None)),
        check_vma=False,
    )
```

```python
import functools


import jax
import jax.numpy as jnp
from jax import lax
from jax.experimental import pallas as pl
from jax.experimental.pallas import tpu as pltpu
from jax.sharding import PartitionSpec as P

ITERS = 2
LANES = 128
F32 = jnp.float32
BF16 = jnp.bfloat16
VMEM_LIMIT = 60 << 20
PIECES = 4
TILES = 4
SOURCE_ROWS = 4


def split(value):
    high = value.astype(BF16)
    return high, (value - high.astype(F32)).astype(BF16)


def dot(a, b):
    return jnp.dot(a, b, preferred_element_type=F32)


def dot_nt(a, b):
    return lax.dot_general(a, b, (((1,), (1,)), ((), ())), preferred_element_type=F32)


def call(kernel, flops, moved, args, grid, in_specs, out_specs, out_shape, scratch_shapes=(), scalars=(), aliases=None, limit=VMEM_LIMIT):
    return pl.pallas_call(
        kernel,
        grid_spec=pltpu.PrefetchScalarGridSpec(
            num_scalar_prefetch=len(scalars),
            grid=grid,
            in_specs=in_specs,
            out_specs=out_specs,
            scratch_shapes=scratch_shapes,
        ),
        out_shape=out_shape,
        input_output_aliases=aliases or {},
        compiler_params=pltpu.CompilerParams(vmem_limit_bytes=limit),
        cost_estimate=pl.CostEstimate(flops=flops, bytes_accessed=moved, transcendentals=0),
    )(*scalars, *args)


def map_factors(count, k, rows, first_ref, second_ref, first_weight_ref, second_weight_ref):
    size = rows.size
    table = jnp.concatenate(
        [
            first_ref[k : k + 1, rows].astype(F32),
            second_ref[k : k + 1, rows].astype(F32),
            first_weight_ref[k, :, rows],
            second_weight_ref[k, :, rows],
            jnp.zeros((6, size), F32),
        ],
        axis=0,
    ).T
    lane = lax.broadcasted_iota(jnp.int32, (1, LANES), 1)

    def factor(index, base):
        grid = index.astype(F32) - table[:, base : base + 1]
        total = jnp.zeros((size, LANES), F32)
        for offset in range(4):
            column = 2 + 4 * base + offset
            total = jnp.where(grid == offset, table[:, column : column + 1], total)
        return total

    high, low = split(factor(lane, 0))
    return high, low, factor(lane - lax.div(lane, count) * count, 1)


def chosen_nodes(count, columns):
    node = lax.broadcasted_iota(jnp.int32, (LANES, columns), 0)
    column = lax.broadcasted_iota(jnp.int32, (LANES, columns), 1)
    inside = jnp.logical_and(column >= node * count, column < (node + 1) * count)
    return jnp.where(inside, 1.0, 0.0).astype(BF16)


def build_rows(count, rows, inputs, chosen, high_ref, low_ref):
    angles, size = inputs[0].shape
    for k in range(angles):
        first_high, first_low, second = map_factors(count, k, rows, *inputs)
        for tile in range(size // LANES):
            lanes = slice(tile * LANES, (tile + 1) * LANES)
            spread = dot(first_high, chosen[:, lanes]) + dot(first_low, chosen[:, lanes])
            high, low = split(spread * second)
            lanes = slice(k * size + tile * LANES, k * size + (tile + 1) * LANES)
            high_ref[:, lanes] = high
            low_ref[:, lanes] = low


def map_kernel(count, *refs):
    inputs, (high_ref, low_ref) = refs[:4], refs[4:]
    size = high_ref.shape[0]
    start = pl.multiple_of(pl.program_id(0) * size, size)
    chosen = chosen_nodes(count, inputs[0].shape[1])
    build_rows(count, pl.ds(start, size), inputs, chosen, high_ref, low_ref)


def spline_maps(first, second, first_weight, second_weight, count):
    angles, size = first.shape
    tile = size // PIECES
    out = jax.ShapeDtypeStruct((size, angles * size), BF16)
    spec = pl.BlockSpec((tile, angles * size), lambda i: (i, 0))
    return call(
        functools.partial(map_kernel, count),
        10 * angles * size * size,
        4 * angles * size * size,
        (first, second, first_weight, second_weight),
        grid=(PIECES,),
        in_specs=[pl.BlockSpec(memory_space=pltpu.VMEM)] * 4,
        out_specs=[spec, spec],
        out_shape=[out, out],
    )


def interpolate(high_ref, low_ref, mixed_high, mixed_low, product):
    high = high_ref[...]
    return (
        product(high, mixed_high[...])
        + product(high, mixed_low[...])
        + product(low_ref[...], mixed_high[...])
    )


def spread_out(flip, value, out_ref, scale_ref=None):
    parts, blocks, near, local, count, channels = out_ref.shape
    rows = near * count
    for b in range(blocks):
        for n in range(local):
            at = b * local + n
            block = value[:, at * channels : (at + 1) * channels]
            if scale_ref is not None:
                block = block * scale_ref[:, at : at + 1]
            for j in range(parts):
                piece = block[j * rows : (j + 1) * rows].reshape(near, count, channels)
                out_ref[j ^ (flip & (parts - 1)), b, :, n, :, :] = piece


def out_spec(shape, tile):
    parts = shape[0] // TILES
    return pl.BlockSpec(
        (parts,) + shape[1:],
        lambda i, flip: (tile(i) ^ lax.div(flip[0], parts), 0, 0, 0, 0, 0),
    )


def gather(me, sets, whole_ref):
    blocks, local, _, _ = whole_ref.shape
    per = sets[0][0].shape[3]
    for s in range(len(sets[0])):
        rows = pl.ds(pl.multiple_of((me ^ s) * per, per), per)
        for b in range(blocks):
            for n in range(local):
                value = sets[0][s][0, b, n]
                for other in sets[1:]:
                    value = value + other[s][0, b, n]
                whole_ref[b, n, rows, :] = value


def finish_rows(flip, t, value, held_ref, out_ref, sems, scale_ref=None):
    devices, blocks, near, local, count, channels = held_ref.shape
    parts = devices // PIECES
    rows = near * count
    group = t ^ lax.div(flip, parts)
    for b in range(blocks):
        for n in range(local):
            at = b * local + n
            block = value[:, at * channels : (at + 1) * channels]
            if scale_ref is not None:
                start = pl.multiple_of(t * parts * rows, parts * rows)
                block = block * scale_ref[pl.ds(start, parts * rows), at : at + 1]
            for j in range(parts):
                piece = block[j * rows : (j + 1) * rows].reshape(near, count, channels)
                held_ref[group * parts + (j ^ (flip & (parts - 1))), b, :, n, :, :] = piece
    part = pl.ds(group * parts, parts)
    pltpu.make_async_copy(held_ref.at[part], out_ref.at[part], sems.at[group]).start()


def finish_copies(held_ref, out_ref, sems):
    parts = held_ref.shape[0] // PIECES
    for t in range(PIECES):
        part = pl.ds(t * parts, parts)
        pltpu.make_async_copy(held_ref.at[part], out_ref.at[part], sems.at[t]).wait()


def mix_source(blocks, source_ref, held, sems, couple_ref, m_high, m_low):
    angles, _, channels, _ = couple_ref.shape
    rows, _, size = held.shape
    quarter = channels // 4
    count = angles * len(blocks) * quarter
    local = rows // 4

    def step(row, carry):
        pltpu.make_async_copy(source_ref.at[row], held.at[row], sems.at[row]).wait()
        r, c = lax.div(row, 4), lax.rem(row, 4)
        picked = [
            couple_ref[k, c, g * quarter : (g + 1) * quarter, :]
            for k in range(angles)
            for g in blocks
        ]
        w_high, w_low = split(jnp.concatenate(picked, axis=0))
        high, low = split(held[row])
        both = dot(jnp.concatenate([w_high, w_low], axis=0), high)
        high, low = split(both[:count] + both[count:] + dot(w_high, low))
        for k in range(angles):
            lanes = slice(k * size, (k + 1) * size)
            for b in range(len(blocks)):
                at = (k * len(blocks) + b) * quarter
                to = pl.multiple_of((b * local + r) * channels + c * quarter, quarter)
                m_high[pl.ds(to, quarter), lanes] = high[at : at + quarter]
                m_low[pl.ds(to, quarter), lanes] = low[at : at + quarter]
        return carry

    lax.fori_loop(0, rows, step, 0)


def building_kernel(blocks, count, flip_ref, source_ref, couple_ref, *refs):
    inputs = refs[:4]
    out_ref, made_high, made_low = refs[4:7]
    held_source, source_sems, high_buf, low_buf, map_sems, m_high, m_low, held_ref, sems = refs[7:]
    for row in range(source_ref.shape[0]):
        pltpu.make_async_copy(source_ref.at[row], held_source.at[row], source_sems.at[row]).start()
    mix_source(blocks, source_ref, held_source, source_sems, couple_ref, m_high, m_low)
    size = inputs[0].shape[1]
    rows = size // PIECES
    chosen = chosen_nodes(count, size)
    made = ((high_buf, made_high), (low_buf, made_low))

    def piece(t):
        part = pl.ds(pl.multiple_of(t * rows, rows), rows)
        build_rows(count, part, inputs, chosen, high_buf.at[part], low_buf.at[part])
        for n, (buf, to) in enumerate(made):
            pltpu.make_async_copy(buf.at[part], to.at[part], map_sems.at[n, t]).start()
        value = interpolate(high_buf.at[part], low_buf.at[part], m_high, m_low, dot_nt)
        finish_rows(flip_ref[0], t, value, held_ref, out_ref, sems)

    def step(t, carry):
        piece(2 * t)
        piece(2 * t + 1)
        return carry

    lax.fori_loop(0, PIECES // 2, step, 0)
    finish_copies(held_ref, out_ref, sems)
    for t in range(PIECES):
        part = pl.ds(t * rows, rows)
        for n, (buf, to) in enumerate(made):
            pltpu.make_async_copy(buf.at[part], to.at[part], map_sems.at[n, t]).wait()


def first_one_building(blocks, flip, source, couple, inputs, near, devices, count):
    rows, channels, size = source.shape
    local = rows // 4
    angles = couple.shape[0]
    out = (devices, len(blocks), near, local, size // (devices * near), channels)
    wide = len(blocks) * local * channels
    vmem = pl.BlockSpec(memory_space=pltpu.VMEM)
    anywhere = pl.BlockSpec(memory_space=pl.ANY)
    made = jax.ShapeDtypeStruct((size, angles * size), BF16)
    return call(
        functools.partial(building_kernel, blocks, count),
        6 * wide * angles * size * (size + channels),
        4 * source.size + 4 * angles * size * size,
        (source, couple, *inputs),
        grid=(),
        in_specs=[anywhere] + [vmem] * 5,
        out_specs=[anywhere] * 3,
        out_shape=[jax.ShapeDtypeStruct(out, F32), made, made],
        scratch_shapes=[pltpu.VMEM(source.shape, F32), pltpu.SemaphoreType.DMA((rows,))]
        + [pltpu.VMEM(made.shape, BF16)] * 2
        + [pltpu.SemaphoreType.DMA((2, PIECES))]
        + [pltpu.VMEM((wide, angles * size), BF16)] * 2
        + [pltpu.VMEM(out, F32), pltpu.SemaphoreType.DMA((PIECES,))],
        scalars=(flip,),
    )


def first_kernel(blocks, steps, flip_ref, source_ref, couple_ref, high_ref, low_ref, out_ref, m_high, m_low):
    angles, _, channels, _ = couple_ref.shape
    quarter = channels // 4
    together, _, size = source_ref.shape
    i = pl.program_id(0)
    count = angles * len(blocks) * quarter
    local = steps * together // 4

    @pl.when(i < steps)
    def _():
        for n in range(together):
            row = i * together + n
            r, c = lax.div(row, 4), lax.rem(row, 4)
            rows = [
                couple_ref[k, c, g * quarter : (g + 1) * quarter, :]
                for k in range(angles)
                for g in blocks
            ]
            w_high, w_low = split(jnp.concatenate(rows, axis=0))
            high, low = split(source_ref[n])
            both = dot(jnp.concatenate([w_high, w_low], axis=0), high)
            high, low = split(both[:count] + both[count:] + dot(w_high, low))
            for k in range(angles):
                lanes = slice(k * size, (k + 1) * size)
                for b in range(len(blocks)):
                    at = (k * len(blocks) + b) * quarter
                    to = pl.multiple_of((b * local + r) * channels + c * quarter, quarter)
                    m_high[pl.ds(to, quarter), lanes] = high[at : at + quarter]
                    m_low[pl.ds(to, quarter), lanes] = low[at : at + quarter]

    @pl.when(i >= steps)
    def _():
        spread_out(flip_ref[0], interpolate(high_ref, low_ref, m_high, m_low, dot_nt), out_ref)


def first_one(blocks, flip, source, couple, maps, near, devices):
    rows, channels, size = source.shape
    local = rows // 4
    angles = couple.shape[0]
    together = SOURCE_ROWS
    steps = rows // together
    out = (devices, len(blocks), near, local, size // (devices * near), channels)
    wide = len(blocks) * local * channels

    def tile(i):
        return jnp.maximum(i - steps, 0)

    return call(
        functools.partial(first_kernel, blocks, steps),
        6 * wide * angles * size * (size + channels),
        4 * source.size + 4 * angles * size * size,
        (source, couple, *maps),
        grid=(steps + TILES,),
        in_specs=[
            pl.BlockSpec((together, channels, size), lambda i, f: (jnp.minimum(i, steps - 1), 0, 0)),
            pl.BlockSpec(couple.shape, lambda i, f: (0, 0, 0, 0)),
        ]
        + [pl.BlockSpec((size // TILES, angles * size), lambda i, f: (tile(i), 0))] * 2,
        out_specs=out_spec(out, tile),
        out_shape=jax.ShapeDtypeStruct(out, F32),
        scratch_shapes=[pltpu.VMEM((wide, angles * size), BF16)] * 2,
        scalars=(flip,),
    )


def chunk_specs(chunk):
    if not isinstance(chunk, list):
        return [chunk], [pl.BlockSpec(chunk.shape, lambda i, f: (0, 0, 0, 0, 0))]
    spec = pl.BlockSpec((1,) + chunk[0].shape[1:], lambda i, f: (0, 0, 0, 0, 0))
    return chunk, [spec] * len(chunk)


def later_kernel(blocks, counts, flip_ref, *refs):
    chunks = []
    for count in counts:
        chunks.append(refs[:count])
        refs = refs[count:]
    couple_ref, high_ref, low_ref, out_ref, w_high, w_low, m_high, m_low = refs[:8]
    wholes = list(refs[8:])
    angles, _, channels, _ = couple_ref.shape
    quarter = channels // 4
    size = high_ref.shape[1] // angles
    _, _, local, per, _ = chunks[0][0].shape

    @pl.when(pl.program_id(0) == 0)
    def _():
        lane = lax.broadcasted_iota(jnp.int32, (quarter, channels), 1)
        for k in range(angles):
            for b, g in enumerate(blocks):
                for c in range(4):
                    rows = couple_ref[k, c, g * quarter : (g + 1) * quarter, :]
                    at = (k * len(blocks) + b) * channels + c * quarter
                    inside = lax.div(lane, quarter) == c
                    for other in range(4):
                        shift = ((c - other) * quarter) % channels
                        moved = pltpu.roll(rows, shift, 1) if shift else rows
                        high, low = split(jnp.where(inside, moved, 0.0))
                        lanes = slice(other * channels, (other + 1) * channels)
                        w_high[at : at + quarter, lanes] = high
                        w_low[at : at + quarter, lanes] = low
        sources = []
        for chunk in chunks:
            if len(chunk) > 1:
                whole = wholes.pop(0)
                gather(flip_ref[1], [chunk], whole)
                sources += [(whole, b, True) for b in range(whole.shape[0])]
            else:
                sources += [(chunk[0], b, False) for b in range(chunk[0].shape[1])]
        rows = min(256, size)

        def step(t, carry):
            for r in range(local):
                pieces = []
                for ref, b, flat in sources:
                    if flat:
                        pieces.append(ref[b, r, pl.ds(pl.multiple_of(t * rows, rows), rows), :])
                    else:
                        piece = ref[pl.ds(t * (rows // per), rows // per), b, r]
                        pieces.append(piece.reshape(rows, channels))
                high, low = split(jnp.concatenate(pieces, axis=1))
                mixed = (
                    dot_nt(high, w_high[...]) + dot_nt(low, w_high[...]) + dot_nt(high, w_low[...])
                )
                high, low = split(mixed)
                for k in range(angles):
                    here = pl.ds(pl.multiple_of(k * size + t * rows, rows), rows)
                    for b in range(len(blocks)):
                        at = (k * len(blocks) + b) * channels
                        to = (b * local + r) * channels
                        m_high[here, to : to + channels] = high[:, at : at + channels]
                        m_low[here, to : to + channels] = low[:, at : at + channels]
            return carry

        lax.fori_loop(0, size // rows, step, 0)

    spread_out(flip_ref[0], interpolate(high_ref, low_ref, m_high, m_low, dot), out_ref)


def later_one(blocks, flip, chunks, couple, maps, near, devices):
    _, _, local, per, channels = chunks[0][0].shape if isinstance(chunks[0], list) else chunks[0].shape
    size = devices * per
    angles = couple.shape[0]
    out = (devices, len(blocks), near, local, size // (devices * near), channels)
    wide = len(blocks) * local * channels
    operands, specs, counts, wholes = [], [], [], []
    for chunk in chunks:
        some, some_specs = chunk_specs(chunk)
        operands += some
        specs += some_specs
        counts.append(len(some))
        if isinstance(chunk, list):
            wholes.append(pltpu.VMEM((chunk[0].shape[1], local, size, channels), F32))
    return call(
        functools.partial(later_kernel, blocks, counts),
        6 * wide * angles * size * (size + 4 * channels),
        16 * local * size * channels + 4 * angles * size * size,
        (*operands, couple, *maps),
        grid=(TILES,),
        in_specs=specs
        + [pl.BlockSpec(couple.shape, lambda i, f: (0, 0, 0, 0))]
        + [pl.BlockSpec((size // TILES, angles * size), lambda i, f: (i, 0))] * 2,
        out_specs=out_spec(out, lambda i: i),
        out_shape=jax.ShapeDtypeStruct(out, F32),
        scratch_shapes=[pltpu.VMEM((angles * len(blocks) * channels, 4 * channels), BF16)] * 2
        + [pltpu.VMEM((angles * size, wide), BF16)] * 2
        + wholes,
        scalars=(flip,),
        limit=44 << 20,
    )


def two_kernel(blocks, counts, flip_ref, *refs):
    chunks = []
    for count in counts:
        chunks.append(refs[:count])
        refs = refs[count:]
    couple_ref, green_ref, high_ref, low_ref, out_ref, turned, w_high, w_low, m_high, m_low = refs[:10]
    angles, _, channels, _ = couple_ref.shape
    quarter = channels // 4
    size = high_ref.shape[1] // angles
    _, _, local, per, _ = chunks[0][0].shape

    @pl.when(pl.program_id(0) == 0)
    def _():
        for k in range(angles):
            for b, g in enumerate(blocks):
                at = k * len(blocks) + b
                rows = [couple_ref[k, g, pl.ds(c, quarter, stride=4), :] for c in range(4)]
                turned[at] = jnp.concatenate(rows, axis=0).T
                rows = [turned[at, pl.ds(c, quarter, stride=4), :] for c in range(4)]
                high, low = split(jnp.concatenate(rows, axis=0))
                w_high[b, :, k * channels : (k + 1) * channels] = high
                w_low[b, :, k * channels : (k + 1) * channels] = low
        if counts[0] > 1:
            gather(flip_ref[1], chunks, refs[10])
        rows = min(256, size)

        def step(t, carry):
            for b in range(len(blocks)):
                for p in range(local):
                    if counts[0] > 1:
                        here = pl.ds(pl.multiple_of(t * rows, rows), rows)
                        value = refs[10][b, p, here, :]
                    else:
                        here = pl.ds(t * (rows // per), rows // per)
                        value = chunks[0][0][here, b, p]
                        for other in chunks[1:]:
                            value = value + other[0][here, b, p]
                        value = value.reshape(rows, channels)
                    high, low = split(value)
                    mixed = dot(high, w_high[b]) + dot(low, w_high[b]) + dot(high, w_low[b])
                    high, low = split(mixed)
                    to = (b * local + p) * channels
                    for k in range(angles):
                        here = pl.ds(pl.multiple_of(k * size + t * rows, rows), rows)
                        lanes = slice(k * channels, (k + 1) * channels)
                        m_high[here, to : to + channels] = high[:, lanes]
                        m_low[here, to : to + channels] = low[:, lanes]
            return carry

        lax.fori_loop(0, size // rows, step, 0)

    spread_out(flip_ref[0], interpolate(high_ref, low_ref, m_high, m_low, dot), out_ref, green_ref)


def component_two(blocks, flip, chunks, couple, green, maps, near, devices):
    _, _, local, per, channels = chunks[0][0].shape if isinstance(chunks[0], list) else chunks[0].shape
    size = devices * per
    angles = couple.shape[0]
    out = (devices, len(blocks), near, local, per // near, channels)
    wide = len(blocks) * local * channels
    operands, specs, counts = [], [], []
    for chunk in chunks:
        some, some_specs = chunk_specs(chunk)
        operands += some
        specs += some_specs
        counts.append(len(some))
    wholes = [pltpu.VMEM((len(blocks), local, size, channels), F32)] if counts[0] > 1 else []
    return call(
        functools.partial(two_kernel, blocks, counts),
        6 * wide * angles * size * (size + channels),
        4 * len(chunks) * wide * size + 4 * angles * size * size,
        (*operands, couple, green, *maps),
        grid=(TILES,),
        in_specs=specs
        + [
            pl.BlockSpec(couple.shape, lambda i, f: (0, 0, 0, 0)),
            pl.BlockSpec((size // TILES, green.shape[1]), lambda i, f: (i, 0)),
        ]
        + [pl.BlockSpec((size // TILES, angles * size), lambda i, f: (i, 0))] * 2,
        out_specs=out_spec(out, lambda i: i),
        out_shape=jax.ShapeDtypeStruct(out, F32),
        scratch_shapes=[pltpu.VMEM((angles * len(blocks), channels, channels), F32)]
        + [pltpu.VMEM((len(blocks), channels, angles * channels), BF16)] * 2
        + [pltpu.VMEM((angles * size, wide), BF16)] * 2
        + wholes,
        scalars=(flip,),
    )


def amplitude_kernel(quarter, count, flip_ref, source_ref, *refs):
    backs, out_ref = refs[:count], refs[-1]
    if count > 1:
        out_ref, whole_ref = refs[-2:]
        per = backs[0].shape[1]
        for s in range(count):
            rows = pl.ds(pl.multiple_of((flip_ref[1] ^ s) * per, per), per)
            whole_ref[rows, :] = backs[s][0]
        turned = whole_ref[...].T
    else:
        back = backs[0][...]
        turned = back.reshape(-1, back.shape[-1]).T
    for c in range(4):
        out_ref[c] = source_ref[c] + turned[c * quarter : (c + 1) * quarter]


def amplitude_chunk(blocks, flip, source, chunk, so_far):
    _, channels, size = source.shape
    quarter = channels // 4
    backs = chunk if isinstance(chunk, list) else [chunk]
    _, _, local, per, _ = backs[0].shape
    spec = pl.BlockSpec((4, quarter, size), lambda b, r, f: (r, blocks[0] + b, 0))
    depth = 1 if len(backs) > 1 else backs[0].shape[0]
    back_spec = pl.BlockSpec((depth, None, None, per, channels), lambda b, r, f: (0, b, r, 0, 0))
    in_specs = [spec] + [back_spec] * len(backs)
    args = [source, *backs]
    aliases = {}
    if so_far is not None:
        in_specs.append(pl.BlockSpec(memory_space=pl.ANY))
        args.append(so_far)
        aliases = {len(args): 0}
    moved = len(blocks) * local * channels * size
    return call(
        functools.partial(amplitude_kernel, quarter, len(backs)),
        moved,
        12 * moved,
        args,
        grid=(len(blocks), local),
        in_specs=in_specs,
        out_specs=spec,
        out_shape=jax.ShapeDtypeStruct(source.shape, F32),
        scratch_shapes=[pltpu.VMEM((size, channels), F32)] if len(backs) > 1 else [],
        scalars=(flip,),
        aliases=aliases,
        limit=16 << 20,
    )


def output_kernel(quarter, flip_ref, sent_ref, *refs):
    out_ref, whole_ref, turned_ref = refs[-3:]
    devices, near, count, channels = sent_ref.shape
    per_tile = LANES // (devices * near)
    for d in range(devices):
        whole_ref[d] = sent_ref[d ^ flip_ref[0]]
    for tile in range(count // per_tile):
        rows = [
            whole_ref[:, :, tile * per_tile + i, :].reshape(devices * near, channels)
            for i in range(per_tile)
        ]
        turned = jnp.concatenate(rows, axis=0).T
        for c in range(4):
            turned_ref[tile, pl.ds(c, quarter, stride=4), :] = turned[
                c * quarter : (c + 1) * quarter
            ]
        out_ref[:, tile * LANES : (tile + 1) * LANES] = turned_ref[tile]


def component_chunk(blocks, flip, sent, so_far):
    devices, _, near, local, count, channels = sent.shape
    size = devices * near * count
    in_specs = [
        pl.BlockSpec(
            (devices, None, near, None, count, channels), lambda b, p, f: (0, b, 0, p, 0, 0)
        )
    ]
    args = [sent]
    aliases = {}
    if so_far is not None:
        in_specs.append(pl.BlockSpec(memory_space=pl.ANY))
        args.append(so_far)
        aliases = {2: 0}
    return call(
        functools.partial(output_kernel, channels // 4),
        0,
        8 * sent.size,
        args,
        grid=(len(blocks), local),
        in_specs=in_specs,
        out_specs=pl.BlockSpec(
            (None, channels, size), lambda b, p, f: (4 * p + blocks[0] + b, 0, 0)
        ),
        out_shape=jax.ShapeDtypeStruct((4 * local, channels, size), F32),
        scratch_shapes=[
            pltpu.VMEM((devices, near, count, channels), F32),
            pltpu.VMEM((size // LANES, channels, LANES), F32),
        ],
        scalars=(flip,),
        aliases=aliases,
    )


def exchange(values, pairs):
    devices, blocks, near, local, count, channels = values.shape
    sent = values.reshape(devices, blocks, near, local * count, channels)
    if not pairs:
        return lax.all_to_all(sent, "mom", split_axis=0, concat_axis=0, tiled=True)
    arrived = [sent]
    for s in range(1, devices):
        route = [(d, d ^ s) for d in range(devices)]
        arrived.append(lax.ppermute(sent[s : s + 1], "mom", route))
    return arrived


CHUNKS = (((0, 1), True), ((2, 3), False))


def shards(
    devices,
    source,
    green,
    couple_one,
    couple_two,
    p_bracket,
    q_bracket,
    p_weight,
    q_weight,
    qr_bracket,
    r_bracket,
    qr_weight,
    r_weight,
):
    rows_one, _, size_one = source.shape
    rows_two, size_two = green.shape
    near_r, near_p = rows_one // 4, rows_two // 4
    r_size, p_size = devices * near_r, devices * near_p
    q_size = size_one // p_size
    me = lax.axis_index("mom").astype(jnp.int32)
    flips = [jnp.stack([me if pairs else jnp.int32(0), me]) for _, pairs in CHUNKS]

    first_inputs = (p_bracket, q_bracket, p_weight, q_weight)

    def by_r(array):
        lead = array.shape[:-1]
        return array.reshape(lead + (q_size, r_size)).swapaxes(-1, -2).reshape(lead + (-1,))

    second_maps = spline_maps(
        by_r(r_bracket), by_r(qr_bracket), by_r(r_weight), by_r(qr_weight), q_size
    )
    green = green.reshape(near_p, 4, q_size, r_size).transpose(3, 2, 1, 0)
    green = green.reshape(size_two, 4 * near_p)
    arrived = []
    for step in range(ITERS):
        ones = []
        for flip, (blocks, pairs) in zip(flips, CHUNKS):
            if step == 0:
                if not ones:
                    one, *first_maps = first_one_building(
                        blocks, flip, source, couple_one, first_inputs, near_p, devices, q_size
                    )
                else:
                    one = first_one(blocks, flip, source, couple_one, first_maps, near_p, devices)
            else:
                one = later_one(blocks, flip, backs, couple_one, first_maps, near_p, devices)
            ones.append(exchange(one, pairs))
        arrived.append(ones)
        twos = []
        backs = []
        for n, (flip, (blocks, pairs)) in enumerate(zip(flips, CHUNKS)):
            chunks = [arrived[0][n]] + ([arrived[step][n]] if step else [])
            lanes = slice(blocks[0] * near_p, (blocks[-1] + 1) * near_p)
            scale = green[:, lanes]
            two = component_two(
                blocks, flip, chunks, couple_two, scale, second_maps, near_r, devices
            )
            twos.append(two)
            backs.append(exchange(two, pairs))
    component = amplitude = None
    for flip, (blocks, _), two, back in zip(flips, CHUNKS, twos, backs):
        component = component_chunk(blocks, flip, two, component)
        amplitude = amplitude_chunk(blocks, flip, source, back, amplitude)
    return amplitude, component


def whole_map(first, second, first_weight, second_weight, first_count, second_count):
    first_rows = jnp.zeros((first.shape[0], first_count), F32)
    second_rows = jnp.zeros((second.shape[0], second_count), F32)
    first_grid = jnp.arange(first_count, dtype=jnp.int32)[None, :] - first[:, None]
    second_grid = jnp.arange(second_count, dtype=jnp.int32)[None, :] - second[:, None]
    for offset in range(4):
        first_rows += jnp.where(first_grid == offset, first_weight[offset][:, None], 0.0)
        second_rows += jnp.where(second_grid == offset, second_weight[offset][:, None], 0.0)
    return (first_rows[:, :, None] * second_rows[:, None, :]).reshape(first.shape[0], -1)


def row_mats(couple, rows, start):
    select = jax.nn.one_hot((start + jnp.arange(rows, dtype=jnp.int32)) % 4, 4, dtype=F32)
    return jnp.einsum("rc,kcmn->krmn", select, couple, precision=lax.Precision.HIGHEST)


def mix_rows(mats, values):
    return jnp.einsum("rmn,rnx->rmx", mats, values, precision=lax.Precision.HIGHEST)


def interpolate_rows(values, matrix):
    return jnp.einsum("rcx,yx->rcy", values, matrix, precision=lax.Precision.HIGHEST)


def shards_by_row(
    devices,
    source,
    green,
    couple_one,
    couple_two,
    p_bracket,
    q_bracket,
    p_weight,
    q_weight,
    qr_bracket,
    r_bracket,
    qr_weight,
    r_weight,
):
    rows_one, channels, size_one = source.shape
    rows_two, size_two = green.shape
    angles = couple_one.shape[0]
    quarter = channels // 4
    r_size, p_size = devices * rows_one // 4, devices * rows_two // 4
    q_size = size_one // p_size
    here = lax.axis_index("mom")
    first = [
        whole_map(p_bracket[k], q_bracket[k], p_weight[k], q_weight[k], p_size, q_size)
        for k in range(angles)
    ]
    second = [
        whole_map(qr_bracket[k], r_bracket[k], qr_weight[k], r_weight[k], q_size, r_size)
        for k in range(angles)
    ]
    mats_one = row_mats(couple_one, rows_one, here * rows_one)
    mats_two = row_mats(couple_two, rows_two, here * rows_two)
    state = source
    for _ in range(ITERS):
        one = sum(interpolate_rows(mix_rows(mats_one[k], state), first[k]) for k in range(angles))
        sent = one.reshape(rows_one, 4, quarter, p_size, q_size).transpose(3, 1, 0, 2, 4)
        sent = sent.reshape(4 * p_size, rows_one, quarter * q_size)
        sent = lax.all_to_all(sent, "mom", split_axis=0, concat_axis=1, tiled=True)
        sent = sent.reshape(rows_two, r_size, 4, quarter, q_size).transpose(0, 3, 2, 4, 1)
        sent = sent.reshape(rows_two, channels, size_two)
        total = sum(mix_rows(mats_two[k], interpolate_rows(sent, second[k])) for k in range(angles))
        component = green[:, None, :] * total
        back = component.reshape(rows_two, quarter, 4, q_size, r_size).transpose(4, 2, 0, 1, 3)
        back = back.reshape(4 * r_size, rows_two, quarter * q_size)
        back = lax.all_to_all(back, "mom", split_axis=0, concat_axis=1, tiled=True)
        back = back.reshape(rows_one, p_size, 4, quarter, q_size).transpose(0, 2, 3, 1, 4)
        state = source + back.reshape(source.shape)
    return state, component


def solution(mesh):
    spread = ("energy", "mom")
    placed = (P(spread, None, None), P(spread, None)) + (P(),) * 10
    devices = mesh.shape["mom"]

    def body(source, green, *rest):
        whole_rows = source.shape[0] % 4 == 0 and green.shape[0] % 4 == 0
        whole_rows = whole_rows and devices >= PIECES and devices & (devices - 1) == 0
        chosen = shards if whole_rows and source.shape[1] == LANES else shards_by_row
        return chosen(devices, source, green, *rest)

    return jax.shard_map(
        body,
        mesh=mesh,
        in_specs=placed,
        out_specs=(P(spread, None, None), P(spread, None, None)),
        check_vma=False,
    )
```
